32 devices in a mesh: row: 4 (over y, x), seq: 8 (over z, core).
Axes of the slice: x: 2, y: 2, z: 4, core: 2. Of those that a mesh axis runs over, the one named last changes fastest.
Arguments:
- tokens: bfloat16 [8, 1024, 1024], P('row', 'seq'), may hold values from -6 to 6
- segment_ids: int32 [8, 1024], P('row'), may hold values from 0 to 7, never falling along the last dimension, each value on 1 to 512 neighbouring positions
- expert_ids: int32 [8, 8, 128, 8], P('seq', 'row'), may hold values from 0 to 15, as said below
- norm1_gain: bfloat16 [1024], P(('row', 'seq')), may hold values from 0.5 to 1.5
- w_query: bfloat16 [1024, 1024], P(('row', 'seq')), may hold values from -0.75 to 0.75
- w_key: bfloat16 [1024, 512], P(('row', 'seq')), may hold values from -0.75 to 0.75
- w_value: bfloat16 [1024, 512], P(('row', 'seq')), may hold values from -0.1875 to 0.1875
- w_out: bfloat16 [1024, 1024], P(None, ('row', 'seq')), may hold values from -2 to 2
- norm2_gain: bfloat16 [1024], P(('row', 'seq')), may hold values from 0.5 to 1.5
- w_router: bfloat16 [1024, 16], P(('row', 'seq')), may hold values from -0.09375 to 0.09375
- w_gate: bfloat16 [16, 1024, 512], P(None, ('row', 'seq')), may hold values from -0.1875 to 0.1875
- w_up: bfloat16 [16, 1024, 512], P(None, ('row', 'seq')), may hold values from -0.1875 to 0.1875
- w_down: bfloat16 [16, 512, 1024], P(None, None, ('row', 'seq')), may hold values from -4 to 4
- out_grad: bfloat16 [8, 1024, 1024], P('row', 'seq'), may hold values from -6 to 6
Outputs:
- layer_out: bfloat16 [8, 1024, 1024], P('row', 'seq')
- input_grad: float32 [8, 1024, 1024], P('row', 'seq')
- grad_norm1_gain: float32 [1024], P(('row', 'seq'))
- grad_w_query: float32 [1024, 1024], P(('row', 'seq'))
- grad_w_key: float32 [1024, 512], P(('row', 'seq'))
- grad_w_value: float32 [1024, 512], P(('row', 'seq'))
- grad_w_out: float32 [1024, 1024], P(None, ('row', 'seq'))
- grad_norm2_gain: float32 [1024], P(('row', 'seq'))
- grad_w_router: float32 [1024, 16], P(('row', 'seq'))
- grad_w_gate: float32 [16, 1024, 512], P(None, ('row', 'seq'))
- grad_w_up: float32 [16, 1024, 512], P(None, ('row', 'seq'))
- grad_w_down: float32 [16, 512, 1024], P(None, None, ('row', 'seq'))
- expert_counts: int32 [16], replicated
The draws below stay inside these ranges and needn't reach their ends.
Inputs may be any that keep to these rules, and one draw needn't show every extreme that they name: `segment_ids`: along a row segment ids never fall; each of the 8 ids covers 1 to 512 consecutive tokens, and one covers exactly that many. `expert_ids`: A token names 8 different experts. Among the tokens of one device (one index of seq and of row), no expert is named by more than 192 tokens, and in every draw some expert is named by exactly 192 of them; every expert is named by some token of each device.
All inputs are finite; a program needn't handle non-finite values.
Results may differ from the reference program's by a relative error of at most 0.015.
Values may be sent and summed in bfloat16 or wider, within the bound.
A program may use at most 320 MiB of HBM per device.

```python
import math
import jax
import jax.numpy as jnp
import numpy as np
from jax import lax

D = 1024
HEADS = 16
KV_HEADS = 8
HEAD = 64
GROUP = 2
FF = 512
EXPERTS = 16
TOPK = 8
SEGS = 8
ROWS_DEV = 2
SPAN = 128
TOK_DEV = 256
ROWS = 8
ROW_LEN = 1024
CAP = 192
N_ROW = 4
N_SEQ = 8


def draw_expert_ids(key, part):
    light = TOK_DEV * TOPK // (2 * EXPERTS)
    rank = jnp.arange(EXPERTS, dtype=jnp.int32)
    loads = jnp.where(rank < EXPERTS // 2, CAP, light).astype(jnp.int32)
    bounds = jnp.cumsum(loads).astype(jnp.int32)
    spots = jnp.arange(TOK_DEV * TOPK, dtype=jnp.int32)
    ranked = jnp.sum((spots[:, None] >= bounds[None, :]).astype(jnp.int32), axis=1)

    def one_device(flat_index):
        device_key = jax.random.fold_in(key, flat_index + 11)
        shift = jax.random.randint(jax.random.fold_in(device_key, 3), (), 0, EXPERTS).astype(jnp.int32)
        labels = (ranked + shift) % EXPERTS
        grid = labels.reshape(TOPK, TOK_DEV).T
        order = jax.random.permutation(jax.random.fold_in(device_key, 1), TOK_DEV)
        grid = grid[order]
        grid = jax.random.permutation(jax.random.fold_in(device_key, 2), grid, axis=1, independent=True)
        return grid.reshape(ROWS_DEV, SPAN, TOPK).astype(jnp.int32)
    row_index = jnp.arange(N_ROW, dtype=jnp.int32)
    seq_index = jnp.arange(N_SEQ, dtype=jnp.int32)
    flat_index = row_index[:, None] * N_SEQ + seq_index[None, :]
    every = jax.vmap(jax.vmap(one_device))(flat_index)
    every = jnp.transpose(every, (1, 0, 2, 3, 4))
    return every.reshape(N_SEQ, N_ROW * ROWS_DEV, SPAN, TOPK)


def block_levels(rng, shape, shards, least, top_value):
    gain = 1.0
    for axis_at, parts in shards:
        steps = jax.random.uniform(jax.random.fold_in(jax.random.fold_in(rng, 6), axis_at), (parts,), jnp.float32, least / len(shards), top_value / len(shards))
        gain = gain * jnp.repeat(jnp.exp(steps), shape[axis_at] // parts).reshape((-1,) + (1,) * (len(shape) - 1 - axis_at))
    return gain


def length_profile(count, total, bound, slope):
    weights = [(1 << 20) // math.isqrt(rank ** slope) + 1 for rank in range(2, count + 1)]
    spare, given = total - bound - (count - 1), [1] * (count - 1)
    while spare > 0:
        candidates = [i for i in range(count - 1) if given[i] < bound]
        mass, budget = sum([weights[i] for i in candidates]), spare
        for i in candidates:
            extra = min(bound - given[i], max(1, budget * weights[i] // mass), spare)
            given[i] = given[i] + extra
            spare = spare - extra
    return np.array([bound] + given)


def ragged(rng, amount, total, limit, skew):
    if amount == 2:
        one = jax.random.randint(rng, (), max(1, total - limit), min(limit, total - 1) + 1)
        return jnp.stack([one, total - one])
    tallies = jnp.asarray(length_profile(amount, total, limit, skew), jnp.int32)
    couples = (amount - 1) // 2
    source_of, receiver = tallies[1:1 + 2 * couples:2], tallies[2:2 + 2 * couples:2]
    slack = jnp.minimum(source_of - 1, limit - receiver)
    shifted = jax.random.randint(jax.random.fold_in(rng, 1), (couples,), 0, 1 << 20) % (slack + 1)
    tallies = tallies.at[1:1 + 2 * couples:2].set(source_of - shifted).at[2:2 + 2 * couples:2].set(receiver + shifted)
    return tallies[jax.random.permutation(jax.random.fold_in(rng, 2), amount)]


def normal_values(own_key, dims, spread, limit, shards=(), kind=jnp.bfloat16):
    values = jax.random.normal(own_key, dims, jnp.float32) * spread
    if len(shards) > 0:
        values = block_levels(own_key, dims, shards, -0.22, 0.18) * values
    return jnp.clip(values, min=-limit, max=limit).astype(kind)


def setup_inputs(seed: int = 0) -> dict:
    splits = jax.random.split(jax.random.key(seed), 15)
    tokens = normal_values(splits[0], (ROWS, ROW_LEN, D), 1.0, 6.0, ((0, 4), (1, 8)))
    segment_ids = jax.vmap(lambda own: jnp.searchsorted(jnp.cumsum(ragged(own, SEGS, ROW_LEN, ROW_LEN // 2, 1)), jnp.arange(ROW_LEN), side="right"))(jax.random.split(splits[1], ROWS)).reshape((ROWS, ROW_LEN)).astype(jnp.int32)
    expert_ids = draw_expert_ids(jax.random.fold_in(splits[14], 71), 0)
    norm1_gain = jnp.clip(1.0 + 0.1 * jax.random.normal(splits[3], (D,), jnp.float32), 0.5, 1.5).astype(jnp.bfloat16)
    w_query = normal_values(splits[4], (D, HEADS * HEAD), (D * HEAD // 1024) ** -0.5, 0.75, ((0, 32),))
    w_key = normal_values(splits[5], (D, KV_HEADS * HEAD), (D * HEAD // 1024) ** -0.5, 0.75, ((0, 32),))
    w_value = normal_values(splits[6], (D, KV_HEADS * HEAD), D ** -0.5, 0.1875, ((0, 32),))
    w_out = normal_values(splits[7], (HEADS * HEAD, D), 8 ** -0.5, 2.0, ((1, 32),))
    norm2_gain = jnp.clip(1.0 + 0.1 * jax.random.normal(splits[8], (D,), jnp.float32), 0.5, 1.5).astype(jnp.bfloat16)
    w_router = normal_values(splits[9], (D, EXPERTS), (4 * D) ** -0.5, 0.09375, ((0, 32),))
    w_gate = normal_values(splits[10], (EXPERTS, D, FF), D ** -0.5, 0.1875, ((1, 32),))
    w_up = normal_values(splits[11], (EXPERTS, D, FF), D ** -0.5, 0.1875, ((1, 32),))
    w_down = normal_values(splits[12], (EXPERTS, FF, D), 2 ** -0.5, 4.0, ((2, 32),))
    out_grad = normal_values(splits[13], (ROWS, ROW_LEN, D), 1.0, 6.0, ((0, 4), (1, 8)))
    return {"tokens": tokens, "segment_ids": segment_ids, "expert_ids": expert_ids, "norm1_gain": norm1_gain, "w_query": w_query, "w_key": w_key, "w_value": w_value, "w_out": w_out, "norm2_gain": norm2_gain, "w_router": w_router, "w_gate": w_gate, "w_up": w_up, "w_down": w_down, "out_grad": out_grad}


EPSILON = 1e-06
SCORE_SCALE = 0.015625
RESIDUAL = 0.22
THETA = 10000.0
NEGATIVE = -1e+30
HIGHEST = lax.Precision.HIGHEST

@jax.custom_vjp
def low(v):
    return lax.optimization_barrier(v.astype(jnp.bfloat16)).astype(jnp.float32)

@jax.custom_vjp
def low_back(v):
    return v

def low_keep(v):
    return (low(v), None)

def low_pass(kept, grad):
    return (grad,)

def back_keep(v):
    return (v, None)

def back_low(kept, grad):
    return (low(grad),)
low.defvjp(low_keep, low_pass)
low_back.defvjp(back_keep, back_low)

def norm_scale(value):
    return lax.rsqrt(lax.optimization_barrier(jnp.mean(value * value, axis=-1, keepdims=True)) + EPSILON)

def positions_of(segments):
    length = segments.shape[-1]
    index = jnp.arange(length, dtype=jnp.int32)
    change = jnp.concatenate([jnp.ones_like(segments[:, :1]), (segments[:, 1:] != segments[:, :-1]).astype(jnp.int32)], axis=1)
    start = lax.cummax(jnp.where(change > 0, index[None, :], 0), axis=1)
    return index[None, :] - start

def rope_tables(positions, width):
    half = width // 2
    frequency = THETA ** (-2.0 * jnp.arange(half, dtype=jnp.float32) / width)
    angle = positions.astype(jnp.float32)[..., None] * frequency
    angle = jnp.concatenate([angle, angle], axis=-1)
    return (jnp.cos(angle), jnp.sin(angle))

def rotate(value, cosine, sine):
    half = value.shape[-1] // 2
    turned = jnp.concatenate([-value[..., half:], value[..., :half]], axis=-1)
    return value * cosine[..., None, :] + turned * sine[..., None, :]

def attend_row(query, keys, values, segments):
    length = segments.shape[0]
    index = jnp.arange(length, dtype=jnp.int32)
    visible = (segments[:, None] == segments[None, :]) & (index[None, :] <= index[:, None])
    raw = jnp.einsum('qkgd,skd->kgqs', query, keys, precision=HIGHEST)
    scores = jnp.where(visible, low_back(SCORE_SCALE * raw), NEGATIVE)
    peak = lax.optimization_barrier(jnp.max(scores, axis=-1, keepdims=True))
    raised = jnp.exp(scores - peak)
    probs = raised / lax.optimization_barrier(jnp.sum(raised, axis=-1, keepdims=True))
    return jnp.einsum('kgqs,skd->qkgd', low(probs), values, precision=HIGHEST)

def reference(tokens, segment_ids, expert_ids, norm1_gain, w_query, w_key, w_value, w_out, norm2_gain, w_router, w_gate, w_up, w_down, out_grad):
    rows, length, width = tokens.shape
    total = rows * length
    routes = jnp.transpose(expert_ids, (1, 0, 2, 3)).reshape(total, TOPK)
    cosine, sine = rope_tables(positions_of(segment_ids).reshape(total), HEAD)
    flat_routes = routes.reshape(-1)
    chosen = routes[:, :, None] == jnp.arange(EXPERTS, dtype=jnp.int32)[None, None, :]
    chosen_float = chosen.astype(jnp.float32)
    counts = lax.optimization_barrier(jnp.sum(chosen.astype(jnp.int32), axis=(0, 1)))
    order = jnp.argsort(flat_routes, stable=True).astype(jnp.int32)
    starts = jnp.cumsum(counts) - counts
    room = CAP * N_ROW * N_SEQ
    slots = jnp.arange(room, dtype=jnp.int32)
    place = jnp.minimum(starts[:, None] + slots[None, :], total * TOPK - 1)
    picks = order[place]
    alive = (slots[None, :] < counts[:, None]).astype(jnp.float32)
    owners = picks // TOPK
    row_step = jax.checkpoint(attend_row)

    def forward(inputs, gain_one, query_weight, key_weight, value_weight, out_weight, gain_two, router_weight, gate_all, up_all, down_all):
        flat = inputs.reshape(total, width)
        normed = low(flat * norm_scale(flat) * gain_one)
        query = low_back(jnp.dot(normed, query_weight, precision=HIGHEST))
        query = low(rotate(query.reshape(total, HEADS, HEAD), cosine, sine))
        keys = low_back(jnp.dot(normed, key_weight, precision=HIGHEST))
        keys = low(rotate(keys.reshape(total, KV_HEADS, HEAD), cosine, sine))
        values = low(low_back(jnp.dot(normed, value_weight, precision=HIGHEST)))
        mixed = lax.map(lambda items: row_step(items[0], items[1], items[2], items[3]), (query.reshape(rows, length, KV_HEADS, GROUP, HEAD), keys.reshape(rows, length, KV_HEADS, HEAD), values.reshape(rows, length, KV_HEADS, HEAD), segment_ids))
        mixed = low(low_back(mixed.reshape(total, HEADS * HEAD)))
        branch = low_back(jnp.dot(mixed, out_weight, precision=HIGHEST))
        hidden = flat + RESIDUAL * branch
        normed_two = low(hidden * norm_scale(hidden) * gain_two)
        logits = low_back(jnp.dot(normed_two, router_weight, precision=HIGHEST))
        picked = lax.optimization_barrier(jnp.sum(chosen_float * logits[:, None, :], axis=-1))
        gates = jax.nn.softmax(picked, axis=-1).reshape(-1)

        def expert_step(accum, items):
            gate_weight, up_weight, down_weight, owner, pick, live = items
            rows_in = normed_two[owner] * live[:, None]
            gate_part = low_back(jnp.dot(rows_in, gate_weight, precision=HIGHEST))
            up_part = low_back(jnp.dot(rows_in, up_weight, precision=HIGHEST))
            inner = low(jax.nn.silu(gate_part) * up_part)
            result = low_back(jnp.dot(inner, down_weight, precision=HIGHEST))
            weight = gates[pick] * live
            return (accum.at[owner].add(weight[:, None] * result), None)
        mixture, _ = lax.scan(jax.checkpoint(expert_step), jnp.zeros((total, width), jnp.float32), (gate_all, up_all, down_all, owners, picks, alive))
        return (hidden + RESIDUAL * mixture).reshape(rows, length, width)
    result, pullback = jax.vjp(forward, tokens.astype(jnp.float32), norm1_gain.astype(jnp.float32), w_query.astype(jnp.float32), w_key.astype(jnp.float32), w_value.astype(jnp.float32), w_out.astype(jnp.float32), norm2_gain.astype(jnp.float32), w_router.astype(jnp.float32), w_gate.astype(jnp.float32), w_up.astype(jnp.float32), w_down.astype(jnp.float32))
    gradients = pullback(out_grad.astype(jnp.float32))
    return (result.astype(jnp.bfloat16), gradients[0], gradients[1], gradients[2], gradients[3], gradients[4], gradients[5], gradients[6], gradients[7], gradients[8], gradients[9], gradients[10], counts)
```

```python
import functools

import jax
import jax.numpy as jnp
from jax import lax
from jax.experimental import pallas as pl
from jax.experimental.pallas import tpu as pltpu
from jax.sharding import PartitionSpec as P

HEADS = 16
KV_HEADS = 8
HEAD = 64
GROUP = 2
EXPERTS = 16
TOPK = 8

EPSILON = 1e-06
SCORE_SCALE = 0.015625
RESIDUAL = 0.22
THETA = 10000.0
NEGATIVE = -1e30

MESH = pl.DeviceIdType.MESH
ANY = pl.BlockSpec(memory_space=pl.ANY)
VMEM = pl.BlockSpec(memory_space=pltpu.VMEM)


def norm_scale(value):
    return lax.rsqrt(jnp.mean(value * value, axis=-1, keepdims=True) + EPSILON)


def positions_of(segments):
    length = segments.shape[-1]
    index = jnp.arange(length, dtype=jnp.int32)
    change = jnp.concatenate(
        [jnp.ones_like(segments[:, :1]), (segments[:, 1:] != segments[:, :-1]).astype(jnp.int32)],
        axis=1,
    )
    start = lax.cummax(jnp.where(change > 0, index[None, :], 0), axis=1)
    return index[None, :] - start


def rope_tables(positions, width):
    half = width // 2
    frequency = THETA ** (-2.0 * jnp.arange(half, dtype=jnp.float32) / width)
    angle = positions.astype(jnp.float32)[..., None] * frequency
    angle = jnp.concatenate([angle, angle], axis=-1)
    return (jnp.cos(angle), jnp.sin(angle))


def rotate(value, cosine, sine):
    half = value.shape[-1] // 2
    turned = jnp.concatenate([-value[..., half:], value[..., :half]], axis=-1)
    return value * cosine[..., None, :] + turned * sine[..., None, :]


def rotate_back(delta, cosine, sine):
    half = delta.shape[-1] // 2
    moved = delta * sine[..., None, :]
    turned = jnp.concatenate([moved[..., half:], -moved[..., :half]], axis=-1)
    return delta * cosine[..., None, :] + turned


def visible_keys(row_segments, query_segments, first):
    key_index = jnp.arange(row_segments.shape[0], dtype=jnp.int32)
    query_index = first + jnp.arange(query_segments.shape[0], dtype=jnp.int32)
    return (query_segments[:, None] == row_segments[None, :]) & (
        key_index[None, :] <= query_index[:, None]
    )


def row_scores(query_row, row_keys, visible):
    raw = jnp.einsum("ckgd,lkd->kgcl", query_row, row_keys, preferred_element_type=jnp.float32)
    return jnp.where(visible, SCORE_SCALE * raw, NEGATIVE)


def greet_all(n_row, n_seq):
    row, seq = lax.axis_index("row"), lax.axis_index("seq")
    me, total = row * n_seq + seq, n_row * n_seq
    barrier = pltpu.get_barrier_semaphore()

    def greet(step, carry):
        other = (me + step) % total
        pl.semaphore_signal(
            barrier, inc=1, device_id=(other // n_seq, other % n_seq), device_id_type=MESH
        )
        return carry

    lax.fori_loop(1, total, greet, 0)
    pl.semaphore_wait(barrier, total - 1)


def weights_kernel(n_row, n_seq, gate, up, down, held, send, recv, local, pass_send, pass_recv):
    row, seq = lax.axis_index("row"), lax.axis_index("seq")
    me, total = row * n_seq + seq, n_row * n_seq
    core = seq % 2
    rows = gate.shape[1]
    greet_all(n_row, n_seq)

    def transfer(kind, source, step):
        other = (me + step) % total
        other_row, other_seq = other // n_seq, other % n_seq
        return pltpu.make_async_remote_copy(
            src_ref=source.at[other_row * 4 + other_seq % 4],
            dst_ref=held.at[other_seq % 2, kind, pl.ds(pl.multiple_of(me * rows, rows), rows)],
            send_sem=send.at[kind, step],
            recv_sem=recv.at[kind, step],
            device_id=(other_row, other_seq),
            device_id_type=MESH,
        )

    def arrival(kind, source, step):
        other = (me + total - step) % total
        return pltpu.make_async_remote_copy(
            src_ref=source.at[0],
            dst_ref=held.at[core, kind, pl.ds(pl.multiple_of(other * rows, rows), rows)],
            send_sem=send.at[kind, step],
            recv_sem=recv.at[kind, step],
            device_id=(row, (seq + 1) % 2 + seq // 2 * 2),
            device_id_type=MESH,
        )

    sources = (gate, up, down)
    own = [
        pltpu.make_async_copy(
            source.at[row * 4 + seq % 4],
            held.at[core, kind, pl.ds(pl.multiple_of(me * rows, rows), rows)],
            local.at[kind],
        )
        for kind, source in enumerate(sources)
    ]
    for copy in own:
        copy.start()

    def start(step, carry):
        for kind, source in enumerate(sources):
            transfer(kind, source, step).start()
        return carry

    lax.fori_loop(1, total, start, 0)

    def settle(step, carry):
        for kind, source in enumerate(sources):
            arrival(kind, source, step).wait_recv()
        return carry

    lax.fori_loop(1, total, settle, 0)
    for copy in own:
        copy.wait()
    share = pltpu.make_async_remote_copy(
        src_ref=held.at[core],
        dst_ref=held.at[core],
        send_sem=pass_send,
        recv_sem=pass_recv,
        device_id=(row, seq // 2 * 2 + (1 - core)),
        device_id_type=MESH,
    )
    share.start()

    def drain(step, carry):
        for kind, source in enumerate(sources):
            transfer(kind, source, step).wait_send()
        return carry

    lax.fori_loop(1, total, drain, 0)
    share.wait_send()
    pltpu.make_async_remote_copy(
        src_ref=held.at[core],
        dst_ref=held.at[1 - core],
        send_sem=pass_send,
        recv_sem=pass_recv,
        device_id=(row, seq // 2 * 2 + (1 - core)),
        device_id_type=MESH,
    ).wait_recv()


def gather_weights(n_row, n_seq, gate, up, down):
    experts, rows, hidden = gate.shape
    total = n_row * n_seq
    return pl.pallas_call(
        functools.partial(weights_kernel, n_row, n_seq),
        out_shape=jax.ShapeDtypeStruct((2, 3, rows * total, hidden), jnp.bfloat16),
        in_specs=[ANY] * 3,
        out_specs=ANY,
        scratch_shapes=[
            pltpu.SemaphoreType.DMA((3, total)),
            pltpu.SemaphoreType.DMA((3, total)),
            pltpu.SemaphoreType.DMA((3,)),
            pltpu.SemaphoreType.DMA,
            pltpu.SemaphoreType.DMA,
        ],
        compiler_params=pltpu.CompilerParams(collective_id=1, has_side_effects=True),
        name="weights",
    )(gate, up, down)


def grads_kernel(n_row, n_seq, grads, held, send, recv, local):
    row, seq = lax.axis_index("row"), lax.axis_index("seq")
    me, total = row * n_seq + seq, n_row * n_seq
    rows = held.shape[3]
    greet_all(n_row, n_seq)

    def transfer(kind, step):
        other = (me + step) % total
        return pltpu.make_async_remote_copy(
            src_ref=grads.at[kind, pl.ds(pl.multiple_of(other * rows, rows), rows)],
            dst_ref=held.at[kind, seq // 4, row * 4 + seq % 4],
            send_sem=send.at[kind, step],
            recv_sem=recv.at[kind, step],
            device_id=(other // n_seq, other % n_seq),
            device_id_type=MESH,
        )

    def arrival(kind, step):
        other = (me + total - step) % total
        return pltpu.make_async_remote_copy(
            src_ref=grads.at[kind, pl.ds(0, rows)],
            dst_ref=held.at[kind, other % n_seq // 4, other // n_seq * 4 + other % 4],
            send_sem=send.at[kind, step],
            recv_sem=recv.at[kind, step],
            device_id=(other // n_seq, other % n_seq),
            device_id_type=MESH,
        )

    own = [
        pltpu.make_async_copy(
            grads.at[kind, pl.ds(pl.multiple_of(me * rows, rows), rows)],
            held.at[kind, seq // 4, row * 4 + seq % 4],
            local.at[kind],
        )
        for kind in range(3)
    ]
    for copy in own:
        copy.start()

    def start(step, carry):
        for kind in range(3):
            transfer(kind, step).start()
        return carry

    lax.fori_loop(1, total, start, 0)
    for copy in own:
        copy.wait()

    def settle(step, carry):
        for kind in range(3):
            transfer(kind, step).wait_send()
            arrival(kind, step).wait_recv()
        return carry

    lax.fori_loop(1, total, settle, 0)


def scatter_grads(n_row, n_seq, grads):
    _, width, hidden = grads.shape
    total = n_row * n_seq
    held = pl.pallas_call(
        functools.partial(grads_kernel, n_row, n_seq),
        out_shape=jax.ShapeDtypeStruct(
            (3, n_seq // 4, n_row * 4, width // total, hidden), jnp.bfloat16
        ),
        in_specs=[ANY],
        out_specs=ANY,
        scratch_shapes=[
            pltpu.SemaphoreType.DMA((3, total)),
            pltpu.SemaphoreType.DMA((3, total)),
            pltpu.SemaphoreType.DMA((3,)),
        ],
        compiler_params=pltpu.CompilerParams(collective_id=2, has_side_effects=True),
        name="grads",
    )(grads)
    return jnp.sum(held.astype(jnp.float32), axis=1)


NN = (((1,), (0,)), ((), ()))
NT = (((1,), (1,)), ((), ()))
TN = (((0,), (0,)), ((), ()))


def mul(a, b, dims):
    return lax.dot_general(a, b, dims, preferred_element_type=jnp.float32)


def column(row_values):
    return jnp.broadcast_to(row_values, (128, row_values.shape[1])).T


def experts_kernel(
    n_seq, x_in, g_in, gates_in, w_in, y_out, dx_out, dg_out, grad_out,
    xs, gs, gates, w, acc, y_acc, dx_acc, dg_made, y_got, dx_got, dg_got, total_low,
    in_send, in_recv, out_send, out_recv, w_sem, half_send, half_recv, ready, done_sem,
):
    row, seq = lax.axis_index("row"), lax.axis_index("seq")
    core, chip_z, base = seq % 2, seq // 2 % 2, seq // 4 * 4
    width = x_in.shape[1]
    chunk = 256
    mine = (row * 2 + chip_z) * 2

    def peer(step):
        other_row = (row // 2 + step // 4) % 2 * 2 + (row % 2 + step // 2 % 2) % 2
        other_seq = base + (chip_z + step % 2) % 2 * 2 + core
        return (other_row, other_seq)

    sibling = (row, seq // 2 * 2 + (1 - core))
    fetch = [pltpu.make_async_copy(w_in.at[j], w.at[j], w_sem.at[j]) for j in range(2)]
    for copy in fetch:
        copy.start()
    barrier = pltpu.get_barrier_semaphore()

    def greet(step, carry):
        pl.semaphore_signal(barrier, inc=1, device_id=peer(step), device_id_type=MESH)
        return carry

    lax.fori_loop(1, 8, greet, 0)
    pl.semaphore_signal(barrier, inc=1, device_id=sibling, device_id_type=MESH)
    pl.semaphore_wait(barrier, 8)

    def inward(step):
        return [
            pltpu.make_async_remote_copy(
                src_ref=source, dst_ref=target.at[step], send_sem=in_send.at[i, step],
                recv_sem=in_recv.at[i, step], device_id=peer(step), device_id_type=MESH,
            )
            for i, (source, target) in enumerate(((x_in, xs), (g_in, gs), (gates_in, gates)))
        ]

    def outward(step):
        return [
            pltpu.make_async_remote_copy(
                src_ref=source.at[step], dst_ref=target.at[step], send_sem=out_send.at[i, step],
                recv_sem=out_recv.at[i, step], device_id=peer(step), device_id_type=MESH,
            )
            for i, (source, target) in enumerate(((xs, y_got), (gs, dx_got), (dg_made, dg_got)))
        ]

    def send_in(step, carry):
        for copy in inward(step):
            copy.start()
        return carry

    lax.fori_loop(1, 8, send_in, 0)
    xs[0] = x_in[...]
    gs[0] = g_in[...]
    gates[0] = gates_in[...]
    acc[...] = jnp.zeros_like(acc)
    for copy in fetch:
        copy.wait()

    def block(step, carry):
        @pl.when(step > 0)
        def _():
            for copy in inward(step):
                copy.wait_recv()

        y_acc[...] = jnp.zeros_like(y_acc)
        dx_acc[...] = jnp.zeros_like(dx_acc)

        def expert(j, inner_carry):
            gate = column(gates[step, pl.ds(mine + j, 1)])[:, :1]
            x = xs[step]
            a = mul(x, w[j, 0], NN)
            b = mul(x, w[j, 1], NN)
            sigma = jax.nn.sigmoid(a)
            smooth = a * sigma
            inner = (smooth * b).astype(jnp.bfloat16)
            dgate = jnp.zeros((x.shape[0], 1), jnp.float32)
            d_inner = jnp.zeros(a.shape, jnp.float32)
            for lo in range(0, width, chunk):
                part = slice(lo, lo + chunk)
                delta = RESIDUAL * gs[step, :, part].astype(jnp.float32)
                y = mul(inner, w[j, 2, part], NT)
                y_acc[:, part] += gate * y
                dgate += jnp.sum(delta * y, axis=1, keepdims=True)
                dy = (gate * delta).astype(jnp.bfloat16)
                d_inner += mul(dy, w[j, 2, part], NN)
                acc[j, 2, part] += mul(dy, inner, TN)
            da = (d_inner * b * sigma * (1.0 + a * (1.0 - sigma))).astype(jnp.bfloat16)
            db = (d_inner * smooth).astype(jnp.bfloat16)
            for lo in range(0, width, chunk):
                part = slice(lo, lo + chunk)
                x_part = xs[step, :, part]
                acc[j, 0, part] += mul(x_part, da, TN)
                acc[j, 1, part] += mul(x_part, db, TN)
                dx_acc[:, part] += mul(da, w[j, 0, part], NT) + mul(db, w[j, 1, part], NT)
            dg_made[step, j] = jnp.broadcast_to(dgate, (dgate.shape[0], 128)).T[:8]
            return inner_carry

        lax.fori_loop(0, 2, expert, 0)
        xs[step] = y_acc[...].astype(jnp.bfloat16)
        gs[step] = dx_acc[...].astype(jnp.bfloat16)

        @pl.when(step > 0)
        def _():
            for copy in outward(step):
                copy.start()

        return carry

    lax.fori_loop(0, 8, block, 0)

    pl.semaphore_signal(ready, inc=1, device_id=sibling, device_id_type=MESH)
    w[1 - core] = acc[1 - core].astype(jnp.bfloat16)
    pl.semaphore_wait(ready, 1)
    half = pltpu.make_async_remote_copy(
        src_ref=w.at[1 - core], dst_ref=total_low, send_sem=half_send, recv_sem=half_recv,
        device_id=sibling, device_id_type=MESH,
    )
    half.start()
    y_got[0] = xs[0]
    dx_got[0] = gs[0]
    dg_got[0] = dg_made[0]
    half.wait_recv()
    total_low[...] = (acc[core] + total_low[...].astype(jnp.float32)).astype(jnp.bfloat16)
    store = pltpu.make_async_copy(total_low, grad_out, done_sem)
    store.start()

    def settle(step, carry):
        for copy in inward(step):
            copy.wait_send()
        for copy in outward(step):
            copy.wait()
        return carry

    lax.fori_loop(1, 8, settle, 0)
    y_out[...] = sum(y_got[i].astype(jnp.float32) for i in range(8))
    dx_out[...] = sum(dx_got[i].astype(jnp.float32) for i in range(8))
    dg_out[...] = dg_got[...]
    half.wait_send()
    store.wait()


def run_experts(n_row, n_seq, x, g, gates, w):
    tokens, width = x.shape
    hidden = w.shape[3]
    low, full = jnp.bfloat16, jnp.float32
    dma = pltpu.SemaphoreType.DMA
    return pl.pallas_call(
        functools.partial(experts_kernel, n_seq),
        out_shape=(
            jax.ShapeDtypeStruct((tokens, width), full),
            jax.ShapeDtypeStruct((tokens, width), full),
            jax.ShapeDtypeStruct((8, 2, 8, tokens), full),
            jax.ShapeDtypeStruct((3, width, hidden), low),
        ),
        in_specs=[VMEM, VMEM, VMEM, ANY],
        out_specs=(VMEM, VMEM, VMEM, ANY),
        scratch_shapes=[
            pltpu.VMEM((8, tokens, width), low),
            pltpu.VMEM((8, tokens, width), low),
            pltpu.VMEM((8, EXPERTS, tokens), full),
            pltpu.VMEM((2, 3, width, hidden), low),
            pltpu.VMEM((2, 3, width, hidden), full),
            pltpu.VMEM((tokens, width), full),
            pltpu.VMEM((tokens, width), full),
            pltpu.VMEM((8, 2, 8, tokens), full),
            pltpu.VMEM((8, tokens, width), low),
            pltpu.VMEM((8, tokens, width), low),
            pltpu.VMEM((8, 2, 8, tokens), full),
            pltpu.VMEM((3, width, hidden), low),
            dma((3, 8)),
            dma((3, 8)),
            dma((3, 8)),
            dma((3, 8)),
            dma((2,)),
            dma,
            dma,
            pltpu.SemaphoreType.REGULAR,
            dma,
        ],
        compiler_params=pltpu.CompilerParams(
            collective_id=3, has_side_effects=True, vmem_limit_bytes=60 << 20
        ),
        name="experts",
    )(x, g, gates, w)


def body(
    n_row,
    n_seq,
    tokens,
    segment_ids,
    expert_ids,
    norm1_gain,
    w_query,
    w_key,
    w_value,
    w_out,
    norm2_gain,
    w_router,
    w_gate,
    w_up,
    w_down,
    out_grad,
):
    row_count, block_len, width = tokens.shape
    token_count = row_count * block_len
    length = segment_ids.shape[1]
    first = lax.axis_index("seq") * block_len
    gain_one, query_weight, key_weight, value_weight, out_weight, gain_two, router_weight = (
        lax.all_gather(norm1_gain, ("row", "seq"), axis=0, tiled=True),
        lax.all_gather(w_query, ("row", "seq"), axis=0, tiled=True),
        lax.all_gather(w_key, ("row", "seq"), axis=0, tiled=True),
        lax.all_gather(w_value, ("row", "seq"), axis=0, tiled=True),
        lax.all_gather(w_out, ("row", "seq"), axis=1, tiled=True),
        lax.all_gather(norm2_gain, ("row", "seq"), axis=0, tiled=True),
        lax.all_gather(w_router, ("row", "seq"), axis=0, tiled=True),
    )
    expert_weights = gather_weights(n_row, n_seq, w_gate, w_up, jnp.swapaxes(w_down, 1, 2))
    flat = tokens.reshape(token_count, width).astype(jnp.float32)
    scale_one = norm_scale(flat)
    normed = (flat * scale_one * gain_one.astype(jnp.float32)).astype(jnp.bfloat16)
    local_positions = lax.dynamic_slice_in_dim(
        positions_of(segment_ids), first, block_len, axis=1
    ).reshape(token_count)
    local_segments = lax.dynamic_slice_in_dim(segment_ids, first, block_len, axis=1)
    cosine, sine = rope_tables(local_positions, HEAD)
    query = jnp.dot(normed, query_weight, preferred_element_type=jnp.float32).reshape(
        token_count, HEADS, HEAD
    )
    query = (
        rotate(query, cosine, sine)
        .astype(jnp.bfloat16)
        .reshape(row_count, block_len, KV_HEADS, GROUP, HEAD)
    )
    keys = jnp.dot(normed, key_weight, preferred_element_type=jnp.float32).reshape(
        token_count, KV_HEADS, HEAD
    )
    keys = (
        rotate(keys, cosine, sine)
        .astype(jnp.bfloat16)
        .reshape(row_count, block_len, KV_HEADS * HEAD)
    )
    values = (
        jnp.dot(normed, value_weight, preferred_element_type=jnp.float32)
        .astype(jnp.bfloat16)
        .reshape(row_count, block_len, KV_HEADS * HEAD)
    )
    key_rows, value_rows = (
        lax.all_gather(keys, "seq", axis=1, tiled=True),
        lax.all_gather(values, "seq", axis=1, tiled=True),
    )

    def attend_forward(carry, items):
        query_row, row_keys, row_values, row_segments, query_segments = items
        row_keys = row_keys.reshape(length, KV_HEADS, HEAD)
        row_values = row_values.reshape(length, KV_HEADS, HEAD)
        scores = row_scores(query_row, row_keys, visible_keys(row_segments, query_segments, first))
        peak = jnp.max(scores, axis=-1, keepdims=True)
        raised = jnp.exp(scores - peak)
        denominator = jnp.sum(raised, axis=-1, keepdims=True)
        probs = (raised / denominator).astype(jnp.bfloat16)
        mixed_row = jnp.einsum(
            "kgcl,lkd->ckgd", probs, row_values, preferred_element_type=jnp.float32
        )
        return (
            carry,
            (
                mixed_row.astype(jnp.bfloat16).reshape(block_len, HEADS * HEAD),
                peak + jnp.log(denominator),
            ),
        )

    _, (mixed, log_total) = lax.scan(
        attend_forward, None, (query, key_rows, value_rows, segment_ids, local_segments)
    )
    mixed = mixed.reshape(token_count, HEADS * HEAD)
    hidden = flat + RESIDUAL * jnp.dot(mixed, out_weight, preferred_element_type=jnp.float32)
    scale_two = norm_scale(hidden)
    normed_two = (hidden * scale_two * gain_two.astype(jnp.float32)).astype(jnp.bfloat16)
    logits = jnp.dot(normed_two, router_weight, preferred_element_type=jnp.float32)
    routes = expert_ids.reshape(token_count, TOPK)
    picks = jnp.sum(
        (routes[:, :, None] == jnp.arange(EXPERTS, dtype=jnp.int32)[None, None, :]).astype(
            jnp.int32
        ),
        axis=1,
    )
    expert_counts = lax.psum(jnp.sum(picks, axis=0), ("row", "seq"))
    gates = jax.nn.softmax(jnp.where(picks > 0, logits, NEGATIVE), axis=-1)
    gates = jnp.where(picks > 0, gates, 0.0)
    flat_grad = out_grad.reshape(token_count, width)
    mixture, from_experts, gate_grads, expert_grads = run_experts(
        n_row, n_seq, normed_two, flat_grad, gates.T, expert_weights
    )
    layer_out = (
        (hidden + RESIDUAL * mixture).astype(jnp.bfloat16).reshape(row_count, block_len, width)
    )
    grads = scatter_grads(n_row, n_seq, expert_grads)
    row, chip_z = lax.axis_index("row"), lax.axis_index("seq") // 2 % 2
    chip = jnp.arange(8)
    slot = ((chip // 4 + row // 2) % 2) * 4 + ((chip // 2 % 2 + row % 2) % 2) * 2 + (chip + chip_z) % 2
    delta_gates = gate_grads[:, :, 0][slot].reshape(EXPERTS, token_count).T

    delta_out = flat_grad.astype(jnp.float32)
    delta_picked = gates * (delta_gates - jnp.sum(gates * delta_gates, axis=-1, keepdims=True))
    delta_logits = delta_picked.astype(jnp.bfloat16)
    delta_router = jnp.dot(normed_two.T, delta_logits, preferred_element_type=jnp.float32)
    delta_normed_two = from_experts + jnp.dot(
        delta_logits, router_weight.T, preferred_element_type=jnp.float32
    )
    weighted_two = gain_two.astype(jnp.float32) * delta_normed_two
    delta_gain_two = jnp.sum(delta_normed_two * hidden * scale_two, axis=0)
    delta_hidden = (
        delta_out
        + scale_two * weighted_two
        - hidden
        * (scale_two * scale_two * scale_two)
        * jnp.mean(weighted_two * hidden, axis=-1, keepdims=True)
    )
    delta_branch = (RESIDUAL * delta_hidden).astype(jnp.bfloat16)
    delta_out_weight = jnp.dot(mixed.T, delta_branch, preferred_element_type=jnp.float32)
    delta_mixed = (
        jnp.dot(delta_branch, out_weight.T, preferred_element_type=jnp.float32)
        .astype(jnp.bfloat16)
        .reshape(row_count, block_len, KV_HEADS, GROUP, HEAD)
    )

    def score_grads(
        query_row, row_keys, row_values, row_segments, query_segments, delta_row, log_row
    ):
        scores = row_scores(query_row, row_keys, visible_keys(row_segments, query_segments, first))
        probs = jnp.exp(scores - log_row)
        delta_probs = jnp.einsum(
            "ckgd,lkd->kgcl", delta_row, row_values, preferred_element_type=jnp.float32
        )
        inner_sum = jnp.sum(probs * delta_probs, axis=-1, keepdims=True)
        delta_scores = (probs * (delta_probs - inner_sum)).astype(jnp.bfloat16)
        return (probs, delta_scores, inner_sum)

    def attend_backward(carry, items):
        query_row, row_keys, row_values, row_segments, query_segments, delta_row, log_row = items
        row_keys = row_keys.reshape(length, KV_HEADS, HEAD)
        row_values = row_values.reshape(length, KV_HEADS, HEAD)
        probs, delta_scores, inner_sum = score_grads(
            query_row, row_keys, row_values, row_segments, query_segments, delta_row, log_row
        )
        delta_query = (
            jnp.einsum("kgcl,lkd->ckgd", delta_scores, row_keys, preferred_element_type=jnp.float32)
            * SCORE_SCALE
        )
        delta_keys = (
            jnp.einsum(
                "kgcl,ckgd->lkd", delta_scores, query_row, preferred_element_type=jnp.float32
            )
            * SCORE_SCALE
        )
        delta_values = jnp.einsum(
            "kgcl,ckgd->lkd",
            probs.astype(jnp.bfloat16),
            delta_row,
            preferred_element_type=jnp.float32,
        )
        return (
            carry,
            (
                delta_query.reshape(block_len, HEADS * HEAD),
                delta_keys.reshape(length, KV_HEADS * HEAD),
                delta_values.reshape(length, KV_HEADS * HEAD),
            ),
        )

    _, (delta_query, delta_key_rows, delta_value_rows) = lax.scan(
        attend_backward,
        None,
        (query, key_rows, value_rows, segment_ids, local_segments, delta_mixed, log_total),
    )
    delta_keys, delta_values = (
        lax.psum_scatter(delta_key_rows, "seq", scatter_dimension=1, tiled=True),
        lax.psum_scatter(delta_value_rows, "seq", scatter_dimension=1, tiled=True),
    )
    delta_query = (
        rotate_back(delta_query.reshape(token_count, HEADS, HEAD), cosine, sine)
        .astype(jnp.bfloat16)
        .reshape(token_count, HEADS * HEAD)
    )
    delta_keys = (
        rotate_back(delta_keys.reshape(token_count, KV_HEADS, HEAD), cosine, sine)
        .astype(jnp.bfloat16)
        .reshape(token_count, KV_HEADS * HEAD)
    )
    delta_values = delta_values.reshape(token_count, KV_HEADS * HEAD).astype(jnp.bfloat16)
    delta_query_weight = jnp.dot(normed.T, delta_query, preferred_element_type=jnp.float32)
    delta_key_weight = jnp.dot(normed.T, delta_keys, preferred_element_type=jnp.float32)
    delta_value_weight = jnp.dot(normed.T, delta_values, preferred_element_type=jnp.float32)
    delta_normed = (
        jnp.dot(delta_query, query_weight.T, preferred_element_type=jnp.float32)
        + jnp.dot(delta_keys, key_weight.T, preferred_element_type=jnp.float32)
        + jnp.dot(delta_values, value_weight.T, preferred_element_type=jnp.float32)
    )
    weighted_one = gain_one.astype(jnp.float32) * delta_normed
    delta_gain_one = jnp.sum(delta_normed * flat * scale_one, axis=0)
    input_grad = (
        delta_hidden
        + scale_one * weighted_one
        - flat
        * (scale_one * scale_one * scale_one)
        * jnp.mean(weighted_one * flat, axis=-1, keepdims=True)
    )
    dense = (
        lax.psum_scatter(delta_gain_one, ("row", "seq"), scatter_dimension=0, tiled=True),
        lax.psum_scatter(delta_query_weight, ("row", "seq"), scatter_dimension=0, tiled=True),
        lax.psum_scatter(delta_key_weight, ("row", "seq"), scatter_dimension=0, tiled=True),
        lax.psum_scatter(delta_value_weight, ("row", "seq"), scatter_dimension=0, tiled=True),
        lax.psum_scatter(delta_out_weight, ("row", "seq"), scatter_dimension=1, tiled=True),
        lax.psum_scatter(delta_gain_two, ("row", "seq"), scatter_dimension=0, tiled=True),
        lax.psum_scatter(delta_router, ("row", "seq"), scatter_dimension=0, tiled=True),
    )
    return (
        layer_out,
        input_grad.reshape(row_count, block_len, width),
        dense[0],
        dense[1],
        dense[2],
        dense[3],
        dense[4],
        dense[5],
        dense[6],
        grads[0],
        grads[1],
        jnp.swapaxes(grads[2], 1, 2),
        expert_counts,
    )


def solution(mesh):
    in_specs = (
        P("row", "seq", None),
        P("row", None),
        P("seq", "row", None, None),
        P(("row", "seq")),
        P(("row", "seq"), None),
        P(("row", "seq"), None),
        P(("row", "seq"), None),
        P(None, ("row", "seq")),
        P(("row", "seq")),
        P(("row", "seq"), None),
        P(None, ("row", "seq"), None),
        P(None, ("row", "seq"), None),
        P(None, None, ("row", "seq")),
        P("row", "seq", None),
    )
    out_specs = (
        P("row", "seq", None),
        P("row", "seq", None),
        P(("row", "seq")),
        P(("row", "seq"), None),
        P(("row", "seq"), None),
        P(("row", "seq"), None),
        P(None, ("row", "seq")),
        P(("row", "seq")),
        P(("row", "seq"), None),
        P(None, ("row", "seq"), None),
        P(None, ("row", "seq"), None),
        P(None, None, ("row", "seq")),
        P(),
    )
    return jax.shard_map(
        functools.partial(body, mesh.shape["row"], mesh.shape["seq"]),
        mesh=mesh,
        in_specs=in_specs,
        out_specs=out_specs,
        check_vma=False,
    )
```

```python
import functools

import jax
import jax.numpy as jnp
from jax import lax
from jax.experimental import pallas as pl
from jax.experimental.pallas import tpu as pltpu
from jax.sharding import PartitionSpec as P

HEAD = 64
EXPERTS = 16
TOPK = 8

EPSILON = 1e-06
SCORE_SCALE = 0.015625
RESIDUAL = 0.22
THETA = 10000.0
NEGATIVE = -1e30

MESH = pl.DeviceIdType.MESH
ANY = pl.BlockSpec(memory_space=pl.ANY)
VMEM = pl.BlockSpec(memory_space=pltpu.VMEM)


def norm_scale(value):
    return lax.rsqrt(jnp.mean(value * value, axis=-1, keepdims=True) + EPSILON)


def rope_tables(positions, width):
    half = width // 2
    frequency = THETA ** (-2.0 * jnp.arange(half, dtype=jnp.float32) / width)
    angle = positions.astype(jnp.float32)[..., None] * frequency
    angle = jnp.concatenate([angle, angle], axis=-1)
    return (jnp.cos(angle), jnp.sin(angle))


def greet_all(n_row, n_seq):
    row, seq = lax.axis_index("row"), lax.axis_index("seq")
    me, total = row * n_seq + seq, n_row * n_seq
    barrier = pltpu.get_barrier_semaphore()

    def greet(step, carry):
        other = (me + step) % total
        pl.semaphore_signal(
            barrier, inc=1, device_id=(other // n_seq, other % n_seq), device_id_type=MESH
        )
        return carry

    lax.fori_loop(1, total, greet, 0)
    pl.semaphore_wait(barrier, total - 1)


NN = (((1,), (0,)), ((), ()))
NT = (((1,), (1,)), ((), ()))
TN = (((0,), (0,)), ((), ()))


def mul(a, b, dims):
    return lax.dot_general(a, b, dims, preferred_element_type=jnp.float32)


def column(row_values):
    return jnp.broadcast_to(row_values, (128, row_values.shape[1])).T


def peer_of(row, seq, step):
    other_row = (row // 2 + step // 4) % 2 * 2 + (row % 2 + step // 2 % 2) % 2
    other_seq = seq // 4 * 4 + (seq // 2 % 2 + step % 2) % 2 * 2 + seq % 2
    return (other_row, other_seq)


def row_of(row, step):
    return (row // 2 + step // 2) % 2 * 2 + (row % 2 + step % 2) % 2


def remote(source, target, send, recv, device):
    return pltpu.make_async_remote_copy(
        src_ref=source, dst_ref=target, send_sem=send, recv_sem=recv, device_id=device,
        device_id_type=MESH,
    )


def forward_kernel(
    n_row, n_seq, back,
    packed, x_in, g_in, cos_in, sin_in, start_in, picks_in, gate, up, down,
    xtwo_out, gates_out, counts_out, hidden_out, mixed_out, lse_out, normed_out, queries_out, kv_out, weights_out, g_out, held,
    wall, kv, queries, normed, mixed, hidden, lse,
    z_send, z_recv, p_send, p_recv, d_send, d_recv, kv_send, kv_recv, kvd_send, kvd_recv,
    g_send, g_recv, e_send, e_recv, e_local, pass_send, pass_recv, local, store,
):
    row, seq = lax.axis_index("row"), lax.axis_index("seq")
    core, deep, n_deep = seq % 2, seq // 2, n_seq // 2
    me, total = row * n_seq + seq, n_row * n_seq
    sibling = (row, deep * 2 + (1 - core))
    rows = packed.shape[0]
    tokens, width = x_in.shape
    block = tokens // 2
    low, full = jnp.bfloat16, jnp.float32
    slots = kv.shape[0]
    greet_all(n_row, n_seq)

    def part(of_row, of_deep, of_core):
        return wall.at[pl.ds(pl.multiple_of((of_row * n_seq + of_deep * 2 + of_core) * rows, rows), rows)]

    mine = part(row, deep, core)
    own_copy = pltpu.make_async_copy(packed, mine, local.at[0])
    own_copy.start()

    def z_copy(step, source):
        return remote(source, mine, z_send.at[step], z_recv.at[step],
                      (row, (deep + step) % n_deep * 2 + core))

    def plane_copy(step, hop, source):
        here = part(row, (deep + n_deep - hop) % n_deep, core)
        return remote(here if source is None else source, here, p_send.at[hop, step], p_recv.at[hop, step],
                      (row_of(row, step), seq))

    def core_copy(step, hop, source):
        here = part(row_of(row, step), (deep + n_deep - hop) % n_deep, core)
        return remote(here if source is None else source, here, d_send.at[hop, step], d_recv.at[hop, step], sibling)

    def start_z(step, carry):
        z_copy(step, packed).start()
        return carry

    lax.fori_loop(1, n_deep, start_z, 0)
    for step in range(1, 4):
        plane_copy(step, 0, packed).start()
    core_copy(0, 0, packed).start()

    x = x_in[...].astype(full)
    scale_one = norm_scale(x)

    def relay(hop, carry):
        there = part(row, (deep + n_deep - hop) % n_deep, core)
        remote(there, there, z_send.at[hop], z_recv.at[hop], sibling).wait_recv()
        for step in range(1, 4):
            plane_copy(step, hop, None).start()
        core_copy(0, hop, None).start()
        return carry

    lax.fori_loop(1, n_deep, relay, 0)

    def expert_copy(kind, source, step):
        other = (me + step) % total
        other_row, other_seq = other // n_seq, other % n_seq
        return remote(
            source.at[other_row * 4 + other_seq % 4],
            held.at[other_seq % 2, kind, pl.ds(pl.multiple_of(me * rows, rows), rows)],
            e_send.at[kind, step], e_recv.at[kind, step], (other_row, other_seq),
        )

    sources = (gate, up, down)
    expert_own = [
        pltpu.make_async_copy(
            source.at[row * 4 + seq % 4],
            held.at[core, kind, pl.ds(pl.multiple_of(me * rows, rows), rows)],
            e_local.at[kind],
        )
        for kind, source in enumerate(sources)
    ]
    for copy in expert_own:
        copy.start()

    def start_experts(step, carry):
        for kind, source in enumerate(sources):
            expert_copy(kind, source, step).start()
        return carry

    def spread(index, carry):
        hop, step = index // 3, index % 3 + 1
        there = part(row_of(row, step), (deep + n_deep - hop) % n_deep, core)
        remote(there, there, p_send.at[hop, step], p_recv.at[hop, step], sibling).wait_recv()
        core_copy(step, hop, None).start()
        return carry

    lax.fori_loop(0, n_deep * 3, spread, 0)
    lax.fori_loop(1, total, start_experts, 0)
    own_copy.wait()

    def gathered(index, carry):
        hop, step = index // 4, index % 4
        there = part(row_of(row, step), (deep + n_deep - hop) % n_deep, 1 - core)
        remote(there, there, d_send.at[hop, step], d_recv.at[hop, step], sibling).wait_recv()
        return carry

    lax.fori_loop(0, n_deep * 4, gathered, 0)

    small = wall[:, 3072:].astype(full).T
    gain_one, gain_two = small[16:17], small[17:18]
    normed[...] = (x * scale_one * gain_one).astype(low)
    counts_out[...] = jnp.broadcast_to(jnp.sum(wall[:, 3072:].astype(full), axis=0, keepdims=True), (8, 128))

    lane = lax.broadcasted_iota(jnp.int32, (tokens, 128), 1)
    cosine, sine = cos_in[...], sin_in[...]

    def turn(value):
        return value * cosine + jnp.where(lane % 64 < 32, pltpu.roll(value, 96, 1), pltpu.roll(value, 32, 1)) * sine

    for pair in range(4):
        lanes = slice(1024 + 128 * pair, 1152 + 128 * pair)
        key = turn(mul(normed[...], wall[:, lanes], NN)).astype(low)
        lanes = slice(1536 + 128 * pair, 1664 + 128 * pair)
        value = mul(normed[...], wall[:, lanes], NN).astype(low)
        for t in range(2):
            here = slice(block * t, block * (t + 1))
            kv[core, t, :, 128 * pair:128 * (pair + 1)] = key[here]
            kv[core, t, :, 512 + 128 * pair:640 + 128 * pair] = value[here]

    def kv_copy(hop):
        return remote(kv.at[core], kv.at[hop * 2 + core], kv_send.at[hop], kv_recv.at[hop],
                      (row, seq + 2 * hop))

    def kv_pass(hop, of_core):
        there = kv.at[hop * 2 + of_core]
        return remote(there, there, kvd_send.at[hop], kvd_recv.at[hop], sibling)

    for hop in range(1, back + 1):
        @pl.when(deep + hop < n_deep)
        def _():
            kv_copy(hop).start()

        @pl.when(deep < hop)
        def _():
            kv[2 * hop] = jnp.zeros(kv.shape[1:], low)
            kv[2 * hop + 1] = jnp.zeros(kv.shape[1:], low)

    kv_pass(0, core).start()

    def g_copy(step):
        return remote(g_in, g_out.at[step], g_send.at[step], g_recv.at[step], peer_of(row, seq, step))

    def start_g(step, carry):
        g_copy(step).start()
        return carry

    lax.fori_loop(1, 8, start_g, 0)
    g_own = pltpu.make_async_copy(g_in, g_out.at[0], g_send.at[0])
    g_own.start()

    half_lane = lax.broadcasted_iota(jnp.int32, (block, 128), 1) < 64
    for head in range(8):
        both = turn(mul(normed[...], wall[:, 128 * head:128 * (head + 1)], NN))
        for t in range(2):
            value = both[block * t:block * (t + 1)]
            other = pltpu.roll(value, 64, 1)
            if head % 2 == 0:
                first, second = jnp.where(half_lane, value, 0.0), jnp.where(half_lane, other, 0.0)
            else:
                first, second = jnp.where(half_lane, 0.0, other), jnp.where(half_lane, 0.0, value)
            queries[t * 8 + head, :block] = first.astype(low)
            queries[t * 8 + head, block:] = second.astype(low)

    for hop in range(1, back + 1):
        @pl.when(deep >= hop)
        def _():
            remote(kv.at[core], kv.at[hop * 2 + core], kv_send.at[hop], kv_recv.at[hop], sibling).wait_recv()
            kv_pass(hop, core).start()

    kv_pass(0, 1 - core).wait_recv()
    for hop in range(1, back + 1):
        @pl.when(deep >= hop)
        def _():
            kv_pass(hop, 1 - core).wait_recv()

    for t in range(2):
        visible = visibility(deep, seq, slots, block, start_in[block * t:block * (t + 1)])

        def attend(pair, carry):
            lanes = pl.ds(pl.multiple_of(128 * pair, 128), 128)
            value_lanes = pl.ds(pl.multiple_of(512 + 128 * pair, 128), 128)
            values = jnp.concatenate([kv[slot, t, :, value_lanes] for slot in range(slots)], axis=0)
            for half in range(2):
                head = 2 * pair + half
                query = queries[t * 8 + head]
                scores = jnp.concatenate(
                    [mul(query, kv[slot, t, :, lanes], NT) for slot in range(slots)], axis=1
                )
                scores = jnp.where(visible, SCORE_SCALE * scores, NEGATIVE)
                peak = jnp.max(scores, axis=1, keepdims=True)
                raised = jnp.exp(scores - peak)
                denominator = jnp.sum(raised, axis=1, keepdims=True)
                probs = (raised / denominator).astype(low)
                out = mul(probs, values, NN)
                if half == 0:
                    joined = jnp.where(half_lane, out[:block], pltpu.roll(out[block:], 64, 1))
                else:
                    joined = jnp.where(half_lane, pltpu.roll(out[:block], 64, 1), out[block:])
                mixed[block * t:block * (t + 1), pl.ds(pl.multiple_of(128 * head, 128), 128)] = joined.astype(low)
                lse[t] = jnp.where(lane == head, peak + jnp.log(denominator), lse[t])
            return carry

        lax.fori_loop(0, 4, attend, 0)

    for lo in range(0, width, 256):
        branch = mul(mixed[...], wall[lo:lo + 256, 2048:3072], NT)
        hidden[:, lo:lo + 256] = x_in[:, lo:lo + 256].astype(full) + RESIDUAL * branch
    scale_two = norm_scale(hidden[...])
    xtwo_out[...] = (hidden[...] * scale_two * gain_two).astype(low)
    logits = mul(xtwo_out[...], wall[:, 3072:], NN)
    picked = picks_in[...] > 0
    logits = jnp.where(picked, logits, NEGATIVE)
    raised = jnp.where(picked, jnp.exp(logits - jnp.max(logits, axis=1, keepdims=True)), 0.0)
    gates = raised / jnp.sum(raised, axis=1, keepdims=True)
    gates_out[...] = gates.T[:EXPERTS]

    stores = [
        pltpu.make_async_copy(source, target, store.at[i])
        for i, (source, target) in enumerate((
            (wall, weights_out), (kv, kv_out), (queries, queries_out), (normed, normed_out),
            (mixed, mixed_out), (hidden, hidden_out), (lse, lse_out),
        ))
    ]
    for copy in stores:
        copy.start()

    def arrived(step, carry):
        other = (me + total - step) % total
        for kind in range(3):
            there = held.at[core, kind, pl.ds(pl.multiple_of(other * rows, rows), rows)]
            remote(there, there, e_send.at[kind, step], e_recv.at[kind, step], sibling).wait_recv()
        return carry

    lax.fori_loop(1, total, arrived, 0)
    for copy in expert_own:
        copy.wait()
    remote(held.at[core], held.at[core], pass_send, pass_recv, sibling).start()

    def settle_experts(step, carry):
        for kind, source in enumerate(sources):
            expert_copy(kind, source, step).wait_send()
        return carry

    lax.fori_loop(1, total, settle_experts, 0)

    def settle_g(step, carry):
        g_copy(step).wait()
        return carry

    lax.fori_loop(1, 8, settle_g, 0)
    g_own.wait()

    def settle_z(step, carry):
        z_copy(step, packed).wait_send()
        return carry

    lax.fori_loop(1, n_deep, settle_z, 0)

    def settle_plane(index, carry):
        hop, step = index // 4, index % 4
        core_copy(step, hop, None).wait_send()

        @pl.when(step > 0)
        def _():
            plane_copy(step, hop, None).wait_send()

        return carry

    lax.fori_loop(0, n_deep * 4, settle_plane, 0)
    kv_pass(0, core).wait_send()
    for hop in range(1, back + 1):
        @pl.when(deep + hop < n_deep)
        def _():
            kv_copy(hop).wait_send()

        @pl.when(deep >= hop)
        def _():
            kv_pass(hop, core).wait_send()

    for copy in stores:
        copy.wait()
    share = remote(held.at[core], held.at[1 - core], pass_send, pass_recv, sibling)
    share.wait_recv()
    remote(held.at[core], held.at[core], pass_send, pass_recv, sibling).wait_send()


def visibility(deep, seq, slots, block, start):
    key = lax.broadcasted_iota(jnp.int32, (block, block), 1)
    query = lax.broadcasted_iota(jnp.int32, (block, block), 0) + seq * block
    tiles = []
    for slot in range(slots):
        position = key + ((deep - slot // 2) * 2 + slot % 2) * block
        seen = jnp.where((position >= start) & (position <= query), 1.0, 0.0)
        tiles.append(jnp.concatenate([seen, seen], axis=0))
    return jnp.concatenate(tiles, axis=1) > 0.5


def run_forward(n_row, n_seq, length, packed, x, g, cosine, sine, start, picks, gate, up, down):
    tokens, width = x.shape
    experts, rows, hidden = gate.shape
    total, n_deep = n_row * n_seq, n_seq // 2
    block = tokens // 2
    back = window_of(length, block, n_deep)
    slots = 2 * (back + 1)
    low, full = jnp.bfloat16, jnp.float32
    dma = pltpu.SemaphoreType.DMA
    kv = (slots, 2, block, 1024)
    shape = jax.ShapeDtypeStruct
    return pl.pallas_call(
        functools.partial(forward_kernel, n_row, n_seq, back),
        out_shape=(
            shape((tokens, width), low),
            shape((EXPERTS, tokens), full),
            shape((8, 128), full),
            shape((tokens, width), full),
            shape((tokens, 1024), low),
            shape((2, 2 * block, 128), full),
            shape((tokens, width), low),
            shape((16, 2 * block, 128), low),
            shape(kv, low),
            shape((width, packed.shape[1]), low),
            shape((8, tokens, width), low),
            shape((2, 3, width, hidden), low),
        ),
        in_specs=[ANY, VMEM, ANY, VMEM, VMEM, VMEM, VMEM, ANY, ANY, ANY],
        out_specs=(VMEM, VMEM, VMEM) + (ANY,) * 9,
        scratch_shapes=[
            pltpu.VMEM((width, packed.shape[1]), low),
            pltpu.VMEM(kv, low),
            pltpu.VMEM((16, 2 * block, 128), low),
            pltpu.VMEM((tokens, width), low),
            pltpu.VMEM((tokens, 1024), low),
            pltpu.VMEM((tokens, width), full),
            pltpu.VMEM((2, 2 * block, 128), full),
            dma((n_deep,)), dma((n_deep,)),
            dma((n_deep, 4)), dma((n_deep, 4)),
            dma((n_deep, 4)), dma((n_deep, 4)),
            dma((back + 1,)), dma((back + 1,)),
            dma((back + 1,)), dma((back + 1,)),
            dma((8,)), dma((8,)),
            dma((3, total)), dma((3, total)), dma((3,)),
            dma, dma, dma((1,)), dma((7,)),
        ],
        compiler_params=pltpu.CompilerParams(
            collective_id=1, has_side_effects=True, vmem_limit_bytes=60 << 20
        ),
        name="forward",
    )(packed, x, g, cosine, sine, start, picks, gate, up, down)


def experts_kernel(
    n_seq, x_in, gates_in, g_in, w_in, y_made, dx_out, dg_out, grad_out,
    xs, gs, gates, w, acc, y_acc, dx_acc, dg_made, dx_got, dg_got, total_low,
    in_send, in_recv, out_send, out_recv, y_store, w_sem, g_sem, half_send, half_recv, ready, done_sem,
):
    row, seq = lax.axis_index("row"), lax.axis_index("seq")
    core, chip_z = seq % 2, seq // 2 % 2
    width = x_in.shape[1]
    chunk = 256
    mine = (row * 2 + chip_z) * 2
    low, full = jnp.bfloat16, jnp.float32
    sibling = (row, seq // 2 * 2 + (1 - core))
    fetch = [pltpu.make_async_copy(w_in.at[j], w.at[j], w_sem.at[j]) for j in range(2)]
    fetch.append(pltpu.make_async_copy(g_in, gs, g_sem))
    for copy in fetch:
        copy.start()
    barrier = pltpu.get_barrier_semaphore()

    def greet(step, carry):
        pl.semaphore_signal(barrier, inc=1, device_id=peer_of(row, seq, step), device_id_type=MESH)
        return carry

    lax.fori_loop(1, 8, greet, 0)
    pl.semaphore_signal(barrier, inc=1, device_id=sibling, device_id_type=MESH)
    pl.semaphore_wait(barrier, 8)

    def inward(step):
        return [
            remote(source, target.at[step], in_send.at[i, step], in_recv.at[i, step], peer_of(row, seq, step))
            for i, (source, target) in enumerate(((x_in, xs), (gates_in, gates)))
        ]

    def outward(step):
        return [
            remote(source.at[step], target.at[step], out_send.at[i, step], out_recv.at[i, step], peer_of(row, seq, step))
            for i, (source, target) in enumerate(((gs, dx_got), (dg_made, dg_got)))
        ]

    def y_copy(step):
        return pltpu.make_async_copy(xs.at[step], y_made.at[step], y_store.at[step])

    def send_in(step, carry):
        for copy in inward(step):
            copy.start()
        return carry

    lax.fori_loop(1, 8, send_in, 0)
    xs[0] = x_in[...]
    gates[0] = gates_in[...]
    acc[...] = jnp.zeros_like(acc)
    for copy in fetch:
        copy.wait()

    def block(step, carry):
        @pl.when(step > 0)
        def _():
            for copy in inward(step):
                copy.wait_recv()

        y_acc[...] = jnp.zeros_like(y_acc)
        dx_acc[...] = jnp.zeros_like(dx_acc)

        def expert(j, inner_carry):
            gate = column(gates[step, pl.ds(mine + j, 1)])[:, :1]
            x = xs[step]
            a = mul(x, w[j, 0], NN)
            b = mul(x, w[j, 1], NN)
            sigma = jax.nn.sigmoid(a)
            smooth = a * sigma
            inner = (smooth * b).astype(low)
            dgate = jnp.zeros((x.shape[0], 1), full)
            d_inner = jnp.zeros(a.shape, full)
            for lo in range(0, width, chunk):
                part = slice(lo, lo + chunk)
                delta = RESIDUAL * gs[step, :, part].astype(full)
                y = mul(inner, w[j, 2, part], NT)
                y_acc[:, part] += gate * y
                dgate += jnp.sum(delta * y, axis=1, keepdims=True)
                dy = (gate * delta).astype(low)
                d_inner += mul(dy, w[j, 2, part], NN)
                acc[j, 2, part] += mul(dy, inner, TN)
            da = (d_inner * b * sigma * (1.0 + a * (1.0 - sigma))).astype(low)
            db = (d_inner * smooth).astype(low)
            for lo in range(0, width, chunk):
                part = slice(lo, lo + chunk)
                x_part = xs[step, :, part]
                acc[j, 0, part] += mul(x_part, da, TN)
                acc[j, 1, part] += mul(x_part, db, TN)
                dx_acc[:, part] += mul(da, w[j, 0, part], NT) + mul(db, w[j, 1, part], NT)
            dg_made[step, j] = jnp.broadcast_to(dgate, (dgate.shape[0], 128)).T[:8]
            return inner_carry

        lax.fori_loop(0, 2, expert, 0)
        xs[step] = y_acc[...].astype(low)
        y_copy(step).start()
        gs[step] = dx_acc[...].astype(low)

        @pl.when(step > 0)
        def _():
            for copy in outward(step):
                copy.start()

        return carry

    lax.fori_loop(0, 8, block, 0)

    pl.semaphore_signal(ready, inc=1, device_id=sibling, device_id_type=MESH)
    w[1 - core] = acc[1 - core].astype(low)
    pl.semaphore_wait(ready, 1)
    half = remote(w.at[1 - core], total_low, half_send, half_recv, sibling)
    half.start()
    dx_got[0] = gs[0]
    dg_got[0] = dg_made[0]
    half.wait_recv()
    total_low[...] = (acc[core] + total_low[...].astype(full)).astype(low)
    store = pltpu.make_async_copy(total_low, grad_out, done_sem)
    store.start()

    def settle(step, carry):
        for copy in inward(step):
            copy.wait_send()
        for copy in outward(step):
            copy.wait()
        return carry

    lax.fori_loop(1, 8, settle, 0)
    dx_out[...] = sum(dx_got[i].astype(full) for i in range(8))

    def place(step, carry):
        other_row, other_seq = peer_of(row, seq, step)
        chip = other_row * 2 + other_seq // 2 % 2
        for j in range(2):
            dg_out[pl.ds(chip * 2 + j, 1)] = dg_got[step, j, :1]
        y_copy(step).wait()
        return carry

    lax.fori_loop(0, 8, place, 0)
    half.wait_send()
    store.wait()


def run_experts(n_row, n_seq, x, gates, g, w):
    tokens, width = x.shape
    hidden = w.shape[3]
    low, full = jnp.bfloat16, jnp.float32
    dma, shape = pltpu.SemaphoreType.DMA, jax.ShapeDtypeStruct
    return pl.pallas_call(
        functools.partial(experts_kernel, n_seq),
        out_shape=(
            shape((8, tokens, width), low),
            shape((tokens, width), full),
            shape((EXPERTS, tokens), full),
            shape((3, width, hidden), low),
        ),
        in_specs=[VMEM, VMEM, ANY, ANY],
        out_specs=(ANY, VMEM, VMEM, ANY),
        scratch_shapes=[
            pltpu.VMEM((8, tokens, width), low),
            pltpu.VMEM((8, tokens, width), low),
            pltpu.VMEM((8, EXPERTS, tokens), full),
            pltpu.VMEM((2, 3, width, hidden), low),
            pltpu.VMEM((2, 3, width, hidden), full),
            pltpu.VMEM((tokens, width), full),
            pltpu.VMEM((tokens, width), full),
            pltpu.VMEM((8, 2, 8, tokens), full),
            pltpu.VMEM((8, tokens, width), low),
            pltpu.VMEM((8, 2, 8, tokens), full),
            pltpu.VMEM((3, width, hidden), low),
            dma((2, 8)),
            dma((2, 8)),
            dma((2, 8)),
            dma((2, 8)),
            dma((8,)),
            dma((2,)),
            dma,
            dma,
            dma,
            pltpu.SemaphoreType.REGULAR,
            dma,
        ],
        compiler_params=pltpu.CompilerParams(
            collective_id=3, has_side_effects=True, vmem_limit_bytes=60 << 20
        ),
        name="experts",
    )(x, gates, g, w)


def backward_kernel(
    n_row, n_seq, back,
    dense, kv_in, queries_in, normed_in, mixed_in, x_in, g_in, cos_in, sin_in, start_in,
    hidden_in, xtwo_in, gates_in, dgates_in, dx_in, lse_in, y_made, expert_grads,
    y_got, input_out, q_out, k_out, v_out, o_out, small_out, held,
    wall, kv, queries, outs, dq, dqkv, dkv_own, dkv_core, dkv_deep, grads, from_core, from_plane, from_deep,
    load, k_send, k_recv, kd_send, kd_recv, y_send, y_recv, e_send, e_recv, e_local,
    d_send, d_recv, p_send, p_recv, z_send, z_recv,
):
    row, seq = lax.axis_index("row"), lax.axis_index("seq")
    core, deep, n_deep = seq % 2, seq // 2, n_seq // 2
    me, total = row * n_seq + seq, n_row * n_seq
    sibling = (row, deep * 2 + (1 - core))
    rows = q_out.shape[0]
    tokens, width = x_in.shape
    block = tokens // 2
    low, full = jnp.bfloat16, jnp.float32
    slots = kv.shape[0]
    loads = [
        pltpu.make_async_copy(source, target, load.at[i])
        for i, (source, target) in enumerate(((dense, wall), (kv_in, kv), (queries_in, queries)))
    ]
    for copy in loads:
        copy.start()
    greet_all(n_row, n_seq)

    def y_copy(step):
        return remote(y_made.at[step], y_got.at[step], y_send.at[step], y_recv.at[step], peer_of(row, seq, step))

    def start_y(step, carry):
        y_copy(step).start()
        return carry

    lax.fori_loop(1, 8, start_y, 0)

    erows = held.shape[3]

    def expert_copy(kind, step):
        other = (me + step) % total
        return remote(
            expert_grads.at[kind, pl.ds(pl.multiple_of(other * erows, erows), erows)],
            held.at[kind, seq // 4, row * 4 + seq % 4],
            e_send.at[kind, step], e_recv.at[kind, step], (other // n_seq, other % n_seq),
        )

    expert_own = [
        pltpu.make_async_copy(
            expert_grads.at[kind, pl.ds(pl.multiple_of(me * erows, erows), erows)],
            held.at[kind, seq // 4, row * 4 + seq % 4], e_local.at[kind],
        )
        for kind in range(3)
    ]
    for copy in expert_own:
        copy.start()

    def start_experts(step, carry):
        for kind in range(3):
            expert_copy(kind, step).start()
        return carry

    lax.fori_loop(1, total, start_experts, 0)
    for copy in loads:
        copy.wait()

    def upright(value):
        return jnp.concatenate([value, jnp.zeros((128 - value.shape[0], tokens), full)], axis=0).T

    small = wall[:, 3072:].astype(full).T
    gain_one, gain_two = small[16:17], small[17:18]
    gates, dgates = upright(gates_in[...]), upright(dgates_in[...])
    dlogits = (gates * (dgates - jnp.sum(gates * dgates, axis=1, keepdims=True))).astype(low)
    dxtwo = dx_in[...] + mul(dlogits, wall[:, 3072:], NT)
    h = hidden_in[...]
    scale_two = norm_scale(h)
    weighted = gain_two * dxtwo
    dgain_two = jnp.sum(dxtwo * h * scale_two, axis=0, keepdims=True)
    input_out[...] = (
        g_in[...].astype(full)
        + scale_two * weighted
        - h * (scale_two * scale_two * scale_two) * jnp.mean(weighted * h, axis=1, keepdims=True)
    )
    dbranch = (RESIDUAL * input_out[...]).astype(low)
    drouter = mul(xtwo_in[...], dlogits, TN)
    for lo in range(0, width, 256):
        grads[lo:lo + 256, 2048:3072] = mul(dbranch[:, lo:lo + 256], mixed_in[...], TN).astype(low)

    half_lane = lax.broadcasted_iota(jnp.int32, (block, 128), 1) < 64
    for head in range(8):
        both = mul(dbranch, wall[:, 2048 + 128 * head:2176 + 128 * head], NN)
        for t in range(2):
            value = both[block * t:block * (t + 1)]
            other = pltpu.roll(value, 64, 1)
            if head % 2 == 0:
                first, second = jnp.where(half_lane, value, 0.0), jnp.where(half_lane, other, 0.0)
            else:
                first, second = jnp.where(half_lane, 0.0, other), jnp.where(half_lane, 0.0, value)
            outs[t * 8 + head, :block] = first.astype(low)
            outs[t * 8 + head, block:] = second.astype(low)

    lane = lax.broadcasted_iota(jnp.int32, (tokens, 128), 1)
    for t in range(2):
        visible = visibility(deep, seq, slots, block, start_in[block * t:block * (t + 1)])

        def attend(pair, carry):
            lanes = pl.ds(pl.multiple_of(128 * pair, 128), 128)
            value_lanes = pl.ds(pl.multiple_of(512 + 128 * pair, 128), 128)
            keys = jnp.concatenate([kv[slot, t, :, lanes] for slot in range(slots)], axis=0)
            values = jnp.concatenate([kv[slot, t, :, value_lanes] for slot in range(slots)], axis=0)
            dk, dv = 0.0, 0.0
            for half in range(2):
                head = 2 * pair + half
                query, dout = queries[t * 8 + head], outs[t * 8 + head]
                scores = jnp.where(visible, SCORE_SCALE * mul(query, keys, NT), NEGATIVE)
                total_log = jnp.sum(jnp.where(lane == head, lse_in[t], 0.0), axis=1, keepdims=True)
                probs = jnp.exp(scores - total_log)
                dprobs = mul(dout, values, NT)
                inner = jnp.sum(probs * dprobs, axis=1, keepdims=True)
                dscores = (probs * (dprobs - inner)).astype(low)
                dquery = SCORE_SCALE * mul(dscores, keys, NN)
                if half == 0:
                    joined = jnp.where(half_lane, dquery[:block], pltpu.roll(dquery[block:], 64, 1))
                else:
                    joined = jnp.where(half_lane, pltpu.roll(dquery[:block], 64, 1), dquery[block:])
                dq[block * t:block * (t + 1), pl.ds(pl.multiple_of(128 * head, 128), 128)] = joined
                dk += SCORE_SCALE * mul(dscores, query, TN)
                dv += mul(probs.astype(low), dout, TN)
            for slot in range(slots):
                kv[slot, t, :, lanes] = dk[block * slot:block * (slot + 1)].astype(low)
                kv[slot, t, :, value_lanes] = dv[block * slot:block * (slot + 1)].astype(low)

            @pl.when(core == 0)
            def _():
                dkv_own[t, :, lanes] = dk[:block]
                dkv_own[t, :, value_lanes] = dv[:block]

            @pl.when(core == 1)
            def _():
                dkv_own[t, :, lanes] = dk[block:2 * block]
                dkv_own[t, :, value_lanes] = dv[block:2 * block]

            return carry

        lax.fori_loop(0, 4, attend, 0)

    def kd_copy(hop):
        return remote(kv.at[hop * 2 + (1 - core)], dkv_core.at[hop], kd_send.at[hop], kd_recv.at[hop], sibling)

    def k_copy(hop):
        return remote(kv.at[hop * 2 + core], dkv_deep.at[hop], k_send.at[hop], k_recv.at[hop], (row, seq - 2 * hop))

    for hop in range(back, -1, -1):
        @pl.when(deep >= hop)
        def _():
            kd_copy(hop).start()

    for hop in range(back, 0, -1):
        @pl.when(deep >= hop)
        def _():
            kd_copy(hop).wait_recv()
            both = kv[hop * 2 + core].astype(full) + dkv_core[hop].astype(full)
            kv[hop * 2 + core] = both.astype(low)
            k_copy(hop).start()

    cosine, sine = cos_in[...], sin_in[...]

    def turn_back(value):
        return value * cosine - jnp.where(lane % 64 < 32, pltpu.roll(value, 96, 1), pltpu.roll(value, 32, 1)) * sine

    for head in range(8):
        lanes = slice(128 * head, 128 * (head + 1))
        dqkv[:, lanes] = turn_back(dq[:, lanes]).astype(low)
    for lo in range(0, width, 256):
        grads[lo:lo + 256, :1024] = mul(normed_in[:, lo:lo + 256], dqkv[:, :1024], TN).astype(low)

    kd_copy(0).wait_recv()
    dkv_own[...] += dkv_core[0].astype(full)
    for hop in range(1, back + 1):
        @pl.when(deep + hop < n_deep)
        def _():
            remote(kv.at[0], dkv_deep.at[hop], k_send.at[hop], k_recv.at[hop], sibling).wait_recv()
            dkv_own[...] += dkv_deep[hop].astype(full)

    for pair in range(4):
        lanes = slice(128 * pair, 128 * (pair + 1))
        value_lanes = slice(512 + 128 * pair, 640 + 128 * pair)
        dkey = jnp.concatenate([dkv_own[0, :, lanes], dkv_own[1, :, lanes]], axis=0)
        dqkv[:, 1024 + 128 * pair:1152 + 128 * pair] = turn_back(dkey).astype(low)
        dvalue = jnp.concatenate([dkv_own[0, :, value_lanes], dkv_own[1, :, value_lanes]], axis=0)
        dqkv[:, 1536 + 128 * pair:1664 + 128 * pair] = dvalue.astype(low)
    for lo in range(0, width, 256):
        grads[lo:lo + 256, 1024:2048] = mul(normed_in[:, lo:lo + 256], dqkv[:, 1024:], TN).astype(low)
    x = x_in[...].astype(full)
    scale_one = norm_scale(x)
    for lo in range(0, width, 256):
        dq[:, lo:lo + 256] = mul(dqkv[...], wall[lo:lo + 256, :2048], NT)
    dxone = dq[...]
    weighted = gain_one * dxone
    dgain_one = jnp.sum(dxone * x * scale_one, axis=0, keepdims=True)
    input_out[...] = (
        input_out[...]
        + scale_one * weighted
        - x * (scale_one * scale_one * scale_one) * jnp.mean(weighted * x, axis=1, keepdims=True)
    )
    wide = lax.broadcasted_iota(jnp.int32, (width, 128), 1)
    grads[:, 3072:] = jnp.where(
        wide == 16, column(dgain_one), jnp.where(wide == 17, column(dgain_two), drouter)
    ).astype(low)

    def part(of_row, of_deep, of_core):
        return pl.ds(pl.multiple_of((of_row * n_seq + of_deep * 2 + of_core) * rows, rows), rows)

    def d_copy(step, hop):
        there = part(row_of(row, step), (deep + hop) % n_deep, 1 - core)
        return remote(grads.at[there], from_core.at[hop, step], d_send.at[hop, step], d_recv.at[hop, step], sibling)

    def p_copy(step, hop):
        there = part(row_of(row, step), (deep + hop) % n_deep, core)
        return remote(grads.at[there], from_plane.at[hop, step - 1], p_send.at[hop, step], p_recv.at[hop, step],
                      (row_of(row, step), seq))

    def z_copy(hop):
        there = part(row, (deep + hop) % n_deep, core)
        return remote(grads.at[there], from_deep.at[hop], z_send.at[hop], z_recv.at[hop],
                      (row, (deep + hop) % n_deep * 2 + core))

    def start_d(index, carry):
        d_copy(3 - index % 4, n_deep - 1 - index // 4).start()
        return carry

    lax.fori_loop(0, 4 * n_deep, start_d, 0)

    def sum_cores(index, carry):
        step, hop = 3 - index % 4, n_deep - 1 - index // 4
        d_copy(step, hop).wait_recv()
        there = part(row_of(row, step), (deep + hop) % n_deep, core)
        grads[there] = (grads[there].astype(full) + from_core[hop, step].astype(full)).astype(low)

        @pl.when(step > 0)
        def _():
            p_copy(step, hop).start()

        return carry

    lax.fori_loop(0, 4 * n_deep, sum_cores, 0)

    def sum_plane(index, carry):
        hop = n_deep - 1 - index
        there = part(row, (deep + hop) % n_deep, core)
        for step in range(1, 4):
            p_copy(step, hop).wait_recv()
        value = grads[there].astype(full)
        for step in range(1, 4):
            value += from_plane[hop, step - 1].astype(full)
        grads[there] = value.astype(low)

        @pl.when(hop > 0)
        def _():
            z_copy(hop).start()

        return carry

    lax.fori_loop(0, n_deep, sum_plane, 0)

    def settle_y(step, carry):
        y_copy(step).wait()
        return carry

    lax.fori_loop(1, 8, settle_y, 0)
    total_grad = grads[part(row, deep, core)].astype(full)
    for hop in range(1, n_deep):
        z_copy(hop).wait_recv()
        total_grad += from_deep[hop].astype(full)
    q_out[...] = total_grad[:, :1024]
    k_out[...] = total_grad[:, 1024:1536]
    v_out[...] = total_grad[:, 1536:2048]
    o_out[...] = total_grad[:, 2048:3072]
    small_out[...] = total_grad[:, 3072:]

    def settle_d(index, carry):
        hop, step = index // 4, index % 4
        d_copy(step, hop).wait_send()

        @pl.when(step > 0)
        def _():
            p_copy(step, hop).wait_send()

        return carry

    lax.fori_loop(0, 4 * n_deep, settle_d, 0)

    def settle_z(hop, carry):
        z_copy(hop).wait_send()
        return carry

    lax.fori_loop(1, n_deep, settle_z, 0)
    for hop in range(back + 1):
        @pl.when(deep >= hop)
        def _():
            kd_copy(hop).wait_send()
            if hop > 0:
                k_copy(hop).wait_send()

    for copy in expert_own:
        copy.wait()

    def settle_experts(step, carry):
        other = (me + total - step) % total
        for kind in range(3):
            expert_copy(kind, step).wait_send()
            there = held.at[kind, other % n_seq // 4, other // n_seq * 4 + other % 4]
            remote(there, there, e_send.at[kind, step], e_recv.at[kind, step], sibling).wait_recv()
        return carry

    lax.fori_loop(1, total, settle_experts, 0)


def window_of(length, block, n_deep):
    return min((length // 2 + 2 * block - 1) // (2 * block), n_deep - 1)


def run_backward(n_row, n_seq, length, dense, kv, queries, normed, mixed, x, g, cosine, sine, start,
                 hidden, xtwo, gates, dgates, dx, lse, y_made, expert_grads):
    tokens, width = x.shape
    total, n_deep = n_row * n_seq, n_seq // 2
    rows, block = width // total, tokens // 2
    back = window_of(length, block, n_deep)
    slots, columns = kv.shape[0], dense.shape[1]
    low, full = jnp.bfloat16, jnp.float32
    dma, shape = pltpu.SemaphoreType.DMA, jax.ShapeDtypeStruct
    ff = expert_grads.shape[2]
    return pl.pallas_call(
        functools.partial(backward_kernel, n_row, n_seq, back),
        out_shape=(
            shape((8, tokens, width), low),
            shape((tokens, width), full),
            shape((rows, 1024), full),
            shape((rows, 512), full),
            shape((rows, 512), full),
            shape((rows, 1024), full),
            shape((rows, 128), full),
            shape((3, n_seq // 4, n_row * 4, rows, ff), low),
        ),
        in_specs=[ANY] * 3 + [VMEM] * 13 + [ANY] * 2,
        out_specs=(ANY,) + (VMEM,) * 6 + (ANY,),
        scratch_shapes=[
            pltpu.VMEM((width, columns), low),
            pltpu.VMEM(kv.shape, low),
            pltpu.VMEM((16, tokens, 128), low),
            pltpu.VMEM((16, tokens, 128), low),
            pltpu.VMEM((tokens, 1024), full),
            pltpu.VMEM((tokens, 2048), low),
            pltpu.VMEM(kv.shape[1:], full),
            pltpu.VMEM((back + 1,) + kv.shape[1:], low),
            pltpu.VMEM((back + 1,) + kv.shape[1:], low),
            pltpu.VMEM((width, columns), low),
            pltpu.VMEM((n_deep, 4, rows, columns), low),
            pltpu.VMEM((n_deep, 3, rows, columns), low),
            pltpu.VMEM((n_deep, rows, columns), low),
            dma((3,)),
            dma((back + 1,)), dma((back + 1,)), dma((back + 1,)), dma((back + 1,)),
            dma((8,)), dma((8,)),
            dma((3, total)), dma((3, total)), dma((3,)),
            dma((n_deep, 4)), dma((n_deep, 4)), dma((n_deep, 4)), dma((n_deep, 4)),
            dma((n_deep,)), dma((n_deep,)),
        ],
        compiler_params=pltpu.CompilerParams(
            collective_id=2, has_side_effects=True, vmem_limit_bytes=62 << 20
        ),
        name="backward",
    )(dense, kv, queries, normed, mixed, x, g, cosine, sine, start, hidden, xtwo, gates, dgates, dx, lse,
      y_made, expert_grads)


def body(
    n_row,
    n_seq,
    tokens,
    segment_ids,
    expert_ids,
    norm1_gain,
    w_query,
    w_key,
    w_value,
    w_out,
    norm2_gain,
    w_router,
    w_gate,
    w_up,
    w_down,
    out_grad,
):
    row_count, block_len, width = tokens.shape
    token_count = row_count * block_len
    length = segment_ids.shape[1]
    rows = w_query.shape[0]
    first = lax.axis_index("seq") * block_len
    low, full = jnp.bfloat16, jnp.float32

    routes = expert_ids.reshape(token_count, TOPK)
    picks = jnp.sum(
        (routes[:, :, None] == jnp.arange(128, dtype=jnp.int32)[None, None, :]).astype(full), axis=1
    )
    counts = jnp.concatenate([jnp.sum(picks, axis=0)[None, :EXPERTS], jnp.zeros((rows - 1, EXPERTS), full)])
    packed = jnp.concatenate(
        [w_query, w_key, w_value, w_out.T, w_router, norm1_gain[:, None], norm2_gain[:, None],
         jnp.zeros((rows, 14), low), counts.astype(low), jnp.zeros((rows, 80), low)],
        axis=1,
    )
    local_segments = lax.dynamic_slice_in_dim(segment_ids, first, block_len, axis=1)
    start = jnp.sum(
        (segment_ids[:, None, :] < local_segments[:, :, None]).astype(jnp.int32), axis=2
    ).reshape(token_count)
    positions = jnp.tile(first + jnp.arange(block_len, dtype=jnp.int32), row_count) - start
    cosine, sine = rope_tables(positions, HEAD)
    cosine = jnp.concatenate([cosine, cosine], axis=1)
    sine = jnp.concatenate([-sine[:, :32], sine[:, 32:]] * 2, axis=1)
    start = jnp.broadcast_to(start[:, None], (token_count, 128))

    x = tokens.reshape(token_count, width)
    g = out_grad.reshape(token_count, width)
    (xtwo, gates, count_rows, hidden, mixed, lse, normed, queries, kv, dense, group_g, expert_weights) = run_forward(
        n_row, n_seq, length, packed, x, g, cosine, sine, start, picks, w_gate, w_up, jnp.swapaxes(w_down, 1, 2)
    )
    expert_counts = count_rows[0, 32:32 + EXPERTS].astype(jnp.int32)
    y_made, dx, dgates, expert_grads = run_experts(n_row, n_seq, xtwo, gates, group_g, expert_weights)
    y_got, input_grad, dq, dk, dv, do, small, held = run_backward(
        n_row, n_seq, length, dense, kv, queries, normed, mixed, x, g, cosine, sine, start,
        hidden, xtwo, gates, dgates, dx, lse, y_made, expert_grads,
    )
    mixture = y_made[0].astype(full) + jnp.sum(y_got[1:].astype(full), axis=0)
    layer_out = (hidden + RESIDUAL * mixture).astype(low)
    grads = jnp.sum(held.astype(full), axis=1)
    return (
        layer_out.reshape(row_count, block_len, width),
        input_grad.reshape(row_count, block_len, width),
        small[:, 16],
        dq,
        dk,
        dv,
        do.T,
        small[:, 17],
        small[:, :EXPERTS],
        grads[0],
        grads[1],
        jnp.swapaxes(grads[2], 1, 2),
        expert_counts,
    )


def solution(mesh):
    in_specs = (
        P("row", "seq", None),
        P("row", None),
        P("seq", "row", None, None),
        P(("row", "seq")),
        P(("row", "seq"), None),
        P(("row", "seq"), None),
        P(("row", "seq"), None),
        P(None, ("row", "seq")),
        P(("row", "seq")),
        P(("row", "seq"), None),
        P(None, ("row", "seq"), None),
        P(None, ("row", "seq"), None),
        P(None, None, ("row", "seq")),
        P("row", "seq", None),
    )
    out_specs = (
        P("row", "seq", None),
        P("row", "seq", None),
        P(("row", "seq")),
        P(("row", "seq"), None),
        P(("row", "seq"), None),
        P(("row", "seq"), None),
        P(None, ("row", "seq")),
        P(("row", "seq")),
        P(("row", "seq"), None),
        P(None, ("row", "seq"), None),
        P(None, ("row", "seq"), None),
        P(None, None, ("row", "seq")),
        P(),
    )
    return jax.shard_map(
        functools.partial(body, mesh.shape["row"], mesh.shape["seq"]),
        mesh=mesh,
        in_specs=in_specs,
        out_specs=out_specs,
        check_vma=False,
    )
```

```python
import functools

import jax
import jax.numpy as jnp
from jax import lax
from jax.experimental import pallas as pl
from jax.experimental.pallas import tpu as pltpu
from jax.sharding import PartitionSpec as P

HEAD = 64
EXPERTS = 16
TOPK = 8

EPSILON = 1e-06
SCORE_SCALE = 0.015625
RESIDUAL = 0.22
THETA = 10000.0
NEGATIVE = -1e30

MESH = pl.DeviceIdType.MESH
STRIDE = 11
ANY = pl.BlockSpec(memory_space=pl.ANY)
VMEM = pl.BlockSpec(memory_space=pltpu.VMEM)


def norm_scale(value):
    return lax.rsqrt(jnp.mean(value * value, axis=-1, keepdims=True) + EPSILON)


def rope_tables(positions, width):
    half = width // 2
    frequency = THETA ** (-2.0 * jnp.arange(half, dtype=jnp.float32) / width)
    angle = positions.astype(jnp.float32)[..., None] * frequency
    angle = jnp.concatenate([angle, angle], axis=-1)
    return (jnp.cos(angle), jnp.sin(angle))


def greet_all(n_row, n_seq):
    row, seq = lax.axis_index("row"), lax.axis_index("seq")
    me, total = row * n_seq + seq, n_row * n_seq
    barrier = pltpu.get_barrier_semaphore()

    def greet(step, carry):
        other = (me + step) % total
        pl.semaphore_signal(
            barrier, inc=1, device_id=(other // n_seq, other % n_seq), device_id_type=MESH
        )
        return carry

    lax.fori_loop(1, total, greet, 0)
    pl.semaphore_wait(barrier, total - 1)


NN = (((1,), (0,)), ((), ()))
NT = (((1,), (1,)), ((), ()))
TN = (((0,), (0,)), ((), ()))


def mul(a, b, dims):
    return lax.dot_general(a, b, dims, preferred_element_type=jnp.float32)


def column(row_values):
    return jnp.broadcast_to(row_values, (128, row_values.shape[1])).T


def peer_of(row, seq, step):
    other_row = (row // 2 + step // 4) % 2 * 2 + (row % 2 + step // 2 % 2) % 2
    other_seq = seq // 4 * 4 + (seq // 2 % 2 + step % 2) % 2 * 2 + seq % 2
    return (other_row, other_seq)


def row_of(row, step):
    return (row // 2 + step // 2) % 2 * 2 + (row % 2 + step % 2) % 2


def remote(source, target, send, recv, device):
    return pltpu.make_async_remote_copy(
        src_ref=source, dst_ref=target, send_sem=send, recv_sem=recv, device_id=device,
        device_id_type=MESH,
    )


def thirds_of(rows):
    cut = rows * 3 // 8
    rest = (rows - cut) // 2
    return ((0, cut), (cut, rest), (cut + rest, rest))


def tree_rounds(row, seq, own, slots, send, recv):
    thirds = thirds_of(own.shape[0])

    def hop(source, slot, toward, index):
        return remote(source, slot, send.at[index], recv.at[index], peer_of(row, seq, toward))

    def piece(slot, third):
        return slots.at[slot, pl.ds(*thirds[third])]

    first = lambda i: hop(own, slots.at[(1, 2, 4)[i]], (1, 2, 4)[i], i)
    second = lambda i: hop(slots.at[(2, 4, 1)[i]], slots.at[(3, 6, 5)[i]], (1, 2, 4)[i], 3 + i)
    third = lambda i: hop(piece((6, 5, 3)[i], i), piece(7, i), (1, 2, 4)[i], 6 + i)

    def start(make):
        for i in range(3):
            make(i).start()

    def landed(make):
        for i in range(3):
            make(i).wait_recv()

    def round_one():
        start(first)

    def round_two():
        landed(first)
        start(second)

    def round_three():
        landed(second)
        start(third)

    def last():
        landed(third)

    def sent():
        for make in (first, second, third):
            for i in range(3):
                make(i).wait_send()

    return round_one, round_two, round_three, last, sent


def forward_kernel(
    n_row, n_seq, back,
    pack_kv, pack_qo, x_in, g_in, cos_in, sin_in, start_in, picks_in, gate, up, down,
    xtwo_out, gates_out, counts_out, hidden_out, mixed_out, lse_out, normed_out, queries_out, kv_out,
    w_kv_out, w_qo_out, g_out, xs_out, gates_all, held,
    w_kv, w_qo, kv, queries, normed, mixed, hidden, lse,
    z_send, z_recv, p_send, p_recv, d_send, d_recv, kv_send, kv_recv, kvd_send, kvd_recv,
    g_send, g_recv, x_send, x_recv, gate_send, gate_recv, group_local, e_send, e_recv, e_local, pass_send, pass_recv, local, store,
):
    row, seq = lax.axis_index("row"), lax.axis_index("seq")
    core, deep, n_deep = seq % 2, seq // 2, n_seq // 2
    me, total = row * n_seq + seq, n_row * n_seq
    sibling = (row, deep * 2 + (1 - core))
    rows = pack_kv.shape[0]
    tokens, width = x_in.shape
    block = tokens // 2
    low, full = jnp.bfloat16, jnp.float32
    slots = kv.shape[0]
    packs, walls = (pack_kv, pack_qo), (w_kv, w_qo)
    greet_all(n_row, n_seq)

    def part(kind, of_row, of_deep, of_core):
        start = (of_row * n_seq + of_deep * 2 + of_core) * rows
        return walls[kind].at[pl.ds(pl.multiple_of(start, rows), rows)]

    own_copies = [
        pltpu.make_async_copy(packs[kind], part(kind, row, deep, core), local.at[kind]) for kind in range(2)
    ]
    for copy in own_copies:
        copy.start()

    def z_copy(kind, step):
        return remote(packs[kind], part(kind, row, deep, core), z_send.at[kind, step], z_recv.at[kind, step],
                      (row, (deep + step) % n_deep * 2 + core))

    def plane_copy(kind, step, hop, source):
        here = part(kind, row, (deep + n_deep - hop) % n_deep, core)
        return remote(here if source is None else source, here, p_send.at[kind, hop, step], p_recv.at[kind, hop, step],
                      (row_of(row, step), seq))

    def core_copy(kind, step, hop, source):
        here = part(kind, row_of(row, step), (deep + n_deep - hop) % n_deep, core)
        return remote(here if source is None else source, here, d_send.at[kind, hop, step], d_recv.at[kind, hop, step],
                      sibling)

    def dense_start(kind):
        def start_z(step, carry):
            z_copy(kind, step).start()
            return carry

        lax.fori_loop(1, n_deep, start_z, 0)
        for step in range(1, 4):
            plane_copy(kind, step, 0, packs[kind]).start()
        core_copy(kind, 0, 0, packs[kind]).start()

    def dense_relay(kind):
        def relay(hop, carry):
            there = part(kind, row, (deep + n_deep - hop) % n_deep, core)
            remote(there, there, z_send.at[kind, hop], z_recv.at[kind, hop], sibling).wait_recv()
            for step in range(1, 4):
                plane_copy(kind, step, hop, None).start()
            core_copy(kind, 0, hop, None).start()
            return carry

        lax.fori_loop(1, n_deep, relay, 0)

    def dense_finish(kind):
        def spread(index, carry):
            hop, step = index // 3, index % 3 + 1
            there = part(kind, row_of(row, step), (deep + n_deep - hop) % n_deep, core)
            remote(there, there, p_send.at[kind, hop, step], p_recv.at[kind, hop, step], sibling).wait_recv()
            core_copy(kind, step, hop, None).start()
            return carry

        lax.fori_loop(0, n_deep * 3, spread, 0)
        own_copies[kind].wait()

        def gathered(index, carry):
            hop, step = index // 4, index % 4
            there = part(kind, row_of(row, step), (deep + n_deep - hop) % n_deep, 1 - core)
            remote(there, there, d_send.at[kind, hop, step], d_recv.at[kind, hop, step], sibling).wait_recv()
            return carry

        lax.fori_loop(0, n_deep * 4, gathered, 0)

    def expert_copy(kind, source, step):
        other = (me + step) % total
        other_row, other_seq = other // n_seq, other % n_seq
        return remote(
            source.at[other_row * 4 + other_seq % 4],
            held.at[other_seq % 2, kind, pl.ds(pl.multiple_of(me * rows, rows), rows)],
            e_send.at[kind, step], e_recv.at[kind, step], (other_row, other_seq),
        )

    sources = (gate, up, down)
    expert_own = [
        pltpu.make_async_copy(
            source.at[row * 4 + seq % 4],
            held.at[core, kind, pl.ds(pl.multiple_of(me * rows, rows), rows)],
            e_local.at[kind],
        )
        for kind, source in enumerate(sources)
    ]

    def experts_start(*kinds):
        def start_experts(index, carry):
            for kind in kinds:
                expert_copy(kind, sources[kind], index * STRIDE % total).start()
            return carry

        lax.fori_loop(1, total, start_experts, 0)

    g_one, g_two, g_three, g_last, g_sent = tree_rounds(row, seq, g_in, g_out, g_send, g_recv)
    g_own = pltpu.make_async_copy(g_in, g_out.at[0], group_local.at[0])

    dense_start(0)
    dense_start(1)
    for copy in expert_own:
        copy.start()
    g_own.start()
    experts_start(0, 1, 2)
    x = x_in[...].astype(full)
    scale_one = norm_scale(x)
    dense_relay(0)
    dense_finish(0)
    small = w_kv[:, 1024:].astype(full)
    counts_out[...] = jnp.broadcast_to(jnp.sum(small, axis=0, keepdims=True), (8, 128))
    small = small.T
    gain_one, gain_two = small[16:17], small[17:18]
    normed[...] = (x * scale_one * gain_one).astype(low)

    lane = lax.broadcasted_iota(jnp.int32, (tokens, 128), 1)
    cosine, sine = cos_in[...], sin_in[...]

    def turn(value):
        return value * cosine + jnp.where(lane % 64 < 32, pltpu.roll(value, 96, 1), pltpu.roll(value, 32, 1)) * sine

    for pair in range(4):
        lanes = slice(128 * pair, 128 * (pair + 1))
        value_lanes = slice(512 + 128 * pair, 640 + 128 * pair)
        key = turn(mul(normed[...], w_kv[:, lanes], NN)).astype(low)
        value = mul(normed[...], w_kv[:, value_lanes], NN).astype(low)
        for t in range(2):
            here = slice(block * t, block * (t + 1))
            kv[core, t, :, lanes] = key[here]
            kv[core, t, :, value_lanes] = value[here]

    def kv_copy(hop):
        return remote(kv.at[(hop - 1) * 2 + core], kv.at[hop * 2 + core], kv_send.at[hop], kv_recv.at[hop],
                      (row, seq + 2))

    def kv_pass(hop, of_core):
        there = kv.at[hop * 2 + of_core]
        return remote(there, there, kvd_send.at[hop], kvd_recv.at[hop], sibling)

    @pl.when(deep + 1 < n_deep)
    def _():
        kv_copy(1).start()

    for hop in range(1, back + 1):
        @pl.when(deep < hop)
        def _():
            kv[2 * hop] = jnp.zeros(kv.shape[1:], low)
            kv[2 * hop + 1] = jnp.zeros(kv.shape[1:], low)

    kv_pass(0, core).start()
    dense_relay(1)
    g_one()
    dense_finish(1)
    half_lane = lax.broadcasted_iota(jnp.int32, (block, 128), 1) < 64
    for head in range(8):
        both = turn(mul(normed[...], w_qo[:, 128 * head:128 * (head + 1)], NN))
        for t in range(2):
            value = both[block * t:block * (t + 1)]
            other = pltpu.roll(value, 64, 1)
            if head % 2 == 0:
                first, second = jnp.where(half_lane, value, 0.0), jnp.where(half_lane, other, 0.0)
            else:
                first, second = jnp.where(half_lane, 0.0, other), jnp.where(half_lane, 0.0, value)
            queries[t * 8 + head, :block] = first.astype(low)
            queries[t * 8 + head, block:] = second.astype(low)

    for hop in range(1, back + 1):
        @pl.when(deep >= hop)
        def _():
            kv_copy(hop).wait_recv()
            if hop < back:
                @pl.when(deep + 1 < n_deep)
                def _():
                    kv_copy(hop + 1).start()

            kv_pass(hop, core).start()


    kv_pass(0, 1 - core).wait_recv()
    for hop in range(1, back + 1):
        @pl.when(deep >= hop)
        def _():
            kv_pass(hop, 1 - core).wait_recv()

    g_two()
    for t in range(2):
        visible = visibility(deep, seq, slots, block, start_in[block * t:block * (t + 1)])

        def attend(pair, carry):
            lanes = pl.ds(pl.multiple_of(128 * pair, 128), 128)
            value_lanes = pl.ds(pl.multiple_of(512 + 128 * pair, 128), 128)
            values = jnp.concatenate([kv[slot, t, :, value_lanes] for slot in range(slots)], axis=0)
            for half in range(2):
                head = 2 * pair + half
                query = queries[t * 8 + head]
                scores = jnp.concatenate(
                    [mul(query, kv[slot, t, :, lanes], NT) for slot in range(slots)], axis=1
                )
                scores = jnp.where(visible, SCORE_SCALE * scores, NEGATIVE)
                peak = jnp.max(scores, axis=1, keepdims=True)
                raised = jnp.exp(scores - peak)
                denominator = jnp.sum(raised, axis=1, keepdims=True)
                probs = (raised / denominator).astype(low)
                out = mul(probs, values, NN)
                if half == 0:
                    joined = jnp.where(half_lane, out[:block], pltpu.roll(out[block:], 64, 1))
                else:
                    joined = jnp.where(half_lane, pltpu.roll(out[:block], 64, 1), out[block:])
                mixed[block * t:block * (t + 1), pl.ds(pl.multiple_of(128 * head, 128), 128)] = joined.astype(low)
                lse[t] = jnp.where(lane == head, peak + jnp.log(denominator), lse[t])
            return carry

        lax.fori_loop(0, 4, attend, 0)

    g_three()
    for lo in range(0, width, 256):
        branch = mul(mixed[...], w_qo[lo:lo + 256, 1024:], NT)
        hidden[:, lo:lo + 256] = x_in[:, lo:lo + 256].astype(full) + RESIDUAL * branch
    scale_two = norm_scale(hidden[...])
    xtwo_out[...] = (hidden[...] * scale_two * gain_two).astype(low)
    x_one, x_two, x_three, x_last, x_sent = tree_rounds(row, seq, xtwo_out, xs_out, x_send, x_recv)
    x_one()
    logits = mul(xtwo_out[...], w_kv[:, 1024:], NN)
    picked = picks_in[...] > 0
    logits = jnp.where(picked, logits, NEGATIVE)
    raised = jnp.where(picked, jnp.exp(logits - jnp.max(logits, axis=1, keepdims=True)), 0.0)
    gates = raised / jnp.sum(raised, axis=1, keepdims=True)
    gates_out[...] = gates.T[:EXPERTS]

    def gate_copy(step):
        return remote(gates_out, gates_all.at[step], gate_send.at[step], gate_recv.at[step], peer_of(row, seq, step))

    def send_gates(step, carry):
        gate_copy(step).start()
        return carry

    lax.fori_loop(1, 8, send_gates, 0)
    group_own = [
        g_own,
        pltpu.make_async_copy(xtwo_out, xs_out.at[0], group_local.at[1]),
        pltpu.make_async_copy(gates_out, gates_all.at[0], group_local.at[2]),
    ]
    for copy in group_own[1:]:
        copy.start()

    stores = [
        pltpu.make_async_copy(source, target, store.at[i])
        for i, (source, target) in enumerate((
            (w_kv, w_kv_out), (w_qo, w_qo_out), (kv, kv_out), (queries, queries_out), (normed, normed_out),
            (mixed, mixed_out), (hidden, hidden_out), (lse, lse_out),
        ))
    ]
    for copy in stores:
        copy.start()

    x_two()
    x_three()

    def arrived(step, carry):
        other = (me + total - step) % total
        for kind in range(3):
            there = held.at[core, kind, pl.ds(pl.multiple_of(other * rows, rows), rows)]
            remote(there, there, e_send.at[kind, step], e_recv.at[kind, step], sibling).wait_recv()
        return carry

    lax.fori_loop(1, total, arrived, 0)
    for copy in expert_own:
        copy.wait()
    remote(held.at[core], held.at[core], pass_send, pass_recv, sibling).start()

    def settle_experts(step, carry):
        for kind, source in enumerate(sources):
            expert_copy(kind, source, step).wait_send()
        return carry

    lax.fori_loop(1, total, settle_experts, 0)
    g_last()
    g_sent()
    x_last()
    x_sent()
    for copy in group_own:
        copy.wait()

    def settle_gates(step, carry):
        gate_copy(step).wait()
        return carry

    lax.fori_loop(1, 8, settle_gates, 0)
    for kind in range(2):
        def settle_z(step, carry):
            z_copy(kind, step).wait_send()
            return carry

        lax.fori_loop(1, n_deep, settle_z, 0)

        def settle_plane(index, carry):
            hop, step = index // 4, index % 4
            core_copy(kind, step, hop, None).wait_send()

            @pl.when(step > 0)
            def _():
                plane_copy(kind, step, hop, None).wait_send()

            return carry

        lax.fori_loop(0, n_deep * 4, settle_plane, 0)

    kv_pass(0, core).wait_send()
    for hop in range(1, back + 1):
        @pl.when((deep + 1 < n_deep) & (deep >= hop - 1))
        def _():
            kv_copy(hop).wait_send()

        @pl.when(deep >= hop)
        def _():
            kv_pass(hop, core).wait_send()

    for copy in stores:
        copy.wait()
    share = remote(held.at[core], held.at[1 - core], pass_send, pass_recv, sibling)
    share.wait_recv()
    remote(held.at[core], held.at[core], pass_send, pass_recv, sibling).wait_send()


def visibility(deep, seq, slots, block, start):
    key = lax.broadcasted_iota(jnp.int32, (block, block), 1)
    query = lax.broadcasted_iota(jnp.int32, (block, block), 0) + seq * block
    tiles = []
    for slot in range(slots):
        position = key + ((deep - slot // 2) * 2 + slot % 2) * block
        seen = jnp.where((position >= start) & (position <= query), 1.0, 0.0)
        tiles.append(jnp.concatenate([seen, seen], axis=0))
    return jnp.concatenate(tiles, axis=1) > 0.5


def run_forward(n_row, n_seq, length, pack_kv, pack_qo, x, g, cosine, sine, start, picks, gate, up, down):
    tokens, width = x.shape
    experts, rows, hidden = gate.shape
    total, n_deep = n_row * n_seq, n_seq // 2
    block = tokens // 2
    back = window_of(length, block, n_deep)
    slots = 2 * (back + 1)
    low, full = jnp.bfloat16, jnp.float32
    dma = pltpu.SemaphoreType.DMA
    kv = (slots, 2, block, 1024)
    shape = jax.ShapeDtypeStruct
    return pl.pallas_call(
        functools.partial(forward_kernel, n_row, n_seq, back),
        out_shape=(
            shape((tokens, width), low),
            shape((EXPERTS, tokens), full),
            shape((8, 128), full),
            shape((tokens, width), full),
            shape((tokens, 1024), low),
            shape((2, 2 * block, 128), full),
            shape((tokens, width), low),
            shape((16, 2 * block, 128), low),
            shape(kv, low),
            shape((width, pack_kv.shape[1]), low),
            shape((width, pack_qo.shape[1]), low),
            shape((8, tokens, width), low),
            shape((8, tokens, width), low),
            shape((8, EXPERTS, tokens), full),
            shape((2, 3, width, hidden), low),
        ),
        in_specs=[ANY, ANY, VMEM, ANY, VMEM, VMEM, VMEM, VMEM, ANY, ANY, ANY],
        out_specs=(VMEM, VMEM, VMEM) + (ANY,) * 12,
        scratch_shapes=[
            pltpu.VMEM((width, pack_kv.shape[1]), low),
            pltpu.VMEM((width, pack_qo.shape[1]), low),
            pltpu.VMEM(kv, low),
            pltpu.VMEM((16, 2 * block, 128), low),
            pltpu.VMEM((tokens, width), low),
            pltpu.VMEM((tokens, 1024), low),
            pltpu.VMEM((tokens, width), full),
            pltpu.VMEM((2, 2 * block, 128), full),
            dma((2, n_deep)), dma((2, n_deep)),
            dma((2, n_deep, 4)), dma((2, n_deep, 4)),
            dma((2, n_deep, 4)), dma((2, n_deep, 4)),
            dma((back + 1,)), dma((back + 1,)),
            dma((back + 1,)), dma((back + 1,)),
            dma((9,)), dma((9,)), dma((9,)), dma((9,)), dma((8,)), dma((8,)), dma((3,)),
            dma((3, total)), dma((3, total)), dma((3,)),
            dma, dma, dma((2,)), dma((8,)),
        ],
        compiler_params=pltpu.CompilerParams(
            collective_id=1, has_side_effects=True, vmem_limit_bytes=60 << 20
        ),
        name="forward",
    )(pack_kv, pack_qo, x, g, cosine, sine, start, picks, gate, up, down)


def experts_kernel(
    n_seq, xs_in, gs_in, gates_in, w_in, hidden_in, layer_out, dx_out, dg_out, grad_out,
    xs, gs, gates, w, acc, mids, thirds_got, second_got, last_got, dg_made, dg_got, half_made, half_got,
    t_send, t_recv, s_send, s_recv, l_send, l_recv, dg_send, dg_recv, load, half_send, half_recv, done_sem,
):
    row, seq = lax.axis_index("row"), lax.axis_index("seq")
    core, chip_z = seq % 2, seq // 2 % 2
    tokens, width = hidden_in.shape
    ff = w.shape[1] // 6
    mine = (row * 2 + chip_z) * 2
    low, full = jnp.bfloat16, jnp.float32
    sibling = (row, seq // 2 * 2 + (1 - core))
    thirds = thirds_of(tokens)
    columns = ((0, 0), (0, 1), (1, 0), (1, 1), (0, 2), (1, 2))
    loads = [
        pltpu.make_async_copy(w_in.at[j, kind], w.at[:, pl.ds(col * ff, ff)], load.at[col])
        for col, (j, kind) in enumerate(columns)
    ]
    loads += [
        pltpu.make_async_copy(source, target, load.at[6 + i])
        for i, (source, target) in enumerate(((xs_in, xs), (gs_in, gs), (gates_in, gates)))
    ]
    for copy in loads:
        copy.start()
    barrier = pltpu.get_barrier_semaphore()

    def greet(step, carry):
        pl.semaphore_signal(barrier, inc=1, device_id=peer_of(row, seq, step), device_id_type=MESH)
        return carry

    lax.fori_loop(1, 8, greet, 0)
    pl.semaphore_signal(barrier, inc=1, device_id=sibling, device_id_type=MESH)
    acc[...] = jnp.zeros_like(acc)
    pl.semaphore_wait(barrier, 8)
    for copy in loads:
        copy.wait()

    def dg_copy(step):
        return remote(dg_made.at[step], dg_got.at[step], dg_send.at[step], dg_recv.at[step], peer_of(row, seq, step))

    results = (xs, gs)

    def third_copy(i, which):
        rows = pl.ds(*thirds[i])
        return remote(results[which].at[7, rows], thirds_got.at[which, rows], t_send.at[which, i], t_recv.at[which, i],
                      peer_of(row, seq, (1, 2, 4)[i]))

    def second_copy(i, which):
        return remote(results[which].at[(6, 5, 3)[i]], second_got.at[which, i], s_send.at[which, i], s_recv.at[which, i],
                      peer_of(row, seq, (2, 4, 1)[i]))

    def last_copy(i, which):
        slot = (4, 1, 2)[i]
        return remote(results[which].at[slot], last_got.at[which, i], l_send.at[which, i], l_recv.at[which, i],
                      peer_of(row, seq, slot))

    def relay_third(i):
        for which in range(2):
            rows, slot = pl.ds(*thirds[i]), (6, 5, 3)[i]
            third_copy(i, which).wait_recv()
            results[which][slot, rows] = (
                results[which][slot, rows].astype(full) + thirds_got[which, rows].astype(full)
            ).astype(low)
            second_copy(i, which).start()

    def relay_second(i):
        for which in range(2):
            slot = (4, 1, 2)[i]
            second_copy(i, which).wait_recv()
            results[which][slot] = (
                results[which][slot].astype(full) + second_got[which, i].astype(full)
            ).astype(low)
            last_copy(i, which).start()

    def block(index, carry):
        step = 7 - index + jnp.where(index == 3, -1, 0) + jnp.where(index == 4, 1, 0)
        step = jnp.where(index == 5, 1, jnp.where(index == 6, 2, step))
        x, g = xs[step], gs[step]
        for j in range(2):
            gate = column(gates[step, pl.ds(mine + j, 1)])[:, :1]
            a = mul(x, w[:, 2 * j * ff:(2 * j + 1) * ff], NN)
            b = mul(x, w[:, (2 * j + 1) * ff:(2 * j + 2) * ff], NN)
            back = RESIDUAL * mul(g, w[:, (4 + j) * ff:(5 + j) * ff], NN)
            sigma = jax.nn.sigmoid(a)
            smooth = a * sigma
            inner = smooth * b
            dgate = jnp.sum(inner * back, axis=1, keepdims=True)
            back = gate * back
            mids[:, (4 + j) * ff:(5 + j) * ff] = (gate * inner).astype(low)
            mids[:, 2 * j * ff:(2 * j + 1) * ff] = (back * b * (sigma + smooth * (1.0 - sigma))).astype(low)
            mids[:, (2 * j + 1) * ff:(2 * j + 2) * ff] = (back * smooth).astype(low)
            dg_made[step, j] = jnp.broadcast_to(dgate, (tokens, 128)).T[:8]
        for lo in range(0, width, 256):
            part = slice(lo, lo + 256)
            acc[part, :4 * ff] += mul(xs[step, :, part], mids[:, :4 * ff], TN)
            acc[part, 4 * ff:] += mul(gs[step, :, part], mids[:, 4 * ff:], TN)
        for lo in range(0, width, 256):
            part = slice(lo, lo + 256)
            xs[step, :, part] = mul(mids[:, 4 * ff:], w[part, 4 * ff:], NT).astype(low)
            gs[step, :, part] = mul(mids[:, :4 * ff], w[part, :4 * ff], NT).astype(low)

        @pl.when(index < 7)
        def _():
            dg_copy(step).start()

        @pl.when(index == 0)
        def _():
            for i in range(3):
                for which in range(2):
                    third_copy(i, which).start()

        for i in range(3):
            @pl.when(index == 1 + i)
            def _():
                relay_third(i)

            @pl.when(index == 5 + i)
            def _():
                relay_second(i)

        return carry

    lax.fori_loop(0, 8, block, 0)

    def share_of(j):
        wide = acc[:, pl.ds(pl.multiple_of(j * 2 * ff, 128), 2 * ff)]
        thin = RESIDUAL * acc[:, pl.ds(pl.multiple_of((4 + j) * ff, 128), ff)]
        return wide, thin

    wide, thin = share_of(1 - core)
    half_made[:, :2 * ff] = wide.astype(low)
    half_made[:, 2 * ff:] = thin.astype(low)
    half = remote(half_made, half_got, half_send, half_recv, sibling)
    half.start()
    dg_got[0] = dg_made[0]
    half.wait_recv()
    wide, thin = share_of(core)
    half_got[:, :2 * ff] = (wide + half_got[:, :2 * ff].astype(full)).astype(low)
    half_got[:, 2 * ff:] = (thin + half_got[:, 2 * ff:].astype(full)).astype(low)
    store = pltpu.make_async_copy(half_got, grad_out, done_sem)
    store.start()

    def settle(step, carry):
        dg_copy(step).wait()
        return carry

    lax.fori_loop(1, 8, settle, 0)

    def place(step, carry):
        other_row, other_seq = peer_of(row, seq, step)
        chip = other_row * 2 + other_seq // 2 % 2
        for j in range(2):
            dg_out[pl.ds(chip * 2 + j, 1)] = dg_got[step, j, :1]
        return carry

    lax.fori_loop(0, 8, place, 0)
    for i in range(3):
        for which in range(2):
            last_copy(i, which).wait_recv()
    dx_out[...] = gs[0].astype(full) + sum(last_got[1, i].astype(full) for i in range(3))
    mixture = xs[0].astype(full) + sum(last_got[0, i].astype(full) for i in range(3))
    layer_out[...] = (hidden_in[...] + RESIDUAL * mixture).astype(low)
    for i in range(3):
        for which in range(2):
            third_copy(i, which).wait_send()
            second_copy(i, which).wait_send()
            last_copy(i, which).wait_send()
    half.wait_send()
    store.wait()


def run_experts(n_row, n_seq, xs, gs, gates, w, hidden):
    _, tokens, width = xs.shape
    ff = w.shape[3]
    low, full = jnp.bfloat16, jnp.float32
    dma, shape = pltpu.SemaphoreType.DMA, jax.ShapeDtypeStruct
    return pl.pallas_call(
        functools.partial(experts_kernel, n_seq),
        out_shape=(
            shape((tokens, width), low),
            shape((tokens, width), full),
            shape((EXPERTS, tokens), full),
            shape((width, 3 * ff), low),
        ),
        in_specs=[ANY, ANY, ANY, ANY, VMEM],
        out_specs=(VMEM, VMEM, VMEM, ANY),
        scratch_shapes=[
            pltpu.VMEM((8, tokens, width), low),
            pltpu.VMEM((8, tokens, width), low),
            pltpu.VMEM((8, EXPERTS, tokens), full),
            pltpu.VMEM((width, 6 * ff), low),
            pltpu.VMEM((width, 6 * ff), full),
            pltpu.VMEM((tokens, 6 * ff), low),
            pltpu.VMEM((2, tokens, width), low),
            pltpu.VMEM((2, 3, tokens, width), low),
            pltpu.VMEM((2, 3, tokens, width), low),
            pltpu.VMEM((8, 2, 8, tokens), full),
            pltpu.VMEM((8, 2, 8, tokens), full),
            pltpu.VMEM((width, 3 * ff), low),
            pltpu.VMEM((width, 3 * ff), low),
            dma((2, 3)), dma((2, 3)), dma((2, 3)), dma((2, 3)), dma((2, 3)), dma((2, 3)),
            dma((8,)), dma((8,)), dma((9,)),
            dma, dma, dma,
        ],
        compiler_params=pltpu.CompilerParams(
            collective_id=3, has_side_effects=True, vmem_limit_bytes=60 << 20
        ),
        name="experts",
    )(xs, gs, gates, w, hidden)


def backward_kernel(
    n_row, n_seq, back,
    w_kv_in, w_qo_in, kv_in, queries_in, normed_in, mixed_in, x_in, g_in, cos_in, sin_in, start_in,
    hidden_in, xtwo_in, gates_in, dgates_in, dx_in, lse_in, expert_grads,
    input_out, q_out, k_out, v_out, o_out, small_out, held,
    w_kv, w_qo, kv, queries, outs, dq, dqkv, dkv_own, dkv_core, dkv_deep,
    grads_o, grads_q, grads_k, core_o, core_q, core_k, plane_o, plane_q, plane_k, deep_o, deep_q, deep_k,
    load, k_send, k_recv, kd_send, kd_recv, e_send, e_recv, e_local,
    d_send, d_recv, p_send, p_recv, z_send, z_recv,
):
    row, seq = lax.axis_index("row"), lax.axis_index("seq")
    core, deep, n_deep = seq % 2, seq // 2, n_seq // 2
    me, total = row * n_seq + seq, n_row * n_seq
    sibling = (row, deep * 2 + (1 - core))
    rows = q_out.shape[0]
    tokens, width = x_in.shape
    block = tokens // 2
    low, full = jnp.bfloat16, jnp.float32
    slots = kv.shape[0]
    loads = [
        pltpu.make_async_copy(source, target, load.at[i])
        for i, (source, target) in enumerate(((w_kv_in, w_kv), (w_qo_in, w_qo), (kv_in, kv), (queries_in, queries)))
    ]
    for copy in loads:
        copy.start()
    greet_all(n_row, n_seq)

    def expert_copy(step):
        other = (me + step) % total
        return remote(
            expert_grads.at[pl.ds(pl.multiple_of(other * rows, rows), rows)],
            held.at[seq // 4, row * 4 + seq % 4],
            e_send.at[step], e_recv.at[step], (other // n_seq, other % n_seq),
        )

    expert_own = pltpu.make_async_copy(
        expert_grads.at[pl.ds(pl.multiple_of(me * rows, rows), rows)],
        held.at[seq // 4, row * 4 + seq % 4], e_local,
    )
    expert_own.start()

    def experts_start(lo, hi):
        def start_experts(index, carry):
            expert_copy(index * STRIDE % total).start()
            return carry

        lax.fori_loop(lo, hi, start_experts, 0)

    experts_start(1, total * 5 // 8)
    for copy in loads:
        copy.wait()

    made, from_core = (grads_o, grads_q, grads_k), (core_o, core_q, core_k)
    from_plane, from_deep = (plane_o, plane_q, plane_k), (deep_o, deep_q, deep_k)

    def part(of_row, of_deep, of_core):
        return pl.ds(pl.multiple_of((of_row * n_seq + of_deep * 2 + of_core) * rows, rows), rows)

    def d_copy(kind, step, hop):
        there = part(row_of(row, step), (deep + hop) % n_deep, 1 - core)
        return remote(made[kind].at[there], from_core[kind].at[hop, step], d_send.at[kind, hop, step],
                      d_recv.at[kind, hop, step], sibling)

    def p_copy(kind, step, hop):
        there = part(row_of(row, step), (deep + hop) % n_deep, core)
        return remote(made[kind].at[there], from_plane[kind].at[hop, step - 1], p_send.at[kind, hop, step],
                      p_recv.at[kind, hop, step], (row_of(row, step), seq))

    def z_copy(kind, hop):
        there = part(row, (deep + hop) % n_deep, core)
        return remote(made[kind].at[there], from_deep[kind].at[hop], z_send.at[kind, hop], z_recv.at[kind, hop],
                      (row, (deep + hop) % n_deep * 2 + core))

    def dense_start(kind):
        def start_d(index, carry):
            d_copy(kind, 3 - index % 4, n_deep - 1 - index // 4).start()
            return carry

        lax.fori_loop(0, 4 * n_deep, start_d, 0)

    def dense_cores(kind):
        def sum_cores(index, carry):
            step, hop = 3 - index % 4, n_deep - 1 - index // 4
            d_copy(kind, step, hop).wait_recv()
            there = part(row_of(row, step), (deep + hop) % n_deep, core)
            made[kind][there] = (made[kind][there].astype(full) + from_core[kind][hop, step].astype(full)).astype(low)

            @pl.when(step > 0)
            def _():
                p_copy(kind, step, hop).start()

            return carry

        lax.fori_loop(0, 4 * n_deep, sum_cores, 0)

    def dense_plane(kind):
        def sum_plane(index, carry):
            hop = n_deep - 1 - index
            there = part(row, (deep + hop) % n_deep, core)
            for step in range(1, 4):
                p_copy(kind, step, hop).wait_recv()
            value = made[kind][there].astype(full)
            for step in range(1, 4):
                value += from_plane[kind][hop, step - 1].astype(full)
            made[kind][there] = value.astype(low)

            @pl.when(hop > 0)
            def _():
                z_copy(kind, hop).start()

            return carry

        lax.fori_loop(0, n_deep, sum_plane, 0)

    def dense_end(kind):
        value = made[kind][part(row, deep, core)].astype(full)
        for hop in range(1, n_deep):
            z_copy(kind, hop).wait_recv()
            value += from_deep[kind][hop].astype(full)
        return value


    def upright(value):
        return jnp.concatenate([value, jnp.zeros((128 - value.shape[0], tokens), full)], axis=0).T

    small = w_kv[:, 1024:].astype(full).T
    gain_one, gain_two = small[16:17], small[17:18]
    gates, dgates = upright(gates_in[...]), upright(dgates_in[...])
    dlogits = (gates * (dgates - jnp.sum(gates * dgates, axis=1, keepdims=True))).astype(low)
    dxtwo = dx_in[...] + mul(dlogits, w_kv[:, 1024:], NT)
    h = hidden_in[...]
    scale_two = norm_scale(h)
    weighted = gain_two * dxtwo
    dgain_two = jnp.sum(dxtwo * h * scale_two, axis=0, keepdims=True)
    input_out[...] = (
        g_in[...].astype(full)
        + scale_two * weighted
        - h * (scale_two * scale_two * scale_two) * jnp.mean(weighted * h, axis=1, keepdims=True)
    )
    dbranch = (RESIDUAL * input_out[...]).astype(low)
    drouter = mul(xtwo_in[...], dlogits, TN)
    for lo in range(0, width, 256):
        grads_o[lo:lo + 256] = mul(dbranch[:, lo:lo + 256], mixed_in[...], TN).astype(low)
    dense_start(0)

    half_lane = lax.broadcasted_iota(jnp.int32, (block, 128), 1) < 64
    for head in range(8):
        both = mul(dbranch, w_qo[:, 1024 + 128 * head:1152 + 128 * head], NN)
        for t in range(2):
            value = both[block * t:block * (t + 1)]
            other = pltpu.roll(value, 64, 1)
            if head % 2 == 0:
                first, second = jnp.where(half_lane, value, 0.0), jnp.where(half_lane, other, 0.0)
            else:
                first, second = jnp.where(half_lane, 0.0, other), jnp.where(half_lane, 0.0, value)
            outs[t * 8 + head, :block] = first.astype(low)
            outs[t * 8 + head, block:] = second.astype(low)

    dense_cores(0)

    lane = lax.broadcasted_iota(jnp.int32, (tokens, 128), 1)
    for t in range(2):
        visible = visibility(deep, seq, slots, block, start_in[block * t:block * (t + 1)])

        def attend(pair, carry):
            lanes = pl.ds(pl.multiple_of(128 * pair, 128), 128)
            value_lanes = pl.ds(pl.multiple_of(512 + 128 * pair, 128), 128)
            keys = jnp.concatenate([kv[slot, t, :, lanes] for slot in range(slots)], axis=0)
            values = jnp.concatenate([kv[slot, t, :, value_lanes] for slot in range(slots)], axis=0)
            dk, dv = 0.0, 0.0
            for half in range(2):
                head = 2 * pair + half
                query, dout = queries[t * 8 + head], outs[t * 8 + head]
                scores = jnp.where(visible, SCORE_SCALE * mul(query, keys, NT), NEGATIVE)
                total_log = jnp.sum(jnp.where(lane == head, lse_in[t], 0.0), axis=1, keepdims=True)
                probs = jnp.exp(scores - total_log)
                dprobs = mul(dout, values, NT)
                inner = jnp.sum(probs * dprobs, axis=1, keepdims=True)
                dscores = (probs * (dprobs - inner)).astype(low)
                dquery = SCORE_SCALE * mul(dscores, keys, NN)
                if half == 0:
                    joined = jnp.where(half_lane, dquery[:block], pltpu.roll(dquery[block:], 64, 1))
                else:
                    joined = jnp.where(half_lane, pltpu.roll(dquery[:block], 64, 1), dquery[block:])
                dq[block * t:block * (t + 1), pl.ds(pl.multiple_of(128 * head, 128), 128)] = joined
                dk += SCORE_SCALE * mul(dscores, query, TN)
                dv += mul(probs.astype(low), dout, TN)
            for slot in range(slots):
                kv[slot, t, :, lanes] = dk[block * slot:block * (slot + 1)].astype(low)
                kv[slot, t, :, value_lanes] = dv[block * slot:block * (slot + 1)].astype(low)

            @pl.when(core == 0)
            def _():
                dkv_own[t, :, lanes] = dk[:block]
                dkv_own[t, :, value_lanes] = dv[:block]

            @pl.when(core == 1)
            def _():
                dkv_own[t, :, lanes] = dk[block:2 * block]
                dkv_own[t, :, value_lanes] = dv[block:2 * block]

            return carry

        lax.fori_loop(0, 4, attend, 0)
        if t == 0:
            dense_plane(0)

    def kd_copy(hop):
        return remote(kv.at[hop * 2 + (1 - core)], dkv_core.at[hop], kd_send.at[hop], kd_recv.at[hop], sibling)

    def k_copy(hop):
        return remote(kv.at[hop * 2 + core], dkv_deep.at[hop - 1], k_send.at[hop], k_recv.at[hop], (row, seq - 2))

    def k_sum(hop):
        kd_copy(hop).wait_recv()
        kv[hop * 2 + core] = (kv[hop * 2 + core].astype(full) + dkv_core[hop].astype(full)).astype(low)
        if hop < back:
            @pl.when(deep + 1 < n_deep)
            def _():
                k_copy(hop + 1).wait_recv()
                kv[hop * 2 + core] = (kv[hop * 2 + core].astype(full) + dkv_deep[hop].astype(full)).astype(low)

        k_copy(hop).start()

    for hop in range(back, -1, -1):
        @pl.when(deep >= hop)
        def _():
            kd_copy(hop).start()

    @pl.when(deep >= back)
    def _():
        k_sum(back)

    cosine, sine = cos_in[...], sin_in[...]

    def turn_back(value):
        return value * cosine - jnp.where(lane % 64 < 32, pltpu.roll(value, 96, 1), pltpu.roll(value, 32, 1)) * sine

    for head in range(8):
        lanes = slice(128 * head, 128 * (head + 1))
        dqkv[:, lanes] = turn_back(dq[:, lanes]).astype(low)
    for lo in range(0, width, 256):
        grads_q[lo:lo + 256] = mul(normed_in[:, lo:lo + 256], dqkv[:, :1024], TN).astype(low)
    dense_start(1)
    for hop in range(back - 1, 0, -1):
        @pl.when(deep >= hop)
        def _():
            k_sum(hop)

    for lo in range(0, width, 256):
        part_q = slice(lo, lo + 256)
        dq[:, part_q] = mul(dqkv[:, :1024], w_qo[part_q, :1024], NT)
    dense_cores(1)
    experts_start(total * 5 // 8, total)
    kd_copy(0).wait_recv()
    dkv_own[...] += dkv_core[0].astype(full)

    @pl.when(deep + 1 < n_deep)
    def _():
        k_copy(1).wait_recv()
        dkv_own[...] += dkv_deep[0].astype(full)

    for pair in range(4):
        lanes = slice(128 * pair, 128 * (pair + 1))
        value_lanes = slice(512 + 128 * pair, 640 + 128 * pair)
        dkey = jnp.concatenate([dkv_own[0, :, lanes], dkv_own[1, :, lanes]], axis=0)
        dqkv[:, 1024 + 128 * pair:1152 + 128 * pair] = turn_back(dkey).astype(low)
        dvalue = jnp.concatenate([dkv_own[0, :, value_lanes], dkv_own[1, :, value_lanes]], axis=0)
        dqkv[:, 1536 + 128 * pair:1664 + 128 * pair] = dvalue.astype(low)
    for lo in range(0, width, 256):
        grads_k[lo:lo + 256, :1024] = mul(normed_in[:, lo:lo + 256], dqkv[:, 1024:], TN).astype(low)
    x = x_in[...].astype(full)
    scale_one = norm_scale(x)
    for lo in range(0, width, 256):
        part_k = slice(lo, lo + 256)
        dq[:, part_k] += mul(dqkv[:, 1024:], w_kv[part_k, :1024], NT)
    dxone = dq[...]
    weighted = gain_one * dxone
    dgain_one = jnp.sum(dxone * x * scale_one, axis=0, keepdims=True)
    wide = lax.broadcasted_iota(jnp.int32, (width, 128), 1)
    grads_k[:, 1024:] = jnp.where(
        wide == 16, column(dgain_one), jnp.where(wide == 17, column(dgain_two), drouter)
    ).astype(low)
    dense_start(2)
    dense_plane(1)
    input_out[...] = (
        input_out[...]
        + scale_one * weighted
        - x * (scale_one * scale_one * scale_one) * jnp.mean(weighted * x, axis=1, keepdims=True)
    )
    dense_cores(2)
    dense_plane(2)
    o_out[...] = dense_end(0)
    q_out[...] = dense_end(1)
    last = dense_end(2)
    k_out[...] = last[:, :512]
    v_out[...] = last[:, 512:1024]
    small_out[...] = last[:, 1024:]
    for kind in range(3):
        def settle_d(index, carry):
            hop, step = index // 4, index % 4
            d_copy(kind, step, hop).wait_send()

            @pl.when(step > 0)
            def _():
                p_copy(kind, step, hop).wait_send()

            return carry

        lax.fori_loop(0, 4 * n_deep, settle_d, 0)

        def settle_z(hop, carry):
            z_copy(kind, hop).wait_send()
            return carry

        lax.fori_loop(1, n_deep, settle_z, 0)

    for hop in range(back + 1):
        @pl.when(deep >= hop)
        def _():
            kd_copy(hop).wait_send()
            if hop > 0:
                k_copy(hop).wait_send()

    expert_own.wait()

    def settle_experts(step, carry):
        other = (me + total - step) % total
        expert_copy(step).wait_send()
        there = held.at[other % n_seq // 4, other // n_seq * 4 + other % 4]
        remote(there, there, e_send.at[step], e_recv.at[step], sibling).wait_recv()
        return carry

    lax.fori_loop(1, total, settle_experts, 0)


def window_of(length, block, n_deep):
    return min((length // 2 + 2 * block - 1) // (2 * block), n_deep - 1)


def run_backward(n_row, n_seq, length, w_kv, w_qo, kv, queries, normed, mixed, x, g, cosine, sine, start,
                 hidden, xtwo, gates, dgates, dx, lse, expert_grads):
    tokens, width = x.shape
    total, n_deep = n_row * n_seq, n_seq // 2
    rows, block = width // total, tokens // 2
    back = window_of(length, block, n_deep)
    columns = (1024, 1024, w_kv.shape[1])
    low, full = jnp.bfloat16, jnp.float32
    dma, shape = pltpu.SemaphoreType.DMA, jax.ShapeDtypeStruct
    return pl.pallas_call(
        functools.partial(backward_kernel, n_row, n_seq, back),
        out_shape=(
            shape((tokens, width), full),
            shape((rows, 1024), full),
            shape((rows, 512), full),
            shape((rows, 512), full),
            shape((rows, 1024), full),
            shape((rows, 128), full),
            shape((n_seq // 4, n_row * 4, rows, expert_grads.shape[1]), low),
        ),
        in_specs=[ANY] * 4 + [VMEM] * 13 + [ANY],
        out_specs=(VMEM,) * 6 + (ANY,),
        scratch_shapes=[
            pltpu.VMEM(w_kv.shape, low),
            pltpu.VMEM(w_qo.shape, low),
            pltpu.VMEM(kv.shape, low),
            pltpu.VMEM((16, tokens, 128), low),
            pltpu.VMEM((16, tokens, 128), low),
            pltpu.VMEM((tokens, 1024), full),
            pltpu.VMEM((tokens, 2048), low),
            pltpu.VMEM(kv.shape[1:], full),
            pltpu.VMEM((back + 1,) + kv.shape[1:], low),
            pltpu.VMEM((back,) + kv.shape[1:], low),
        ]
        + [pltpu.VMEM((width, c), low) for c in columns]
        + [pltpu.VMEM((n_deep, 4, rows, c), low) for c in columns]
        + [pltpu.VMEM((n_deep, 3, rows, c), low) for c in columns]
        + [pltpu.VMEM((n_deep, rows, c), low) for c in columns]
        + [
            dma((4,)),
            dma((back + 1,)), dma((back + 1,)), dma((back + 1,)), dma((back + 1,)),
            dma((total,)), dma((total,)), dma,
            dma((3, n_deep, 4)), dma((3, n_deep, 4)), dma((3, n_deep, 4)), dma((3, n_deep, 4)),
            dma((3, n_deep)), dma((3, n_deep)),
        ],
        compiler_params=pltpu.CompilerParams(
            collective_id=2, has_side_effects=True, vmem_limit_bytes=62 << 20
        ),
        name="backward",
    )(w_kv, w_qo, kv, queries, normed, mixed, x, g, cosine, sine, start, hidden, xtwo, gates, dgates, dx, lse,
      expert_grads)


def body(
    n_row,
    n_seq,
    tokens,
    segment_ids,
    expert_ids,
    norm1_gain,
    w_query,
    w_key,
    w_value,
    w_out,
    norm2_gain,
    w_router,
    w_gate,
    w_up,
    w_down,
    out_grad,
):
    row_count, block_len, width = tokens.shape
    token_count = row_count * block_len
    length = segment_ids.shape[1]
    rows, ff = w_query.shape[0], w_gate.shape[2]
    first = lax.axis_index("seq") * block_len
    low, full = jnp.bfloat16, jnp.float32

    routes = expert_ids.reshape(token_count, TOPK)
    picks = jnp.sum(
        (routes[:, :, None] == jnp.arange(128, dtype=jnp.int32)[None, None, :]).astype(full), axis=1
    )
    counts = jnp.concatenate([jnp.sum(picks, axis=0)[None, :EXPERTS], jnp.zeros((rows - 1, EXPERTS), full)])
    pack_kv = jnp.concatenate(
        [w_key, w_value, w_router, norm1_gain[:, None], norm2_gain[:, None],
         jnp.zeros((rows, 14), low), counts.astype(low), jnp.zeros((rows, 80), low)],
        axis=1,
    )
    pack_qo = jnp.concatenate([w_query, w_out.T], axis=1)
    local_segments = lax.dynamic_slice_in_dim(segment_ids, first, block_len, axis=1)
    start = jnp.sum(
        (segment_ids[:, None, :] < local_segments[:, :, None]).astype(jnp.int32), axis=2
    ).reshape(token_count)
    positions = jnp.tile(first + jnp.arange(block_len, dtype=jnp.int32), row_count) - start
    cosine, sine = rope_tables(positions, HEAD)
    cosine = jnp.concatenate([cosine, cosine], axis=1)
    sine = jnp.concatenate([-sine[:, :32], sine[:, 32:]] * 2, axis=1)
    start = jnp.broadcast_to(start[:, None], (token_count, 128))

    x = tokens.reshape(token_count, width)
    g = out_grad.reshape(token_count, width)
    (xtwo, gates, count_rows, hidden, mixed, lse, normed, queries, kv, w_kv, w_qo, group_g, group_x, group_gates, expert_weights) = run_forward(
        n_row, n_seq, length, pack_kv, pack_qo, x, g, cosine, sine, start, picks, w_gate, w_up, jnp.swapaxes(w_down, 1, 2)
    )
    expert_counts = count_rows[0, 32:32 + EXPERTS].astype(jnp.int32)
    layer_out, dx, dgates, expert_grads = run_experts(
        n_row, n_seq, group_x, group_g, group_gates, expert_weights, hidden
    )
    input_grad, dq, dk, dv, do, small, held = run_backward(
        n_row, n_seq, length, w_kv, w_qo, kv, queries, normed, mixed, x, g, cosine, sine, start,
        hidden, xtwo, gates, dgates, dx, lse, expert_grads,
    )
    grads = jnp.sum(held.astype(full), axis=0)
    return (
        layer_out.reshape(row_count, block_len, width),
        input_grad.reshape(row_count, block_len, width),
        small[:, 16],
        dq,
        dk,
        dv,
        do.T,
        small[:, 17],
        small[:, :EXPERTS],
        grads[:, :, :ff],
        grads[:, :, ff:2 * ff],
        jnp.swapaxes(grads[:, :, 2 * ff:], 1, 2),
        expert_counts,
    )


def solution(mesh):
    in_specs = (
        P("row", "seq", None),
        P("row", None),
        P("seq", "row", None, None),
        P(("row", "seq")),
        P(("row", "seq"), None),
        P(("row", "seq"), None),
        P(("row", "seq"), None),
        P(None, ("row", "seq")),
        P(("row", "seq")),
        P(("row", "seq"), None),
        P(None, ("row", "seq"), None),
        P(None, ("row", "seq"), None),
        P(None, None, ("row", "seq")),
        P("row", "seq", None),
    )
    out_specs = (
        P("row", "seq", None),
        P("row", "seq", None),
        P(("row", "seq")),
        P(("row", "seq"), None),
        P(("row", "seq"), None),
        P(("row", "seq"), None),
        P(None, ("row", "seq")),
        P(("row", "seq")),
        P(("row", "seq"), None),
        P(None, ("row", "seq"), None),
        P(None, ("row", "seq"), None),
        P(None, None, ("row", "seq")),
        P(),
    )
    return jax.shard_map(
        functools.partial(body, mesh.shape["row"], mesh.shape["seq"]),
        mesh=mesh,
        in_specs=in_specs,
        out_specs=out_specs,
        check_vma=False,
    )
```

```python
import functools

import jax
import jax.numpy as jnp
import numpy as np
from jax import lax
from jax.experimental import pallas as pl
from jax.experimental.pallas import tpu as pltpu
from jax.sharding import PartitionSpec as P

HEAD = 64
EXPERTS = 16
TOPK = 8

EPSILON = 1e-06
SCORE_SCALE = 0.015625
RESIDUAL = 0.22
THETA = 10000.0
NEGATIVE = -1e30

MESH = pl.DeviceIdType.MESH
STRIDE = 11
ANY = pl.BlockSpec(memory_space=pl.ANY)
VMEM = pl.BlockSpec(memory_space=pltpu.VMEM)


def norm_scale(value):
    return lax.rsqrt(jnp.mean(value * value, axis=-1, keepdims=True) + EPSILON)


def greet_all(n_row, n_seq, wait=True):
    row, seq = lax.axis_index("row"), lax.axis_index("seq")
    me, total = row * n_seq + seq, n_row * n_seq
    barrier = pltpu.get_barrier_semaphore()

    def greet(step, carry):
        other = (me + step) % total
        pl.semaphore_signal(
            barrier, inc=1, device_id=(other // n_seq, other % n_seq), device_id_type=MESH
        )
        return carry

    lax.fori_loop(1, total, greet, 0)
    if wait:
        pl.semaphore_wait(barrier, total - 1)


NN = (((1,), (0,)), ((), ()))
NT = (((1,), (1,)), ((), ()))
TN = (((0,), (0,)), ((), ()))


def mul(a, b, dims):
    return lax.dot_general(a, b, dims, preferred_element_type=jnp.float32)


def column(row_values):
    return jnp.broadcast_to(row_values, (128, row_values.shape[1])).T


def peer_of(row, seq, step):
    other_row = (row // 2 + step // 4) % 2 * 2 + (row % 2 + step // 2 % 2) % 2
    other_seq = seq // 4 * 4 + (seq // 2 % 2 + step % 2) % 2 * 2 + seq % 2
    return (other_row, other_seq)


def row_of(row, step):
    return (row // 2 + step // 2) % 2 * 2 + (row % 2 + step % 2) % 2


def remote(source, target, send, recv, device):
    return pltpu.make_async_remote_copy(
        src_ref=source, dst_ref=target, send_sem=send, recv_sem=recv, device_id=device,
        device_id_type=MESH,
    )


def thirds_of(rows):
    cut = rows * 3 // 8
    rest = (rows - cut) // 2
    return ((0, cut), (cut, rest), (cut + rest, rest))


def tree_rounds(row, seq, own, slots, send, recv):
    thirds = thirds_of(own.shape[0])

    def hop(source, slot, toward, index):
        return remote(source, slot, send.at[index], recv.at[index], peer_of(row, seq, toward))

    def piece(slot, third):
        return slots.at[slot, pl.ds(*thirds[third])]

    first = lambda i: hop(own, slots.at[(1, 2, 4)[i]], (1, 2, 4)[i], i)
    second = lambda i: hop(slots.at[(2, 4, 1)[i]], slots.at[(3, 6, 5)[i]], (1, 2, 4)[i], 3 + i)
    third = lambda i: hop(piece((6, 5, 3)[i], i), piece(7, i), (1, 2, 4)[i], 6 + i)

    def start(make):
        for i in range(3):
            make(i).start()

    def landed(make):
        for i in range(3):
            make(i).wait_recv()

    def round_one():
        start(first)

    def round_two():
        landed(first)
        start(second)

    def round_three():
        landed(second)
        start(third)

    def last():
        landed(third)

    def sent():
        for make in (first, second, third):
            for i in range(3):
                make(i).wait_send()

    return round_one, round_two, round_three, last, sent


def forward_kernel(
    n_row, n_seq, back,
    key_in, value_in, query_in, out_in, small_in, turns_in, segments_in, ids_in, x_in, g_in, gate, up, down,
    cos_in, sin_in, start_in, xtwo_out, gates_out, counts_out, hidden_out, mixed_out, lse_out, normed_out, queries_out, kv_out,
    w_kv_out, w_qo_out, g_out, xs_out, gates_all, held,
    pack_kv, pack_qo, upright, picks_in, w_kv, w_qo, kv, queries, normed, mixed, hidden, lse,
    z_send, z_recv, p_send, p_recv, d_send, d_recv, kv_send, kv_recv, kvd_send, kvd_recv,
    g_send, g_recv, x_send, x_recv, gate_send, gate_recv, group_local, e_send, e_recv, e_local, pass_send, pass_recv, local, store,
):
    row, seq = lax.axis_index("row"), lax.axis_index("seq")
    core, deep, n_deep = seq % 2, seq // 2, n_seq // 2
    me, total = row * n_seq + seq, n_row * n_seq
    sibling = (row, deep * 2 + (1 - core))
    rows = key_in.shape[0]
    tokens, width = x_in.shape
    block = tokens // 2
    low, full = jnp.bfloat16, jnp.float32
    slots = kv.shape[0]
    packs, walls = (pack_kv, pack_qo), (w_kv, w_qo)
    greet_all(n_row, n_seq, False)

    sublane = lax.broadcasted_iota(jnp.int32, (128, 128), 0)
    for t in range(2):
        chosen = jnp.zeros((128, block), full)
        for choice in range(TOPK):
            chosen += jnp.where(ids_in[t, choice:choice + 1] == sublane, 1.0, 0.0)
        picks_in[block * t:block * (t + 1)] = chosen.T
    count = jnp.broadcast_to(jnp.sum(picks_in[...], axis=0, keepdims=True), (8, 128))
    upright[...] = jnp.zeros_like(upright)
    upright[:small_in.shape[0], :rows] = small_in[...]
    small = upright[...].T[:rows]
    counts = jnp.where(sublane[:rows] == 0, pltpu.roll(count, 32, 1)[:1], 0.0)
    pack_kv[:, :512] = key_in[...]
    pack_kv[:, 512:1024] = value_in[...]
    pack_kv[:, 1024:] = (small + counts).astype(low)
    pack_qo[:, :1024] = query_in[...]
    pack_qo[:, 1024:] = out_in[...]
    pl.semaphore_wait(pltpu.get_barrier_semaphore(), total - 1)

    def part(kind, of_row, of_deep, of_core):
        start = (of_row * n_seq + of_deep * 2 + of_core) * rows
        return walls[kind].at[pl.ds(pl.multiple_of(start, rows), rows)]

    own_copies = [
        pltpu.make_async_copy(packs[kind], part(kind, row, deep, core), local.at[kind]) for kind in range(2)
    ]
    for copy in own_copies:
        copy.start()

    def z_copy(kind, step):
        return remote(packs[kind], part(kind, row, deep, core), z_send.at[kind, step], z_recv.at[kind, step],
                      (row, (deep + step) % n_deep * 2 + core))

    def plane_copy(kind, step, hop, source):
        here = part(kind, row, (deep + n_deep - hop) % n_deep, core)
        return remote(here if source is None else source, here, p_send.at[kind, hop, step], p_recv.at[kind, hop, step],
                      (row_of(row, step), seq))

    def core_copy(kind, step, hop, source):
        here = part(kind, row_of(row, step), (deep + n_deep - hop) % n_deep, core)
        return remote(here if source is None else source, here, d_send.at[kind, hop, step], d_recv.at[kind, hop, step],
                      sibling)

    def dense_start(kind):
        def start_z(step, carry):
            z_copy(kind, step).start()
            return carry

        lax.fori_loop(1, n_deep, start_z, 0)
        for step in range(1, 4):
            plane_copy(kind, step, 0, packs[kind]).start()
        core_copy(kind, 0, 0, packs[kind]).start()

    def dense_relay(kind):
        def relay(hop, carry):
            there = part(kind, row, (deep + n_deep - hop) % n_deep, core)
            remote(there, there, z_send.at[kind, hop], z_recv.at[kind, hop], sibling).wait_recv()
            for step in range(1, 4):
                plane_copy(kind, step, hop, None).start()
            core_copy(kind, 0, hop, None).start()
            return carry

        lax.fori_loop(1, n_deep, relay, 0)

    def dense_finish(kind):
        def spread(index, carry):
            hop, step = index // 3, index % 3 + 1
            there = part(kind, row_of(row, step), (deep + n_deep - hop) % n_deep, core)
            remote(there, there, p_send.at[kind, hop, step], p_recv.at[kind, hop, step], sibling).wait_recv()
            core_copy(kind, step, hop, None).start()
            return carry

        lax.fori_loop(0, n_deep * 3, spread, 0)
        own_copies[kind].wait()

        def gathered(index, carry):
            hop, step = index // 4, index % 4
            there = part(kind, row_of(row, step), (deep + n_deep - hop) % n_deep, 1 - core)
            remote(there, there, d_send.at[kind, hop, step], d_recv.at[kind, hop, step], sibling).wait_recv()
            return carry

        lax.fori_loop(0, n_deep * 4, gathered, 0)

    def expert_copy(kind, source, step):
        other = (me + step) % total
        other_row, other_seq = other // n_seq, other % n_seq
        return remote(
            source.at[other_row * 4 + other_seq % 4],
            held.at[other_seq % 2, kind, pl.ds(pl.multiple_of(me * rows, rows), rows)],
            e_send.at[kind, step], e_recv.at[kind, step], (other_row, other_seq),
        )

    sources = (gate, up, down)
    expert_own = [
        pltpu.make_async_copy(
            source.at[row * 4 + seq % 4],
            held.at[core, kind, pl.ds(pl.multiple_of(me * rows, rows), rows)],
            e_local.at[kind],
        )
        for kind, source in enumerate(sources)
    ]

    def experts_start(lo, hi):
        def start_experts(index, carry):
            for kind in range(3):
                expert_copy(kind, sources[kind], index * STRIDE % total).start()
            return carry

        lax.fori_loop(lo, hi, start_experts, 0)

    g_one, g_two, g_three, g_last, g_sent = tree_rounds(row, seq, g_in, g_out, g_send, g_recv)
    g_own = pltpu.make_async_copy(g_in, g_out.at[0], group_local.at[0])

    dense_start(0)
    dense_start(1)
    for copy in expert_own:
        copy.start()
    g_own.start()
    experts_start(1, total * 5 // 8)
    x = x_in[...].astype(full)
    scale_one = norm_scale(x)
    for t in range(2):
        own = segments_in[t:t + 1, pl.ds(pl.multiple_of(seq * block, block), block)].astype(full)
        own = column(own)
        smaller = jnp.zeros((block, 128), full)
        for lo in range(0, segments_in.shape[1], 128):
            smaller += jnp.where(segments_in[t:t + 1, lo:lo + 128].astype(full) < own, 1.0, 0.0)
        begin = jnp.broadcast_to(jnp.sum(smaller, axis=1, keepdims=True), (block, 128))
        start_in[block * t:block * (t + 1)] = begin.astype(jnp.int32)
        place = lax.broadcasted_iota(jnp.int32, (block, 128), 0) + seq * block
        angle = (place.astype(full) - begin) * turns_in[:1]
        cos_in[block * t:block * (t + 1)] = jnp.cos(angle)
        sin_in[block * t:block * (t + 1)] = jnp.sin(angle) * turns_in[1:2]

    dense_relay(0)
    dense_finish(0)
    small = w_kv[:, 1024:].astype(full)
    counts_out[...] = jnp.broadcast_to(jnp.sum(small, axis=0, keepdims=True), (8, 128))
    small = small.T
    gain_one, gain_two = small[16:17], small[17:18]
    normed[...] = (x * scale_one * gain_one).astype(low)

    lane = lax.broadcasted_iota(jnp.int32, (tokens, 128), 1)
    cosine, sine = cos_in[...], sin_in[...]

    def turn(value):
        return value * cosine + jnp.where(lane % 64 < 32, pltpu.roll(value, 96, 1), pltpu.roll(value, 32, 1)) * sine

    for pair in range(4):
        lanes = slice(128 * pair, 128 * (pair + 1))
        value_lanes = slice(512 + 128 * pair, 640 + 128 * pair)
        key = turn(mul(normed[...], w_kv[:, lanes], NN)).astype(low)
        value = mul(normed[...], w_kv[:, value_lanes], NN).astype(low)
        for t in range(2):
            here = slice(block * t, block * (t + 1))
            kv[core, t, :, lanes] = key[here]
            kv[core, t, :, value_lanes] = value[here]

    def kv_copy(hop):
        return remote(kv.at[(hop - 1) * 2 + core], kv.at[hop * 2 + core], kv_send.at[hop], kv_recv.at[hop],
                      (row, seq + 2))

    def kv_pass(hop, of_core):
        there = kv.at[hop * 2 + of_core]
        return remote(there, there, kvd_send.at[hop], kvd_recv.at[hop], sibling)

    @pl.when(deep + 1 < n_deep)
    def _():
        kv_copy(1).start()

    for hop in range(1, back + 1):
        @pl.when(deep < hop)
        def _():
            kv[2 * hop] = jnp.zeros(kv.shape[1:], low)
            kv[2 * hop + 1] = jnp.zeros(kv.shape[1:], low)

    kv_pass(0, core).start()
    dense_relay(1)
    g_one()
    dense_finish(1)
    half_lane = lax.broadcasted_iota(jnp.int32, (block, 128), 1) < 64
    for head in range(8):
        both = turn(mul(normed[...], w_qo[:, 128 * head:128 * (head + 1)], NN))
        for t in range(2):
            value = both[block * t:block * (t + 1)]
            other = pltpu.roll(value, 64, 1)
            if head % 2 == 0:
                first, second = jnp.where(half_lane, value, 0.0), jnp.where(half_lane, other, 0.0)
            else:
                first, second = jnp.where(half_lane, 0.0, other), jnp.where(half_lane, 0.0, value)
            queries[t * 8 + head, :block] = first.astype(low)
            queries[t * 8 + head, block:] = second.astype(low)

    for hop in range(1, back + 1):
        @pl.when(deep >= hop)
        def _():
            kv_copy(hop).wait_recv()
            if hop < back:
                @pl.when(deep + 1 < n_deep)
                def _():
                    kv_copy(hop + 1).start()

            kv_pass(hop, core).start()


    kv_pass(0, 1 - core).wait_recv()
    for hop in range(1, back + 1):
        @pl.when(deep >= hop)
        def _():
            kv_pass(hop, 1 - core).wait_recv()

    g_two()
    experts_start(total * 5 // 8, total)
    for t in range(2):
        visible = visibility(deep, seq, slots, block, start_in[block * t:block * (t + 1)])

        def attend(pair, carry):
            lanes = pl.ds(pl.multiple_of(128 * pair, 128), 128)
            value_lanes = pl.ds(pl.multiple_of(512 + 128 * pair, 128), 128)
            values = jnp.concatenate([kv[slot, t, :, value_lanes] for slot in range(slots)], axis=0)
            for half in range(2):
                head = 2 * pair + half
                query = queries[t * 8 + head]
                scores = jnp.concatenate(
                    [mul(query, kv[slot, t, :, lanes], NT) for slot in range(slots)], axis=1
                )
                scores = jnp.where(visible, SCORE_SCALE * scores, NEGATIVE)
                peak = jnp.max(scores, axis=1, keepdims=True)
                raised = jnp.exp(scores - peak)
                denominator = jnp.sum(raised, axis=1, keepdims=True)
                probs = (raised / denominator).astype(low)
                out = mul(probs, values, NN)
                if half == 0:
                    joined = jnp.where(half_lane, out[:block], pltpu.roll(out[block:], 64, 1))
                else:
                    joined = jnp.where(half_lane, pltpu.roll(out[:block], 64, 1), out[block:])
                mixed[block * t:block * (t + 1), pl.ds(pl.multiple_of(128 * head, 128), 128)] = joined.astype(low)
                lse[t] = jnp.where(lane == head, peak + jnp.log(denominator), lse[t])
            return carry

        lax.fori_loop(0, 4, attend, 0)

    g_three()
    for lo in range(0, width, 256):
        branch = mul(mixed[...], w_qo[lo:lo + 256, 1024:], NT)
        hidden[:, lo:lo + 256] = x_in[:, lo:lo + 256].astype(full) + RESIDUAL * branch
    scale_two = norm_scale(hidden[...])
    xtwo_out[...] = (hidden[...] * scale_two * gain_two).astype(low)
    x_one, x_two, x_three, x_last, x_sent = tree_rounds(row, seq, xtwo_out, xs_out, x_send, x_recv)
    x_one()
    logits = mul(xtwo_out[...], w_kv[:, 1024:], NN)
    picked = picks_in[...] > 0
    logits = jnp.where(picked, logits, NEGATIVE)
    raised = jnp.where(picked, jnp.exp(logits - jnp.max(logits, axis=1, keepdims=True)), 0.0)
    gates = raised / jnp.sum(raised, axis=1, keepdims=True)
    gates_out[...] = gates.T[:EXPERTS]

    def gate_copy(step):
        return remote(gates_out, gates_all.at[step], gate_send.at[step], gate_recv.at[step], peer_of(row, seq, step))

    def send_gates(step, carry):
        gate_copy(step).start()
        return carry

    lax.fori_loop(1, 8, send_gates, 0)
    group_own = [
        g_own,
        pltpu.make_async_copy(xtwo_out, xs_out.at[0], group_local.at[1]),
        pltpu.make_async_copy(gates_out, gates_all.at[0], group_local.at[2]),
    ]
    for copy in group_own[1:]:
        copy.start()

    stores = [
        pltpu.make_async_copy(source, target, store.at[i])
        for i, (source, target) in enumerate((
            (w_kv, w_kv_out), (w_qo, w_qo_out), (kv, kv_out), (queries, queries_out), (normed, normed_out),
            (mixed, mixed_out), (hidden, hidden_out), (lse, lse_out),
        ))
    ]
    for copy in stores:
        copy.start()

    x_two()
    x_three()

    def arrived(step, carry):
        other = (me + total - step) % total
        for kind in range(3):
            there = held.at[core, kind, pl.ds(pl.multiple_of(other * rows, rows), rows)]
            remote(there, there, e_send.at[kind, step], e_recv.at[kind, step], sibling).wait_recv()
        return carry

    lax.fori_loop(1, total, arrived, 0)
    for copy in expert_own:
        copy.wait()
    remote(held.at[core], held.at[core], pass_send, pass_recv, sibling).start()

    def settle_experts(step, carry):
        for kind, source in enumerate(sources):
            expert_copy(kind, source, step).wait_send()
        return carry

    lax.fori_loop(1, total, settle_experts, 0)
    g_last()
    g_sent()
    x_last()
    x_sent()
    for copy in group_own:
        copy.wait()

    def settle_gates(step, carry):
        gate_copy(step).wait()
        return carry

    lax.fori_loop(1, 8, settle_gates, 0)
    for kind in range(2):
        def settle_z(step, carry):
            z_copy(kind, step).wait_send()
            return carry

        lax.fori_loop(1, n_deep, settle_z, 0)

        def settle_plane(index, carry):
            hop, step = index // 4, index % 4
            core_copy(kind, step, hop, None).wait_send()

            @pl.when(step > 0)
            def _():
                plane_copy(kind, step, hop, None).wait_send()

            return carry

        lax.fori_loop(0, n_deep * 4, settle_plane, 0)

    kv_pass(0, core).wait_send()
    for hop in range(1, back + 1):
        @pl.when((deep + 1 < n_deep) & (deep >= hop - 1))
        def _():
            kv_copy(hop).wait_send()

        @pl.when(deep >= hop)
        def _():
            kv_pass(hop, core).wait_send()

    for copy in stores:
        copy.wait()
    share = remote(held.at[core], held.at[1 - core], pass_send, pass_recv, sibling)
    share.wait_recv()
    remote(held.at[core], held.at[core], pass_send, pass_recv, sibling).wait_send()


def visibility(deep, seq, slots, block, start):
    key = lax.broadcasted_iota(jnp.int32, (block, block), 1)
    query = lax.broadcasted_iota(jnp.int32, (block, block), 0) + seq * block
    tiles = []
    for slot in range(slots):
        position = key + ((deep - slot // 2) * 2 + slot % 2) * block
        seen = jnp.where((position >= start) & (position <= query), 1.0, 0.0)
        tiles.append(jnp.concatenate([seen, seen], axis=0))
    return jnp.concatenate(tiles, axis=1) > 0.5


def run_forward(n_row, n_seq, length, key, value, query, out, small, turns, segments, ids, x, g, gate, up, down):
    tokens, width = x.shape
    experts, rows, hidden = gate.shape
    total, n_deep = n_row * n_seq, n_seq // 2
    block = tokens // 2
    back = window_of(length, block, n_deep)
    slots = 2 * (back + 1)
    low, full = jnp.bfloat16, jnp.float32
    dma = pltpu.SemaphoreType.DMA
    kv = (slots, 2, block, 1024)
    shape = jax.ShapeDtypeStruct
    return pl.pallas_call(
        functools.partial(forward_kernel, n_row, n_seq, back),
        out_shape=(
            shape((tokens, 128), full),
            shape((tokens, 128), full),
            shape((tokens, 128), jnp.int32),
            shape((tokens, width), low),
            shape((EXPERTS, tokens), full),
            shape((8, 128), full),
            shape((tokens, width), full),
            shape((tokens, 1024), low),
            shape((2, 2 * block, 128), full),
            shape((tokens, width), low),
            shape((16, 2 * block, 128), low),
            shape(kv, low),
            shape((width, 1152), low),
            shape((width, 2048), low),
            shape((8, tokens, width), low),
            shape((8, tokens, width), low),
            shape((8, EXPERTS, tokens), full),
            shape((2, 3, width, hidden), low),
        ),
        in_specs=[VMEM] * 9 + [ANY] * 4,
        out_specs=(VMEM,) * 6 + (ANY,) * 12,
        scratch_shapes=[
            pltpu.VMEM((rows, 1152), low),
            pltpu.VMEM((rows, 2048), low),
            pltpu.VMEM((128, 128), full),
            pltpu.VMEM((tokens, 128), full),
            pltpu.VMEM((width, 1152), low),
            pltpu.VMEM((width, 2048), low),
            pltpu.VMEM(kv, low),
            pltpu.VMEM((16, 2 * block, 128), low),
            pltpu.VMEM((tokens, width), low),
            pltpu.VMEM((tokens, 1024), low),
            pltpu.VMEM((tokens, width), full),
            pltpu.VMEM((2, 2 * block, 128), full),
            dma((2, n_deep)), dma((2, n_deep)),
            dma((2, n_deep, 4)), dma((2, n_deep, 4)),
            dma((2, n_deep, 4)), dma((2, n_deep, 4)),
            dma((back + 1,)), dma((back + 1,)),
            dma((back + 1,)), dma((back + 1,)),
            dma((9,)), dma((9,)), dma((9,)), dma((9,)), dma((8,)), dma((8,)), dma((3,)),
            dma((3, total)), dma((3, total)), dma((3,)),
            dma, dma, dma((2,)), dma((8,)),
        ],
        compiler_params=pltpu.CompilerParams(
            collective_id=1, has_side_effects=True, vmem_limit_bytes=60 << 20
        ),
        name="forward",
    )(key, value, query, out, small, turns, segments, ids, x, g, gate, up, down)


def experts_kernel(
    n_seq, xs_in, gs_in, gates_in, w_in, hidden_in, layer_out, dx_out, dg_out, grad_out,
    xs, gs, gates, w, acc, mids, thirds_got, second_got, last_got, dg_made, dg_got, half_made, half_got,
    t_send, t_recv, s_send, s_recv, l_send, l_recv, dg_send, dg_recv, load, half_send, half_recv, done_sem,
):
    row, seq = lax.axis_index("row"), lax.axis_index("seq")
    core, chip_z = seq % 2, seq // 2 % 2
    tokens, width = hidden_in.shape
    ff = w.shape[1] // 6
    mine = (row * 2 + chip_z) * 2
    low, full = jnp.bfloat16, jnp.float32
    sibling = (row, seq // 2 * 2 + (1 - core))
    thirds = thirds_of(tokens)
    columns = ((0, 0), (0, 1), (1, 0), (1, 1), (0, 2), (1, 2))
    loads = [
        pltpu.make_async_copy(w_in.at[j, kind], w.at[:, pl.ds(col * ff, ff)], load.at[col])
        for col, (j, kind) in enumerate(columns)
    ]
    loads += [
        pltpu.make_async_copy(source, target, load.at[6 + i])
        for i, (source, target) in enumerate(((xs_in, xs), (gs_in, gs), (gates_in, gates)))
    ]
    for copy in loads:
        copy.start()
    barrier = pltpu.get_barrier_semaphore()

    def greet(step, carry):
        pl.semaphore_signal(barrier, inc=1, device_id=peer_of(row, seq, step), device_id_type=MESH)
        return carry

    lax.fori_loop(1, 8, greet, 0)
    pl.semaphore_signal(barrier, inc=1, device_id=sibling, device_id_type=MESH)
    acc[...] = jnp.zeros_like(acc)
    pl.semaphore_wait(barrier, 8)
    for copy in loads:
        copy.wait()

    def dg_copy(step):
        return remote(dg_made.at[step], dg_got.at[step], dg_send.at[step], dg_recv.at[step], peer_of(row, seq, step))

    results = (xs, gs)

    def third_copy(i, which):
        rows = pl.ds(*thirds[i])
        return remote(results[which].at[7, rows], thirds_got.at[which, rows], t_send.at[which, i], t_recv.at[which, i],
                      peer_of(row, seq, (1, 2, 4)[i]))

    def second_copy(i, which):
        return remote(results[which].at[(6, 5, 3)[i]], second_got.at[which, i], s_send.at[which, i], s_recv.at[which, i],
                      peer_of(row, seq, (2, 4, 1)[i]))

    def last_copy(i, which):
        slot = (4, 1, 2)[i]
        return remote(results[which].at[slot], last_got.at[which, i], l_send.at[which, i], l_recv.at[which, i],
                      peer_of(row, seq, slot))

    def relay_third(i):
        for which in range(2):
            rows, slot = pl.ds(*thirds[i]), (6, 5, 3)[i]
            third_copy(i, which).wait_recv()
            results[which][slot, rows] = (
                results[which][slot, rows].astype(full) + thirds_got[which, rows].astype(full)
            ).astype(low)
            second_copy(i, which).start()

    def relay_second(i):
        for which in range(2):
            slot = (4, 1, 2)[i]
            second_copy(i, which).wait_recv()
            results[which][slot] = (
                results[which][slot].astype(full) + second_got[which, i].astype(full)
            ).astype(low)
            last_copy(i, which).start()

    def block(index, carry):
        step = 7 - index + jnp.where(index == 3, -1, 0) + jnp.where(index == 4, 1, 0)
        step = jnp.where(index == 5, 1, jnp.where(index == 6, 2, step))
        x, g = xs[step], gs[step]
        for j in range(2):
            gate = column(gates[step, pl.ds(mine + j, 1)])[:, :1]
            a = mul(x, w[:, 2 * j * ff:(2 * j + 1) * ff], NN)
            b = mul(x, w[:, (2 * j + 1) * ff:(2 * j + 2) * ff], NN)
            back = RESIDUAL * mul(g, w[:, (4 + j) * ff:(5 + j) * ff], NN)
            sigma = jax.nn.sigmoid(a)
            smooth = a * sigma
            inner = smooth * b
            dgate = jnp.sum(inner * back, axis=1, keepdims=True)
            back = gate * back
            mids[:, (4 + j) * ff:(5 + j) * ff] = (gate * inner).astype(low)
            mids[:, 2 * j * ff:(2 * j + 1) * ff] = (back * b * (sigma + smooth * (1.0 - sigma))).astype(low)
            mids[:, (2 * j + 1) * ff:(2 * j + 2) * ff] = (back * smooth).astype(low)
            dg_made[step, j] = jnp.broadcast_to(dgate, (tokens, 128)).T[:8]
        for lo in range(0, width, 256):
            part = slice(lo, lo + 256)
            acc[part, :4 * ff] += mul(xs[step, :, part], mids[:, :4 * ff], TN)
            acc[part, 4 * ff:] += mul(gs[step, :, part], mids[:, 4 * ff:], TN)
        for lo in range(0, width, 256):
            part = slice(lo, lo + 256)
            xs[step, :, part] = mul(mids[:, 4 * ff:], w[part, 4 * ff:], NT).astype(low)
            gs[step, :, part] = mul(mids[:, :4 * ff], w[part, :4 * ff], NT).astype(low)

        @pl.when(index < 7)
        def _():
            dg_copy(step).start()

        @pl.when(index == 0)
        def _():
            for i in range(3):
                for which in range(2):
                    third_copy(i, which).start()

        for i in range(3):
            @pl.when(index == 1 + i)
            def _():
                relay_third(i)

            @pl.when(index == 5 + i)
            def _():
                relay_second(i)

        return carry

    lax.fori_loop(0, 8, block, 0)

    def share_of(j):
        wide = acc[:, pl.ds(pl.multiple_of(j * 2 * ff, 128), 2 * ff)]
        thin = RESIDUAL * acc[:, pl.ds(pl.multiple_of((4 + j) * ff, 128), ff)]
        return wide, thin

    wide, thin = share_of(1 - core)
    half_made[:, :2 * ff] = wide.astype(low)
    half_made[:, 2 * ff:] = thin.astype(low)
    half = remote(half_made, half_got, half_send, half_recv, sibling)
    half.start()
    dg_got[0] = dg_made[0]
    half.wait_recv()
    wide, thin = share_of(core)
    half_got[:, :2 * ff] = (wide + half_got[:, :2 * ff].astype(full)).astype(low)
    half_got[:, 2 * ff:] = (thin + half_got[:, 2 * ff:].astype(full)).astype(low)
    store = pltpu.make_async_copy(half_got, grad_out, done_sem)
    store.start()

    def settle(step, carry):
        dg_copy(step).wait()
        return carry

    lax.fori_loop(1, 8, settle, 0)

    def place(step, carry):
        other_row, other_seq = peer_of(row, seq, step)
        chip = other_row * 2 + other_seq // 2 % 2
        for j in range(2):
            dg_out[pl.ds(chip * 2 + j, 1)] = dg_got[step, j, :1]
        return carry

    lax.fori_loop(0, 8, place, 0)
    for i in range(3):
        for which in range(2):
            last_copy(i, which).wait_recv()
    dx_out[...] = gs[0].astype(full) + sum(last_got[1, i].astype(full) for i in range(3))
    mixture = xs[0].astype(full) + sum(last_got[0, i].astype(full) for i in range(3))
    layer_out[...] = (hidden_in[...] + RESIDUAL * mixture).astype(low)
    for i in range(3):
        for which in range(2):
            third_copy(i, which).wait_send()
            second_copy(i, which).wait_send()
            last_copy(i, which).wait_send()
    half.wait_send()
    store.wait()


def run_experts(n_row, n_seq, xs, gs, gates, w, hidden):
    _, tokens, width = xs.shape
    ff = w.shape[3]
    low, full = jnp.bfloat16, jnp.float32
    dma, shape = pltpu.SemaphoreType.DMA, jax.ShapeDtypeStruct
    return pl.pallas_call(
        functools.partial(experts_kernel, n_seq),
        out_shape=(
            shape((tokens, width), low),
            shape((tokens, width), full),
            shape((EXPERTS, tokens), full),
            shape((width, 3 * ff), low),
        ),
        in_specs=[ANY, ANY, ANY, ANY, VMEM],
        out_specs=(VMEM, VMEM, VMEM, ANY),
        scratch_shapes=[
            pltpu.VMEM((8, tokens, width), low),
            pltpu.VMEM((8, tokens, width), low),
            pltpu.VMEM((8, EXPERTS, tokens), full),
            pltpu.VMEM((width, 6 * ff), low),
            pltpu.VMEM((width, 6 * ff), full),
            pltpu.VMEM((tokens, 6 * ff), low),
            pltpu.VMEM((2, tokens, width), low),
            pltpu.VMEM((2, 3, tokens, width), low),
            pltpu.VMEM((2, 3, tokens, width), low),
            pltpu.VMEM((8, 2, 8, tokens), full),
            pltpu.VMEM((8, 2, 8, tokens), full),
            pltpu.VMEM((width, 3 * ff), low),
            pltpu.VMEM((width, 3 * ff), low),
            dma((2, 3)), dma((2, 3)), dma((2, 3)), dma((2, 3)), dma((2, 3)), dma((2, 3)),
            dma((8,)), dma((8,)), dma((9,)),
            dma, dma, dma,
        ],
        compiler_params=pltpu.CompilerParams(
            collective_id=3, has_side_effects=True, vmem_limit_bytes=60 << 20
        ),
        name="experts",
    )(xs, gs, gates, w, hidden)


def backward_kernel(
    n_row, n_seq, back,
    w_kv_in, w_qo_in, kv_in, queries_in, normed_in, mixed_in, x_in, g_in, cos_in, sin_in, start_in,
    hidden_in, xtwo_in, gates_in, dgates_in, dx_in, lse_in, expert_grads,
    input_out, q_out, k_out, v_out, o_out, small_out, held,
    w_kv, w_qo, kv, queries, outs, dq, dqkv, dkv_own, dkv_core, dkv_deep,
    grads_o, grads_q, grads_k, core_o, core_q, core_k, plane_o, plane_q, plane_k, deep_o, deep_q, deep_k,
    spread_out, load, k_send, k_recv, kd_send, kd_recv, e_send, e_recv, e_local,
    d_send, d_recv, p_send, p_recv, z_send, z_recv,
):
    row, seq = lax.axis_index("row"), lax.axis_index("seq")
    core, deep, n_deep = seq % 2, seq // 2, n_seq // 2
    me, total = row * n_seq + seq, n_row * n_seq
    sibling = (row, deep * 2 + (1 - core))
    rows = q_out.shape[0]
    tokens, width = x_in.shape
    block = tokens // 2
    low, full = jnp.bfloat16, jnp.float32
    slots = kv.shape[0]
    loads = [
        pltpu.make_async_copy(source, target, load.at[i])
        for i, (source, target) in enumerate(((w_kv_in, w_kv), (w_qo_in, w_qo), (kv_in, kv), (queries_in, queries)))
    ]
    for copy in loads:
        copy.start()
    greet_all(n_row, n_seq)

    def expert_copy(step):
        other = (me + step) % total
        return remote(
            expert_grads.at[pl.ds(pl.multiple_of(other * rows, rows), rows)],
            held.at[seq // 4, row * 4 + seq % 4],
            e_send.at[step], e_recv.at[step], (other // n_seq, other % n_seq),
        )

    expert_own = pltpu.make_async_copy(
        expert_grads.at[pl.ds(pl.multiple_of(me * rows, rows), rows)],
        held.at[seq // 4, row * 4 + seq % 4], e_local,
    )
    expert_own.start()

    def experts_start(lo, hi):
        def start_experts(index, carry):
            expert_copy(index * STRIDE % total).start()
            return carry

        lax.fori_loop(lo, hi, start_experts, 0)

    experts_start(1, total * 5 // 8)
    for copy in loads:
        copy.wait()

    made, from_core = (grads_o, grads_q, grads_k), (core_o, core_q, core_k)
    from_plane, from_deep = (plane_o, plane_q, plane_k), (deep_o, deep_q, deep_k)

    def part(of_row, of_deep, of_core):
        return pl.ds(pl.multiple_of((of_row * n_seq + of_deep * 2 + of_core) * rows, rows), rows)

    def d_copy(kind, step, hop):
        there = part(row_of(row, step), (deep + hop) % n_deep, 1 - core)
        return remote(made[kind].at[there], from_core[kind].at[hop, step], d_send.at[kind, hop, step],
                      d_recv.at[kind, hop, step], sibling)

    def p_copy(kind, step, hop):
        there = part(row_of(row, step), (deep + hop) % n_deep, core)
        return remote(made[kind].at[there], from_plane[kind].at[hop, step - 1], p_send.at[kind, hop, step],
                      p_recv.at[kind, hop, step], (row_of(row, step), seq))

    def z_copy(kind, hop):
        there = part(row, (deep + hop) % n_deep, core)
        return remote(made[kind].at[there], from_deep[kind].at[hop], z_send.at[kind, hop], z_recv.at[kind, hop],
                      (row, (deep + hop) % n_deep * 2 + core))

    def dense_start(kind):
        def start_d(index, carry):
            d_copy(kind, 3 - index % 4, n_deep - 1 - index // 4).start()
            return carry

        lax.fori_loop(0, 4 * n_deep, start_d, 0)

    def dense_cores(kind):
        def sum_cores(index, carry):
            step, hop = 3 - index % 4, n_deep - 1 - index // 4
            d_copy(kind, step, hop).wait_recv()
            there = part(row_of(row, step), (deep + hop) % n_deep, core)
            made[kind][there] = (made[kind][there].astype(full) + from_core[kind][hop, step].astype(full)).astype(low)

            @pl.when(step > 0)
            def _():
                p_copy(kind, step, hop).start()

            return carry

        lax.fori_loop(0, 4 * n_deep, sum_cores, 0)

    def dense_plane(kind):
        def sum_plane(index, carry):
            hop = n_deep - 1 - index
            there = part(row, (deep + hop) % n_deep, core)
            for step in range(1, 4):
                p_copy(kind, step, hop).wait_recv()
            value = made[kind][there].astype(full)
            for step in range(1, 4):
                value += from_plane[kind][hop, step - 1].astype(full)
            made[kind][there] = value.astype(low)

            @pl.when(hop > 0)
            def _():
                z_copy(kind, hop).start()

            return carry

        lax.fori_loop(0, n_deep, sum_plane, 0)

    def dense_end(kind):
        value = made[kind][part(row, deep, core)].astype(full)
        for hop in range(1, n_deep):
            z_copy(kind, hop).wait_recv()
            value += from_deep[kind][hop].astype(full)
        return value


    def upright(value):
        return jnp.concatenate([value, jnp.zeros((128 - value.shape[0], tokens), full)], axis=0).T

    small = w_kv[:, 1024:].astype(full).T
    gain_one, gain_two = small[16:17], small[17:18]
    gates, dgates = upright(gates_in[...]), upright(dgates_in[...])
    dlogits = (gates * (dgates - jnp.sum(gates * dgates, axis=1, keepdims=True))).astype(low)
    dxtwo = dx_in[...] + mul(dlogits, w_kv[:, 1024:], NT)
    h = hidden_in[...]
    scale_two = norm_scale(h)
    weighted = gain_two * dxtwo
    dgain_two = jnp.sum(dxtwo * h * scale_two, axis=0, keepdims=True)
    input_out[...] = (
        g_in[...].astype(full)
        + scale_two * weighted
        - h * (scale_two * scale_two * scale_two) * jnp.mean(weighted * h, axis=1, keepdims=True)
    )
    dbranch = (RESIDUAL * input_out[...]).astype(low)
    drouter = mul(xtwo_in[...], dlogits, TN)
    for lo in range(0, width, 256):
        grads_o[lo:lo + 256] = mul(dbranch[:, lo:lo + 256], mixed_in[...], TN).astype(low)
    dense_start(0)

    half_lane = lax.broadcasted_iota(jnp.int32, (block, 128), 1) < 64
    for head in range(8):
        both = mul(dbranch, w_qo[:, 1024 + 128 * head:1152 + 128 * head], NN)
        for t in range(2):
            value = both[block * t:block * (t + 1)]
            other = pltpu.roll(value, 64, 1)
            if head % 2 == 0:
                first, second = jnp.where(half_lane, value, 0.0), jnp.where(half_lane, other, 0.0)
            else:
                first, second = jnp.where(half_lane, 0.0, other), jnp.where(half_lane, 0.0, value)
            outs[t * 8 + head, :block] = first.astype(low)
            outs[t * 8 + head, block:] = second.astype(low)

    dense_cores(0)

    lane = lax.broadcasted_iota(jnp.int32, (tokens, 128), 1)
    for t in range(2):
        visible = visibility(deep, seq, slots, block, start_in[block * t:block * (t + 1)])

        def attend(pair, carry):
            lanes = pl.ds(pl.multiple_of(128 * pair, 128), 128)
            value_lanes = pl.ds(pl.multiple_of(512 + 128 * pair, 128), 128)
            keys = jnp.concatenate([kv[slot, t, :, lanes] for slot in range(slots)], axis=0)
            values = jnp.concatenate([kv[slot, t, :, value_lanes] for slot in range(slots)], axis=0)
            dk, dv = 0.0, 0.0
            for half in range(2):
                head = 2 * pair + half
                query, dout = queries[t * 8 + head], outs[t * 8 + head]
                scores = jnp.where(visible, SCORE_SCALE * mul(query, keys, NT), NEGATIVE)
                total_log = jnp.sum(jnp.where(lane == head, lse_in[t], 0.0), axis=1, keepdims=True)
                probs = jnp.exp(scores - total_log)
                dprobs = mul(dout, values, NT)
                inner = jnp.sum(probs * dprobs, axis=1, keepdims=True)
                dscores = (probs * (dprobs - inner)).astype(low)
                dquery = SCORE_SCALE * mul(dscores, keys, NN)
                if half == 0:
                    joined = jnp.where(half_lane, dquery[:block], pltpu.roll(dquery[block:], 64, 1))
                else:
                    joined = jnp.where(half_lane, pltpu.roll(dquery[:block], 64, 1), dquery[block:])
                dq[block * t:block * (t + 1), pl.ds(pl.multiple_of(128 * head, 128), 128)] = joined
                dk += SCORE_SCALE * mul(dscores, query, TN)
                dv += mul(probs.astype(low), dout, TN)
            for slot in range(slots):
                kv[slot, t, :, lanes] = dk[block * slot:block * (slot + 1)].astype(low)
                kv[slot, t, :, value_lanes] = dv[block * slot:block * (slot + 1)].astype(low)

            @pl.when(core == 0)
            def _():
                dkv_own[t, :, lanes] = dk[:block]
                dkv_own[t, :, value_lanes] = dv[:block]

            @pl.when(core == 1)
            def _():
                dkv_own[t, :, lanes] = dk[block:2 * block]
                dkv_own[t, :, value_lanes] = dv[block:2 * block]

            return carry

        lax.fori_loop(0, 4, attend, 0)
        if t == 0:
            dense_plane(0)

    def kd_copy(hop):
        return remote(kv.at[hop * 2 + (1 - core)], dkv_core.at[hop], kd_send.at[hop], kd_recv.at[hop], sibling)

    def k_copy(hop):
        return remote(kv.at[hop * 2 + core], dkv_deep.at[hop - 1], k_send.at[hop], k_recv.at[hop], (row, seq - 2))

    def k_sum(hop):
        kd_copy(hop).wait_recv()
        kv[hop * 2 + core] = (kv[hop * 2 + core].astype(full) + dkv_core[hop].astype(full)).astype(low)
        if hop < back:
            @pl.when(deep + 1 < n_deep)
            def _():
                k_copy(hop + 1).wait_recv()
                kv[hop * 2 + core] = (kv[hop * 2 + core].astype(full) + dkv_deep[hop].astype(full)).astype(low)

        k_copy(hop).start()

    for hop in range(back, -1, -1):
        @pl.when(deep >= hop)
        def _():
            kd_copy(hop).start()

    @pl.when(deep >= back)
    def _():
        k_sum(back)

    cosine, sine = cos_in[...], sin_in[...]

    def turn_back(value):
        return value * cosine - jnp.where(lane % 64 < 32, pltpu.roll(value, 96, 1), pltpu.roll(value, 32, 1)) * sine

    for head in range(8):
        lanes = slice(128 * head, 128 * (head + 1))
        dqkv[:, lanes] = turn_back(dq[:, lanes]).astype(low)
    for lo in range(0, width, 256):
        grads_q[lo:lo + 256] = mul(normed_in[:, lo:lo + 256], dqkv[:, :1024], TN).astype(low)
    dense_start(1)
    for hop in range(back - 1, 0, -1):
        @pl.when(deep >= hop)
        def _():
            k_sum(hop)

    for lo in range(0, width, 256):
        part_q = slice(lo, lo + 256)
        dq[:, part_q] = mul(dqkv[:, :1024], w_qo[part_q, :1024], NT)
    dense_cores(1)
    experts_start(total * 5 // 8, total)
    kd_copy(0).wait_recv()
    dkv_own[...] += dkv_core[0].astype(full)

    @pl.when(deep + 1 < n_deep)
    def _():
        k_copy(1).wait_recv()
        dkv_own[...] += dkv_deep[0].astype(full)

    for pair in range(4):
        lanes = slice(128 * pair, 128 * (pair + 1))
        value_lanes = slice(512 + 128 * pair, 640 + 128 * pair)
        dkey = jnp.concatenate([dkv_own[0, :, lanes], dkv_own[1, :, lanes]], axis=0)
        dqkv[:, 1024 + 128 * pair:1152 + 128 * pair] = turn_back(dkey).astype(low)
        dvalue = jnp.concatenate([dkv_own[0, :, value_lanes], dkv_own[1, :, value_lanes]], axis=0)
        dqkv[:, 1536 + 128 * pair:1664 + 128 * pair] = dvalue.astype(low)
    for lo in range(0, width, 256):
        grads_k[lo:lo + 256, :1024] = mul(normed_in[:, lo:lo + 256], dqkv[:, 1024:], TN).astype(low)
    x = x_in[...].astype(full)
    scale_one = norm_scale(x)
    for lo in range(0, width, 256):
        part_k = slice(lo, lo + 256)
        dq[:, part_k] += mul(dqkv[:, 1024:], w_kv[part_k, :1024], NT)
    dxone = dq[...]
    weighted = gain_one * dxone
    dgain_one = jnp.sum(dxone * x * scale_one, axis=0, keepdims=True)
    wide = lax.broadcasted_iota(jnp.int32, (width, 128), 1)
    grads_k[:, 1024:] = jnp.where(
        wide == 16, column(dgain_one), jnp.where(wide == 17, column(dgain_two), drouter)
    ).astype(low)
    dense_start(2)
    dense_plane(1)
    input_out[...] = (
        input_out[...]
        + scale_one * weighted
        - x * (scale_one * scale_one * scale_one) * jnp.mean(weighted * x, axis=1, keepdims=True)
    )
    dense_cores(2)
    dense_plane(2)
    o_out[...] = dense_end(0)
    q_out[...] = dense_end(1)
    last = dense_end(2)
    k_out[...] = last[:, :512]
    v_out[...] = last[:, 512:1024]
    spread_out[:rows] = last[:, 1024:]
    small_out[...] = spread_out[...].T
    for kind in range(3):
        def settle_d(index, carry):
            hop, step = index // 4, index % 4
            d_copy(kind, step, hop).wait_send()

            @pl.when(step > 0)
            def _():
                p_copy(kind, step, hop).wait_send()

            return carry

        lax.fori_loop(0, 4 * n_deep, settle_d, 0)

        def settle_z(hop, carry):
            z_copy(kind, hop).wait_send()
            return carry

        lax.fori_loop(1, n_deep, settle_z, 0)

    for hop in range(back + 1):
        @pl.when(deep >= hop)
        def _():
            kd_copy(hop).wait_send()
            if hop > 0:
                k_copy(hop).wait_send()

    expert_own.wait()

    def settle_experts(step, carry):
        other = (me + total - step) % total
        expert_copy(step).wait_send()
        there = held.at[other % n_seq // 4, other // n_seq * 4 + other % 4]
        remote(there, there, e_send.at[step], e_recv.at[step], sibling).wait_recv()
        return carry

    lax.fori_loop(1, total, settle_experts, 0)


def window_of(length, block, n_deep):
    return min((length // 2 + 2 * block - 1) // (2 * block), n_deep - 1)


def run_backward(n_row, n_seq, length, w_kv, w_qo, kv, queries, normed, mixed, x, g, cosine, sine, start,
                 hidden, xtwo, gates, dgates, dx, lse, expert_grads):
    tokens, width = x.shape
    total, n_deep = n_row * n_seq, n_seq // 2
    rows, block = width // total, tokens // 2
    back = window_of(length, block, n_deep)
    columns = (1024, 1024, w_kv.shape[1])
    low, full = jnp.bfloat16, jnp.float32
    dma, shape = pltpu.SemaphoreType.DMA, jax.ShapeDtypeStruct
    return pl.pallas_call(
        functools.partial(backward_kernel, n_row, n_seq, back),
        out_shape=(
            shape((tokens, width), full),
            shape((rows, 1024), full),
            shape((rows, 512), full),
            shape((rows, 512), full),
            shape((rows, 1024), full),
            shape((128, 128), full),
            shape((n_seq // 4, n_row * 4, rows, expert_grads.shape[1]), low),
        ),
        in_specs=[ANY] * 4 + [VMEM] * 13 + [ANY],
        out_specs=(VMEM,) * 6 + (ANY,),
        scratch_shapes=[
            pltpu.VMEM(w_kv.shape, low),
            pltpu.VMEM(w_qo.shape, low),
            pltpu.VMEM(kv.shape, low),
            pltpu.VMEM((16, tokens, 128), low),
            pltpu.VMEM((16, tokens, 128), low),
            pltpu.VMEM((tokens, 1024), full),
            pltpu.VMEM((tokens, 2048), low),
            pltpu.VMEM(kv.shape[1:], full),
            pltpu.VMEM((back + 1,) + kv.shape[1:], low),
            pltpu.VMEM((back,) + kv.shape[1:], low),
        ]
        + [pltpu.VMEM((width, c), low) for c in columns]
        + [pltpu.VMEM((n_deep, 4, rows, c), low) for c in columns]
        + [pltpu.VMEM((n_deep, 3, rows, c), low) for c in columns]
        + [pltpu.VMEM((n_deep, rows, c), low) for c in columns]
        + [
            pltpu.VMEM((128, 128), full),
            dma((4,)),
            dma((back + 1,)), dma((back + 1,)), dma((back + 1,)), dma((back + 1,)),
            dma((total,)), dma((total,)), dma,
            dma((3, n_deep, 4)), dma((3, n_deep, 4)), dma((3, n_deep, 4)), dma((3, n_deep, 4)),
            dma((3, n_deep)), dma((3, n_deep)),
        ],
        compiler_params=pltpu.CompilerParams(
            collective_id=2, has_side_effects=True, vmem_limit_bytes=62 << 20
        ),
        name="backward",
    )(w_kv, w_qo, kv, queries, normed, mixed, x, g, cosine, sine, start, hidden, xtwo, gates, dgates, dx, lse,
      expert_grads)


def results_kernel(
    held, counts, small, *refs
):
    passed, copied = refs[:6], refs[6:12]
    gate_out, up_out, down_out, router_out, one_out, two_out, counts_out = refs[12:]
    ff = gate_out.shape[2]
    rows = router_out.shape[1]
    for source, target in zip(passed[:2], copied[:2]):
        target[...] = source[...]

    @pl.when(pl.program_id(0) == 0)
    def _():
        for source, target in zip(passed[2:], copied[2:]):
            target[...] = source[...]
        router_out[...] = small[:EXPERTS, :rows]
        one_out[...] = small[EXPERTS:EXPERTS + 1, :rows]
        two_out[...] = small[EXPERTS + 1:EXPERTS + 2, :rows]
        counts_out[...] = pltpu.roll(counts[...], 96, 1)[:1].astype(jnp.int32)

    for out, lo in ((gate_out, 0), (up_out, ff), (down_out, 2 * ff)):
        value = held[0, :, :, lo:lo + ff].astype(jnp.float32)
        for group in range(1, held.shape[0]):
            value += held[group, :, :, lo:lo + ff].astype(jnp.float32)
        out[...] = value


def run_results(held, counts, small, *passed):
    groups, experts, rows, wide = held.shape
    ff, full = wide // 3, jnp.float32
    some = experts // 4
    shape = jax.ShapeDtypeStruct
    whole = lambda i: (0, 0)
    moved = [pl.BlockSpec((a.shape[0] // 4, a.shape[1]), lambda i: (i, 0)) for a in passed[:2]]
    moved += [pl.BlockSpec(a.shape, whole) for a in passed[2:]]
    return pl.pallas_call(
        results_kernel,
        grid=(4,),
        out_shape=tuple(shape(a.shape, a.dtype) for a in passed) + (
            shape((experts, rows, ff), full),
            shape((experts, rows, ff), full),
            shape((experts, rows, ff), full),
            shape((EXPERTS, rows), full),
            shape((1, rows), full),
            shape((1, rows), full),
            shape((1, 128), jnp.int32),
        ),
        in_specs=[
            pl.BlockSpec((groups, some, rows, wide), lambda i: (0, i, 0, 0)),
            pl.BlockSpec((8, 128), whole),
            pl.BlockSpec((128, 128), whole),
        ] + moved,
        out_specs=tuple(moved) + (pl.BlockSpec((some, rows, ff), lambda i: (i, 0, 0)),) * 3 + (
            pl.BlockSpec((EXPERTS, rows), whole),
            pl.BlockSpec((1, rows), whole),
            pl.BlockSpec((1, rows), whole),
            pl.BlockSpec((1, 128), whole),
        ),
        name="results",
    )(held, counts, small, *passed)


def body(
    n_row,
    n_seq,
    tokens,
    segment_ids,
    expert_ids,
    norm1_gain,
    w_query,
    w_key,
    w_value,
    w_out,
    norm2_gain,
    w_router,
    w_gate,
    w_up,
    w_down,
    out_grad,
):
    row_count, block_len, width = tokens.shape
    token_count = row_count * block_len
    length = segment_ids.shape[1]
    rows = w_query.shape[0]
    full = jnp.float32
    small = jnp.concatenate([w_router.T, norm1_gain[None], norm2_gain[None], jnp.zeros((14, rows), norm1_gain.dtype)])
    lanes = np.arange(128) % HEAD
    half = HEAD // 2
    frequency = (THETA ** (-2.0 * (lanes % half) / HEAD)).astype(np.float32)
    turns = np.zeros((8, 128), np.float32)
    turns[0], turns[1] = frequency, np.where(lanes < half, -1.0, 1.0)
    x = tokens.reshape(token_count, width)
    g = out_grad.reshape(token_count, width)
    (cosine, sine, start, xtwo, gates, counts, hidden, mixed, lse, normed, queries, kv, w_kv, w_qo,
     group_g, group_x, group_gates, expert_weights) = run_forward(
        n_row, n_seq, length, w_key, w_value, w_query, w_out.T, small.astype(full), jnp.asarray(turns), segment_ids,
        jnp.swapaxes(expert_ids[0], 1, 2), x, g, w_gate, w_up, jnp.swapaxes(w_down, 1, 2)
    )
    layer_out, dx, dgates, expert_grads = run_experts(
        n_row, n_seq, group_x, group_g, group_gates, expert_weights, hidden
    )
    input_grad, dq, dk, dv, do, small, held = run_backward(
        n_row, n_seq, length, w_kv, w_qo, kv, queries, normed, mixed, x, g, cosine, sine, start,
        hidden, xtwo, gates, dgates, dx, lse, expert_grads,
    )
    layer_out, input_grad, dq, dk, dv, do, d_gate, d_up, d_down, router, one, two, counts = run_results(
        held, counts, small, layer_out, input_grad, dq, dk, dv, do
    )
    return (
        layer_out.reshape(row_count, block_len, width),
        input_grad.reshape(row_count, block_len, width),
        one[0],
        dq,
        dk,
        dv,
        do.T,
        two[0],
        router.T,
        d_gate,
        d_up,
        jnp.swapaxes(d_down, 1, 2),
        counts[0, :EXPERTS],
    )


def solution(mesh):
    in_specs = (
        P("row", "seq", None),
        P("row", None),
        P("seq", "row", None, None),
        P(("row", "seq")),
        P(("row", "seq"), None),
        P(("row", "seq"), None),
        P(("row", "seq"), None),
        P(None, ("row", "seq")),
        P(("row", "seq")),
        P(("row", "seq"), None),
        P(None, ("row", "seq"), None),
        P(None, ("row", "seq"), None),
        P(None, None, ("row", "seq")),
        P("row", "seq", None),
    )
    out_specs = (
        P("row", "seq", None),
        P("row", "seq", None),
        P(("row", "seq")),
        P(("row", "seq"), None),
        P(("row", "seq"), None),
        P(("row", "seq"), None),
        P(None, ("row", "seq")),
        P(("row", "seq")),
        P(("row", "seq"), None),
        P(None, ("row", "seq"), None),
        P(None, ("row", "seq"), None),
        P(None, None, ("row", "seq")),
        P(),
    )
    return jax.shard_map(
        functools.partial(body, mesh.shape["row"], mesh.shape["seq"]),
        mesh=mesh,
        in_specs=in_specs,
        out_specs=out_specs,
        check_vma=False,
    )
```

```python
import functools

import jax
import jax.numpy as jnp
import numpy as np
from jax import lax
from jax.experimental import pallas as pl
from jax.experimental.pallas import tpu as pltpu
from jax.sharding import PartitionSpec as P

HEAD = 64
EXPERTS = 16
TOPK = 8

EPSILON = 1e-06
SCORE_SCALE = 0.015625
RESIDUAL = 0.22
THETA = 10000.0
NEGATIVE = -1e30

MESH = pl.DeviceIdType.MESH
STRIDE = 11
ANY = pl.BlockSpec(memory_space=pl.ANY)
VMEM = pl.BlockSpec(memory_space=pltpu.VMEM)


def norm_scale(value):
    return lax.rsqrt(jnp.mean(value * value, axis=-1, keepdims=True) + EPSILON)


def greet_all(n_row, n_seq, wait=True):
    row, seq = lax.axis_index("row"), lax.axis_index("seq")
    me, total = row * n_seq + seq, n_row * n_seq
    barrier = pltpu.get_barrier_semaphore()

    def greet(step, carry):
        other = (me + step) % total
        pl.semaphore_signal(
            barrier, inc=1, device_id=(other // n_seq, other % n_seq), device_id_type=MESH
        )
        return carry

    lax.fori_loop(1, total, greet, 0)
    if wait:
        pl.semaphore_wait(barrier, total - 1)


NN = (((1,), (0,)), ((), ()))
NT = (((1,), (1,)), ((), ()))
TN = (((0,), (0,)), ((), ()))


def mul(a, b, dims):
    return lax.dot_general(a, b, dims, preferred_element_type=jnp.float32)


def column(row_values):
    return jnp.broadcast_to(row_values, (128, row_values.shape[1])).T


def peer_of(row, seq, step):
    other_row = (row // 2 + step // 4) % 2 * 2 + (row % 2 + step // 2 % 2) % 2
    other_seq = seq // 4 * 4 + (seq // 2 % 2 + step % 2) % 2 * 2 + seq % 2
    return (other_row, other_seq)


def row_of(row, step):
    return (row // 2 + step // 2) % 2 * 2 + (row % 2 + step % 2) % 2


def remote(source, target, send, recv, device):
    return pltpu.make_async_remote_copy(
        src_ref=source, dst_ref=target, send_sem=send, recv_sem=recv, device_id=device,
        device_id_type=MESH,
    )


def thirds_of(rows):
    cut = rows * 3 // 8
    rest = (rows - cut) // 2
    return ((0, cut), (cut, rest), (cut + rest, rest))


def tree_rounds(row, seq, own, slots, send, recv):
    thirds = thirds_of(own.shape[0])

    def hop(source, slot, toward, index):
        return remote(source, slot, send.at[index], recv.at[index], peer_of(row, seq, toward))

    def piece(slot, third):
        return slots.at[slot, pl.ds(*thirds[third])]

    first = lambda i: hop(own, slots.at[(1, 2, 4)[i]], (1, 2, 4)[i], i)
    second = lambda i: hop(slots.at[(2, 4, 1)[i]], slots.at[(3, 6, 5)[i]], (1, 2, 4)[i], 3 + i)
    third = lambda i: hop(piece((6, 5, 3)[i], i), piece(7, i), (1, 2, 4)[i], 6 + i)

    def start(make):
        for i in range(3):
            make(i).start()

    def landed(make):
        for i in range(3):
            make(i).wait_recv()

    def round_one():
        start(first)

    def round_two():
        landed(first)
        start(second)

    def round_three():
        landed(second)
        start(third)

    def last():
        landed(third)

    def sent():
        for make in (first, second, third):
            for i in range(3):
                make(i).wait_send()

    return round_one, round_two, round_three, last, sent


def forward_kernel(
    n_row, n_seq, back,
    key_in, value_in, query_in, out_in, small_in, turns_in, segments_in, ids_in, x_in, g_in, gate, up, down,
    cos_in, sin_in, start_in, xtwo_out, gates_out, counts_out, hidden_out, mixed_out, lse_out, normed_out, queries_out, kv_out,
    w_kv_out, w_qo_out, g_out, xs_out, gates_all, held,
    pack_kv, pack_qo, upright, picks_in, w_kv, w_qo, kv, queries, normed, mixed, hidden, lse,
    z_send, z_recv, p_send, p_recv, d_send, d_recv, kv_send, kv_recv, kvd_send, kvd_recv,
    g_send, g_recv, x_send, x_recv, gate_send, gate_recv, group_local, e_send, e_recv, e_local, pass_send, pass_recv, local, store,
):
    row, seq = lax.axis_index("row"), lax.axis_index("seq")
    core, deep, n_deep = seq % 2, seq // 2, n_seq // 2
    me, total = row * n_seq + seq, n_row * n_seq
    sibling = (row, deep * 2 + (1 - core))
    rows = key_in.shape[0]
    tokens, width = x_in.shape
    block = tokens // 2
    low, full = jnp.bfloat16, jnp.float32
    slots = kv.shape[0]
    packs, walls = (pack_kv, pack_qo), (w_kv, w_qo)
    greet_all(n_row, n_seq, False)

    sublane = lax.broadcasted_iota(jnp.int32, (128, 128), 0)
    for t in range(2):
        chosen = jnp.zeros((128, block), full)
        for choice in range(TOPK):
            chosen += jnp.where(ids_in[t, choice:choice + 1] == sublane, 1.0, 0.0)
        picks_in[block * t:block * (t + 1)] = chosen.T
    count = jnp.broadcast_to(jnp.sum(picks_in[...], axis=0, keepdims=True), (8, 128))
    upright[...] = jnp.zeros_like(upright)
    upright[:small_in.shape[0], :rows] = small_in[...]
    small = upright[...].T[:rows]
    counts = jnp.where(sublane[:rows] == 0, pltpu.roll(count, 32, 1)[:1], 0.0)
    pack_kv[:, :512] = key_in[...]
    pack_kv[:, 512:1024] = value_in[...]
    pack_kv[:, 1024:] = (small + counts).astype(low)
    pack_qo[:, :1024] = query_in[...]
    pack_qo[:, 1024:] = out_in[...]
    pl.semaphore_wait(pltpu.get_barrier_semaphore(), total - 1)

    def part(kind, of_row, of_deep, of_core):
        start = (of_row * n_seq + of_deep * 2 + of_core) * rows
        return walls[kind].at[pl.ds(pl.multiple_of(start, rows), rows)]

    own_copies = [
        pltpu.make_async_copy(packs[kind], part(kind, row, deep, core), local.at[kind]) for kind in range(2)
    ]
    for copy in own_copies:
        copy.start()

    def z_copy(kind, step):
        return remote(packs[kind], part(kind, row, deep, core), z_send.at[kind, step], z_recv.at[kind, step],
                      (row, (deep + step) % n_deep * 2 + core))

    def plane_copy(kind, step, hop, source):
        here = part(kind, row, (deep + n_deep - hop) % n_deep, core)
        return remote(here if source is None else source, here, p_send.at[kind, hop, step], p_recv.at[kind, hop, step],
                      (row_of(row, step), seq))

    def corner_copy(kind, step, hop):
        here = part(kind, row_of(row, step), (deep + n_deep - hop) % n_deep, core)
        return remote(here, here, p_send.at[kind, hop, 3], p_recv.at[kind, hop, 3], (row_of(row, 3 - step), seq))

    def core_copy(kind, step, hop, source):
        here = part(kind, row_of(row, step), (deep + n_deep - hop) % n_deep, core)
        return remote(here if source is None else source, here, d_send.at[kind, hop, step], d_recv.at[kind, hop, step],
                      sibling)

    def dense_start(kind):
        def start_z(step, carry):
            z_copy(kind, step).start()
            return carry

        lax.fori_loop(1, n_deep, start_z, 0)
        for step in range(1, 3):
            plane_copy(kind, step, 0, packs[kind]).start()
        core_copy(kind, 0, 0, packs[kind]).start()

    def dense_relay(kind):
        def relay(hop, carry):
            there = part(kind, row, (deep + n_deep - hop) % n_deep, core)
            remote(there, there, z_send.at[kind, hop], z_recv.at[kind, hop], sibling).wait_recv()
            for step in range(1, 3):
                plane_copy(kind, step, hop, None).start()
            core_copy(kind, 0, hop, None).start()
            return carry

        lax.fori_loop(1, n_deep, relay, 0)

    def dense_finish(kind):
        def landed(hop, step):
            there = part(kind, row_of(row, step), (deep + n_deep - hop) % n_deep, core)
            remote(there, there, p_send.at[kind, hop, step], p_recv.at[kind, hop, step], sibling).wait_recv()
            core_copy(kind, step, hop, None).start()

        def spread(hop, carry):
            for step in range(1, 3):
                landed(hop, step)

                @pl.when(hop % 2 == step - 1)
                def _():
                    corner_copy(kind, step, hop).start()

            return carry

        lax.fori_loop(0, n_deep, spread, 0)

        def corner(hop, carry):
            landed(hop, 3)
            return carry

        lax.fori_loop(0, n_deep, corner, 0)
        own_copies[kind].wait()

        def gathered(index, carry):
            hop, step = index // 4, index % 4
            there = part(kind, row_of(row, step), (deep + n_deep - hop) % n_deep, 1 - core)
            remote(there, there, d_send.at[kind, hop, step], d_recv.at[kind, hop, step], sibling).wait_recv()
            return carry

        lax.fori_loop(0, n_deep * 4, gathered, 0)

    def expert_copy(kind, source, step):
        other = (me + step) % total
        other_row, other_seq = other // n_seq, other % n_seq
        return remote(
            source.at[other_row * 4 + other_seq % 4],
            held.at[other_seq % 2, kind, pl.ds(pl.multiple_of(me * rows, rows), rows)],
            e_send.at[kind, step], e_recv.at[kind, step], (other_row, other_seq),
        )

    sources = (gate, up, down)
    expert_own = [
        pltpu.make_async_copy(
            source.at[row * 4 + seq % 4],
            held.at[core, kind, pl.ds(pl.multiple_of(me * rows, rows), rows)],
            e_local.at[kind],
        )
        for kind, source in enumerate(sources)
    ]

    def experts_start(lo, hi):
        def start_experts(index, carry):
            for kind in range(3):
                expert_copy(kind, sources[kind], index * STRIDE % total).start()
            return carry

        lax.fori_loop(lo, hi, start_experts, 0)

    g_one, g_two, g_three, g_last, g_sent = tree_rounds(row, seq, g_in, g_out, g_send, g_recv)
    g_own = pltpu.make_async_copy(g_in, g_out.at[0], group_local.at[0])

    dense_start(0)
    dense_start(1)
    for copy in expert_own:
        copy.start()
    g_own.start()
    experts_start(1, total * 5 // 8)
    x = x_in[...].astype(full)
    scale_one = norm_scale(x)
    for t in range(2):
        own = segments_in[t:t + 1, pl.ds(pl.multiple_of(seq * block, block), block)].astype(full)
        own = column(own)
        smaller = jnp.zeros((block, 128), full)
        for lo in range(0, segments_in.shape[1], 128):
            smaller += jnp.where(segments_in[t:t + 1, lo:lo + 128].astype(full) < own, 1.0, 0.0)
        begin = jnp.broadcast_to(jnp.sum(smaller, axis=1, keepdims=True), (block, 128))
        start_in[block * t:block * (t + 1)] = begin.astype(jnp.int32)
        place = lax.broadcasted_iota(jnp.int32, (block, 128), 0) + seq * block
        angle = (place.astype(full) - begin) * turns_in[:1]
        cos_in[block * t:block * (t + 1)] = jnp.cos(angle)
        sin_in[block * t:block * (t + 1)] = jnp.sin(angle) * turns_in[1:2]

    dense_relay(0)
    dense_finish(0)
    small = w_kv[:, 1024:].astype(full)
    counts_out[...] = jnp.broadcast_to(jnp.sum(small, axis=0, keepdims=True), (8, 128))
    small = small.T
    gain_one, gain_two = small[16:17], small[17:18]
    normed[...] = (x * scale_one * gain_one).astype(low)

    lane = lax.broadcasted_iota(jnp.int32, (tokens, 128), 1)
    cosine, sine = cos_in[...], sin_in[...]

    def turn(value):
        return value * cosine + jnp.where(lane % 64 < 32, pltpu.roll(value, 96, 1), pltpu.roll(value, 32, 1)) * sine

    for pair in range(4):
        lanes = slice(128 * pair, 128 * (pair + 1))
        value_lanes = slice(512 + 128 * pair, 640 + 128 * pair)
        key = turn(mul(normed[...], w_kv[:, lanes], NN)).astype(low)
        value = mul(normed[...], w_kv[:, value_lanes], NN).astype(low)
        for t in range(2):
            here = slice(block * t, block * (t + 1))
            kv[core, t, :, lanes] = key[here]
            kv[core, t, :, value_lanes] = value[here]

    def kv_copy(hop):
        return remote(kv.at[(hop - 1) * 2 + core], kv.at[hop * 2 + core], kv_send.at[hop], kv_recv.at[hop],
                      (row, seq + 2))

    def kv_pass(hop, of_core):
        there = kv.at[hop * 2 + of_core]
        return remote(there, there, kvd_send.at[hop], kvd_recv.at[hop], sibling)

    @pl.when(deep + 1 < n_deep)
    def _():
        kv_copy(1).start()

    for hop in range(1, back + 1):
        @pl.when(deep < hop)
        def _():
            kv[2 * hop] = jnp.zeros(kv.shape[1:], low)
            kv[2 * hop + 1] = jnp.zeros(kv.shape[1:], low)

    kv_pass(0, core).start()
    dense_relay(1)
    g_one()
    dense_finish(1)
    g_two()
    half_lane = lax.broadcasted_iota(jnp.int32, (block, 128), 1) < 64
    for head in range(8):
        both = turn(mul(normed[...], w_qo[:, 128 * head:128 * (head + 1)], NN))
        for t in range(2):
            value = both[block * t:block * (t + 1)]
            other = pltpu.roll(value, 64, 1)
            if head % 2 == 0:
                first, second = jnp.where(half_lane, value, 0.0), jnp.where(half_lane, other, 0.0)
            else:
                first, second = jnp.where(half_lane, 0.0, other), jnp.where(half_lane, 0.0, value)
            queries[t * 8 + head, :block] = first.astype(low)
            queries[t * 8 + head, block:] = second.astype(low)

    for hop in range(1, back + 1):
        @pl.when(deep >= hop)
        def _():
            kv_copy(hop).wait_recv()
            if hop < back:
                @pl.when(deep + 1 < n_deep)
                def _():
                    kv_copy(hop + 1).start()

            kv_pass(hop, core).start()

        if hop == 1:
            experts_start(total * 5 // 8, total)

    kv_pass(0, 1 - core).wait_recv()
    for hop in range(1, back + 1):
        @pl.when(deep >= hop)
        def _():
            kv_pass(hop, 1 - core).wait_recv()

    g_three()
    places = window_slots(core, slots)
    for t in range(2):
        visible = visibility(seq, slots, block, start_in[block * t:block * (t + 1)])

        def attend(pair, carry):
            lanes = pl.ds(pl.multiple_of(128 * pair, 128), 128)
            value_lanes = pl.ds(pl.multiple_of(512 + 128 * pair, 128), 128)
            values = jnp.concatenate([kv[slot, t, :, value_lanes] for slot in places], axis=0)
            for half in range(2):
                head = 2 * pair + half
                query = queries[t * 8 + head]
                scores = jnp.concatenate(
                    [mul(query, kv[slot, t, :, lanes], NT) for slot in places], axis=1
                )
                scores = jnp.where(visible, SCORE_SCALE * scores, NEGATIVE)
                peak = jnp.max(scores, axis=1, keepdims=True)
                raised = jnp.exp(scores - peak)
                denominator = jnp.sum(raised, axis=1, keepdims=True)
                probs = (raised / denominator).astype(low)
                out = mul(probs, values, NN)
                if half == 0:
                    joined = jnp.where(half_lane, out[:block], pltpu.roll(out[block:], 64, 1))
                else:
                    joined = jnp.where(half_lane, pltpu.roll(out[:block], 64, 1), out[block:])
                mixed[block * t:block * (t + 1), pl.ds(pl.multiple_of(128 * head, 128), 128)] = joined.astype(low)
                lse[t] = jnp.where(lane == head, peak + jnp.log(denominator), lse[t])
            return carry

        lax.fori_loop(0, 4, attend, 0)

    for lo in range(0, width, 256):
        branch = mul(mixed[...], w_qo[lo:lo + 256, 1024:], NT)
        hidden[:, lo:lo + 256] = x_in[:, lo:lo + 256].astype(full) + RESIDUAL * branch
    scale_two = norm_scale(hidden[...])
    xtwo_out[...] = (hidden[...] * scale_two * gain_two).astype(low)
    x_one, x_two, x_three, x_last, x_sent = tree_rounds(row, seq, xtwo_out, xs_out, x_send, x_recv)
    x_one()
    logits = mul(xtwo_out[...], w_kv[:, 1024:], NN)
    picked = picks_in[...] > 0
    logits = jnp.where(picked, logits, NEGATIVE)
    raised = jnp.where(picked, jnp.exp(logits - jnp.max(logits, axis=1, keepdims=True)), 0.0)
    gates = raised / jnp.sum(raised, axis=1, keepdims=True)
    gates_out[...] = gates.T[:EXPERTS]

    def gate_copy(step):
        return remote(gates_out, gates_all.at[step], gate_send.at[step], gate_recv.at[step], peer_of(row, seq, step))

    def send_gates(step, carry):
        gate_copy(step).start()
        return carry

    lax.fori_loop(1, 8, send_gates, 0)
    group_own = [
        g_own,
        pltpu.make_async_copy(xtwo_out, xs_out.at[0], group_local.at[1]),
        pltpu.make_async_copy(gates_out, gates_all.at[0], group_local.at[2]),
    ]
    for copy in group_own[1:]:
        copy.start()

    stores = [
        pltpu.make_async_copy(source, target, store.at[i])
        for i, (source, target) in enumerate((
            (w_kv, w_kv_out), (w_qo, w_qo_out), (kv, kv_out), (queries, queries_out), (normed, normed_out),
            (mixed, mixed_out), (hidden, hidden_out), (lse, lse_out),
        ))
    ]
    for copy in stores:
        copy.start()

    def arrived(step, carry):
        other = (me + total - step) % total
        for kind in range(3):
            there = held.at[core, kind, pl.ds(pl.multiple_of(other * rows, rows), rows)]
            remote(there, there, e_send.at[kind, step], e_recv.at[kind, step], sibling).wait_recv()
        return carry

    lax.fori_loop(1, total, arrived, 0)
    for copy in expert_own:
        copy.wait()
    remote(held.at[core], held.at[core], pass_send, pass_recv, sibling).start()

    def settle_experts(step, carry):
        for kind, source in enumerate(sources):
            expert_copy(kind, source, step).wait_send()
        return carry

    lax.fori_loop(1, total, settle_experts, 0)
    g_last()
    g_sent()
    x_two()
    x_three()
    x_last()
    x_sent()
    for copy in group_own:
        copy.wait()

    def settle_gates(step, carry):
        gate_copy(step).wait()
        return carry

    lax.fori_loop(1, 8, settle_gates, 0)
    for kind in range(2):
        def settle_z(step, carry):
            z_copy(kind, step).wait_send()
            return carry

        lax.fori_loop(1, n_deep, settle_z, 0)

        def settle_plane(index, carry):
            hop, step = index // 4, index % 4
            core_copy(kind, step, hop, None).wait_send()

            @pl.when((step > 0) & (step < 3))
            def _():
                plane_copy(kind, step, hop, None).wait_send()

            @pl.when((step > 0) & (step < 3) & (hop % 2 == step - 1))
            def _():
                corner_copy(kind, step, hop).wait_send()

            return carry

        lax.fori_loop(0, n_deep * 4, settle_plane, 0)

    kv_pass(0, core).wait_send()
    for hop in range(1, back + 1):
        @pl.when((deep + 1 < n_deep) & (deep >= hop - 1))
        def _():
            kv_copy(hop).wait_send()

        @pl.when(deep >= hop)
        def _():
            kv_pass(hop, core).wait_send()

    for copy in stores:
        copy.wait()
    share = remote(held.at[core], held.at[1 - core], pass_send, pass_recv, sibling)
    share.wait_recv()
    remote(held.at[core], held.at[core], pass_send, pass_recv, sibling).wait_send()


def window_slots(core, slots):
    return [(d + 1 - core) // 2 * 2 + (core + d) % 2 for d in range(slots - 1)]


def visibility(seq, slots, block, start):
    key = lax.broadcasted_iota(jnp.int32, (block, block), 1)
    query = lax.broadcasted_iota(jnp.int32, (block, block), 0) + seq * block
    tiles = []
    for d in range(slots - 1):
        position = key + (seq - d) * block
        seen = jnp.where((position >= start) & (position <= query), 1.0, 0.0)
        tiles.append(jnp.concatenate([seen, seen], axis=0))
    return jnp.concatenate(tiles, axis=1) > 0.5


def run_forward(n_row, n_seq, length, key, value, query, out, small, turns, segments, ids, x, g, gate, up, down):
    tokens, width = x.shape
    experts, rows, hidden = gate.shape
    total, n_deep = n_row * n_seq, n_seq // 2
    block = tokens // 2
    back = window_of(length, block, n_deep)
    slots = 2 * (back + 1)
    low, full = jnp.bfloat16, jnp.float32
    dma = pltpu.SemaphoreType.DMA
    kv = (slots, 2, block, 1024)
    shape = jax.ShapeDtypeStruct
    return pl.pallas_call(
        functools.partial(forward_kernel, n_row, n_seq, back),
        out_shape=(
            shape((tokens, 128), full),
            shape((tokens, 128), full),
            shape((tokens, 128), jnp.int32),
            shape((tokens, width), low),
            shape((EXPERTS, tokens), full),
            shape((8, 128), full),
            shape((tokens, width), full),
            shape((tokens, 1024), low),
            shape((2, 2 * block, 128), full),
            shape((tokens, width), low),
            shape((16, 2 * block, 128), low),
            shape(kv, low),
            shape((width, 1152), low),
            shape((width, 2048), low),
            shape((8, tokens, width), low),
            shape((8, tokens, width), low),
            shape((8, EXPERTS, tokens), full),
            shape((2, 3, width, hidden), low),
        ),
        in_specs=[VMEM] * 9 + [ANY] * 4,
        out_specs=(VMEM,) * 6 + (ANY,) * 12,
        scratch_shapes=[
            pltpu.VMEM((rows, 1152), low),
            pltpu.VMEM((rows, 2048), low),
            pltpu.VMEM((128, 128), full),
            pltpu.VMEM((tokens, 128), full),
            pltpu.VMEM((width, 1152), low),
            pltpu.VMEM((width, 2048), low),
            pltpu.VMEM(kv, low),
            pltpu.VMEM((16, 2 * block, 128), low),
            pltpu.VMEM((tokens, width), low),
            pltpu.VMEM((tokens, 1024), low),
            pltpu.VMEM((tokens, width), full),
            pltpu.VMEM((2, 2 * block, 128), full),
            dma((2, n_deep)), dma((2, n_deep)),
            dma((2, n_deep, 4)), dma((2, n_deep, 4)),
            dma((2, n_deep, 4)), dma((2, n_deep, 4)),
            dma((back + 1,)), dma((back + 1,)),
            dma((back + 1,)), dma((back + 1,)),
            dma((9,)), dma((9,)), dma((9,)), dma((9,)), dma((8,)), dma((8,)), dma((3,)),
            dma((3, total)), dma((3, total)), dma((3,)),
            dma, dma, dma((2,)), dma((8,)),
        ],
        compiler_params=pltpu.CompilerParams(
            collective_id=1, has_side_effects=True, vmem_limit_bytes=60 << 20
        ),
        name="forward",
    )(key, value, query, out, small, turns, segments, ids, x, g, gate, up, down)


def experts_kernel(
    n_seq, xs_in, gs_in, gates_in, w_in, hidden_in, layer_out, dx_out, dg_out, grad_out,
    xs, gs, gates, w, acc, mids, thirds_got, second_got, last_got, dg_made, dg_got, half_made, half_got,
    t_send, t_recv, s_send, s_recv, l_send, l_recv, dg_send, dg_recv, load, half_send, half_recv, done_sem,
):
    row, seq = lax.axis_index("row"), lax.axis_index("seq")
    core, chip_z = seq % 2, seq // 2 % 2
    tokens, width = hidden_in.shape
    ff = w.shape[1] // 6
    mine = (row * 2 + chip_z) * 2
    low, full = jnp.bfloat16, jnp.float32
    sibling = (row, seq // 2 * 2 + (1 - core))
    thirds = thirds_of(tokens)
    columns = ((0, 0), (0, 1), (1, 0), (1, 1), (0, 2), (1, 2))
    loads = [
        pltpu.make_async_copy(w_in.at[j, kind], w.at[:, pl.ds(col * ff, ff)], load.at[col])
        for col, (j, kind) in enumerate(columns)
    ]
    loads.append(pltpu.make_async_copy(gates_in, gates, load.at[6]))
    loads += [
        pltpu.make_async_copy(source.at[7], target.at[7], load.at[7 + i])
        for i, (source, target) in enumerate(((xs_in, xs), (gs_in, gs)))
    ]
    others = [
        pltpu.make_async_copy(source.at[pl.ds(0, 7)], target.at[pl.ds(0, 7)], load.at[9 + i])
        for i, (source, target) in enumerate(((xs_in, xs), (gs_in, gs)))
    ]
    for copy in loads + others:
        copy.start()
    barrier = pltpu.get_barrier_semaphore()

    def greet(step, carry):
        pl.semaphore_signal(barrier, inc=1, device_id=peer_of(row, seq, step), device_id_type=MESH)
        return carry

    lax.fori_loop(1, 8, greet, 0)
    pl.semaphore_signal(barrier, inc=1, device_id=sibling, device_id_type=MESH)
    acc[...] = jnp.zeros_like(acc)
    pl.semaphore_wait(barrier, 8)
    for copy in loads:
        copy.wait()

    def dg_copy(step):
        return remote(dg_made.at[step], dg_got.at[step], dg_send.at[step], dg_recv.at[step], peer_of(row, seq, step))

    results = (xs, gs)

    def third_copy(i, which):
        rows = pl.ds(*thirds[i])
        return remote(results[which].at[7, rows], thirds_got.at[which, rows], t_send.at[which, i], t_recv.at[which, i],
                      peer_of(row, seq, (1, 2, 4)[i]))

    def second_copy(i, which):
        return remote(results[which].at[(6, 5, 3)[i]], second_got.at[which, i], s_send.at[which, i], s_recv.at[which, i],
                      peer_of(row, seq, (2, 4, 1)[i]))

    def last_copy(i, which):
        slot = (4, 1, 2)[i]
        return remote(results[which].at[slot], last_got.at[which, i], l_send.at[which, i], l_recv.at[which, i],
                      peer_of(row, seq, slot))

    def relay_third(i):
        for which in range(2):
            rows, slot = pl.ds(*thirds[i]), (6, 5, 3)[i]
            third_copy(i, which).wait_recv()
            results[which][slot, rows] = (
                results[which][slot, rows].astype(full) + thirds_got[which, rows].astype(full)
            ).astype(low)
            second_copy(i, which).start()

    def relay_second(i):
        for which in range(2):
            slot = (4, 1, 2)[i]
            second_copy(i, which).wait_recv()
            results[which][slot] = (
                results[which][slot].astype(full) + second_got[which, i].astype(full)
            ).astype(low)
            last_copy(i, which).start()

    def block(index, carry):
        step = 7 - index + jnp.where(index == 3, -1, 0) + jnp.where(index == 4, 1, 0)
        step = jnp.where(index == 5, 1, jnp.where(index == 6, 2, step))
        @pl.when(index == 1)
        def _():
            for copy in others:
                copy.wait()

        x, g = xs[step], gs[step]
        for j in range(2):
            gate = column(gates[step, pl.ds(mine + j, 1)])[:, :1]
            a = mul(x, w[:, 2 * j * ff:(2 * j + 1) * ff], NN)
            b = mul(x, w[:, (2 * j + 1) * ff:(2 * j + 2) * ff], NN)
            back = RESIDUAL * mul(g, w[:, (4 + j) * ff:(5 + j) * ff], NN)
            sigma = jax.nn.sigmoid(a)
            smooth = a * sigma
            inner = smooth * b
            dgate = jnp.sum(inner * back, axis=1, keepdims=True)
            back = gate * back
            mids[:, (4 + j) * ff:(5 + j) * ff] = (gate * inner).astype(low)
            mids[:, 2 * j * ff:(2 * j + 1) * ff] = (back * b * (sigma + smooth * (1.0 - sigma))).astype(low)
            mids[:, (2 * j + 1) * ff:(2 * j + 2) * ff] = (back * smooth).astype(low)
            dg_made[step, j] = jnp.broadcast_to(dgate, (tokens, 128)).T[:8]
        for lo in range(0, width, 256):
            part = slice(lo, lo + 256)
            acc[part, :4 * ff] += mul(xs[step, :, part], mids[:, :4 * ff], TN)
            acc[part, 4 * ff:] += mul(gs[step, :, part], mids[:, 4 * ff:], TN)
        for lo in range(0, width, 256):
            part = slice(lo, lo + 256)
            xs[step, :, part] = mul(mids[:, 4 * ff:], w[part, 4 * ff:], NT).astype(low)
            gs[step, :, part] = mul(mids[:, :4 * ff], w[part, :4 * ff], NT).astype(low)

        @pl.when(index < 7)
        def _():
            dg_copy(step).start()

        @pl.when(index == 0)
        def _():
            for i in range(3):
                for which in range(2):
                    third_copy(i, which).start()

        for i in range(3):
            @pl.when(index == 1 + i)
            def _():
                relay_third(i)

            @pl.when(index == 5 + i)
            def _():
                relay_second(i)

        return carry

    lax.fori_loop(0, 8, block, 0)

    def share_of(j):
        wide = acc[:, pl.ds(pl.multiple_of(j * 2 * ff, 128), 2 * ff)]
        thin = RESIDUAL * acc[:, pl.ds(pl.multiple_of((4 + j) * ff, 128), ff)]
        return wide, thin

    wide, thin = share_of(1 - core)
    half_made[:, :2 * ff] = wide.astype(low)
    half_made[:, 2 * ff:] = thin.astype(low)
    half = remote(half_made, half_got, half_send, half_recv, sibling)
    half.start()
    dg_got[0] = dg_made[0]
    half.wait_recv()
    wide, thin = share_of(core)
    half_got[:, :2 * ff] = (wide + half_got[:, :2 * ff].astype(full)).astype(low)
    half_got[:, 2 * ff:] = (thin + half_got[:, 2 * ff:].astype(full)).astype(low)
    store = pltpu.make_async_copy(half_got, grad_out, done_sem)
    store.start()

    def settle(step, carry):
        dg_copy(step).wait()
        return carry

    lax.fori_loop(1, 8, settle, 0)

    def place(step, carry):
        other_row, other_seq = peer_of(row, seq, step)
        chip = other_row * 2 + other_seq // 2 % 2
        for j in range(2):
            dg_out[pl.ds(chip * 2 + j, 1)] = dg_got[step, j, :1]
        return carry

    lax.fori_loop(0, 8, place, 0)
    for i in range(3):
        for which in range(2):
            last_copy(i, which).wait_recv()
    dx_out[...] = gs[0].astype(full) + sum(last_got[1, i].astype(full) for i in range(3))
    mixture = xs[0].astype(full) + sum(last_got[0, i].astype(full) for i in range(3))
    layer_out[...] = (hidden_in[...] + RESIDUAL * mixture).astype(low)
    for i in range(3):
        for which in range(2):
            third_copy(i, which).wait_send()
            second_copy(i, which).wait_send()
            last_copy(i, which).wait_send()
    half.wait_send()
    store.wait()


def run_experts(n_row, n_seq, xs, gs, gates, w, hidden):
    _, tokens, width = xs.shape
    ff = w.shape[3]
    low, full = jnp.bfloat16, jnp.float32
    dma, shape = pltpu.SemaphoreType.DMA, jax.ShapeDtypeStruct
    return pl.pallas_call(
        functools.partial(experts_kernel, n_seq),
        out_shape=(
            shape((tokens, width), low),
            shape((tokens, width), full),
            shape((EXPERTS, tokens), full),
            shape((width, 3 * ff), low),
        ),
        in_specs=[ANY, ANY, ANY, ANY, VMEM],
        out_specs=(VMEM, VMEM, VMEM, ANY),
        scratch_shapes=[
            pltpu.VMEM((8, tokens, width), low),
            pltpu.VMEM((8, tokens, width), low),
            pltpu.VMEM((8, EXPERTS, tokens), full),
            pltpu.VMEM((width, 6 * ff), low),
            pltpu.VMEM((width, 6 * ff), full),
            pltpu.VMEM((tokens, 6 * ff), low),
            pltpu.VMEM((2, tokens, width), low),
            pltpu.VMEM((2, 3, tokens, width), low),
            pltpu.VMEM((2, 3, tokens, width), low),
            pltpu.VMEM((8, 2, 8, tokens), full),
            pltpu.VMEM((8, 2, 8, tokens), full),
            pltpu.VMEM((width, 3 * ff), low),
            pltpu.VMEM((width, 3 * ff), low),
            dma((2, 3)), dma((2, 3)), dma((2, 3)), dma((2, 3)), dma((2, 3)), dma((2, 3)),
            dma((8,)), dma((8,)), dma((11,)),
            dma, dma, dma,
        ],
        compiler_params=pltpu.CompilerParams(
            collective_id=3, has_side_effects=True, vmem_limit_bytes=60 << 20
        ),
        name="experts",
    )(xs, gs, gates, w, hidden)


def backward_kernel(
    n_row, n_seq, back,
    w_kv_in, w_qo_in, kv_in, queries_in, normed_in, mixed_in, x_in, g_in, cos_in, sin_in, start_in,
    hidden_in, xtwo_in, gates_in, dgates_in, dx_in, lse_in, expert_grads,
    input_out, q_out, k_out, v_out, o_out, small_out, held,
    w_kv, w_qo, kv, queries, outs, dq, dqkv, dkv_own, dkv_core, dkv_deep,
    grads_o, grads_q, grads_k, core_o, core_q, core_k, plane_o, plane_q, plane_k, deep_o, deep_q, deep_k,
    spread_out, load, k_send, k_recv, kd_send, kd_recv, e_send, e_recv, e_local,
    d_send, d_recv, p_send, p_recv, z_send, z_recv,
):
    row, seq = lax.axis_index("row"), lax.axis_index("seq")
    core, deep, n_deep = seq % 2, seq // 2, n_seq // 2
    me, total = row * n_seq + seq, n_row * n_seq
    sibling = (row, deep * 2 + (1 - core))
    rows = q_out.shape[0]
    tokens, width = x_in.shape
    block = tokens // 2
    low, full = jnp.bfloat16, jnp.float32
    slots = kv.shape[0]
    loads = [
        pltpu.make_async_copy(source, target, load.at[i])
        for i, (source, target) in enumerate(((w_kv_in, w_kv), (w_qo_in, w_qo), (kv_in, kv), (queries_in, queries)))
    ]
    for copy in loads:
        copy.start()
    greet_all(n_row, n_seq)

    def expert_copy(step):
        other = (me + step) % total
        return remote(
            expert_grads.at[pl.ds(pl.multiple_of(other * rows, rows), rows)],
            held.at[seq // 4, row * 4 + seq % 4],
            e_send.at[step], e_recv.at[step], (other // n_seq, other % n_seq),
        )

    expert_own = pltpu.make_async_copy(
        expert_grads.at[pl.ds(pl.multiple_of(me * rows, rows), rows)],
        held.at[seq // 4, row * 4 + seq % 4], e_local,
    )
    expert_own.start()

    def experts_start(lo, hi):
        def start_experts(index, carry):
            expert_copy(index * STRIDE % total).start()
            return carry

        lax.fori_loop(lo, hi, start_experts, 0)

    experts_start(1, total * 5 // 8)
    loads[0].wait()

    made, from_core = (grads_o, grads_q, grads_k), (core_o, core_q, core_k)
    from_plane, from_deep = (plane_o, plane_q, plane_k), (deep_o, deep_q, deep_k)

    def part(of_row, of_deep, of_core):
        return pl.ds(pl.multiple_of((of_row * n_seq + of_deep * 2 + of_core) * rows, rows), rows)

    def d_copy(kind, step, hop):
        there = part(row_of(row, step), (deep + hop) % n_deep, 1 - core)
        return remote(made[kind].at[there], from_core[kind].at[hop, step], d_send.at[kind, hop, step],
                      d_recv.at[kind, hop, step], sibling)

    def p_copy(kind, step, hop):
        there = part(row_of(row, step), (deep + hop) % n_deep, core)
        return remote(made[kind].at[there], from_plane[kind].at[hop, step - 1], p_send.at[kind, hop, step],
                      p_recv.at[kind, hop, step], (row_of(row, step), seq))

    def z_copy(kind, hop):
        there = part(row, (deep + hop) % n_deep, core)
        return remote(made[kind].at[there], from_deep[kind].at[hop], z_send.at[kind, hop], z_recv.at[kind, hop],
                      (row, (deep + hop) % n_deep * 2 + core))

    def dense_start(kind):
        def start_d(index, carry):
            d_copy(kind, 3 - index % 4, n_deep - 1 - index // 4).start()
            return carry

        lax.fori_loop(0, 4 * n_deep, start_d, 0)

    def dense_cores(kind):
        def sum_cores(index, carry):
            step, hop = 3 - index % 4, n_deep - 1 - index // 4
            d_copy(kind, step, hop).wait_recv()
            there = part(row_of(row, step), (deep + hop) % n_deep, core)
            made[kind][there] = (made[kind][there].astype(full) + from_core[kind][hop, step].astype(full)).astype(low)

            @pl.when(step > 0)
            def _():
                p_copy(kind, step, hop).start()

            return carry

        lax.fori_loop(0, 4 * n_deep, sum_cores, 0)

    def dense_plane(kind):
        def sum_plane(index, carry):
            hop = n_deep - 1 - index
            there = part(row, (deep + hop) % n_deep, core)
            for step in range(1, 4):
                p_copy(kind, step, hop).wait_recv()
            value = made[kind][there].astype(full)
            for step in range(1, 4):
                value += from_plane[kind][hop, step - 1].astype(full)
            made[kind][there] = value.astype(low)

            @pl.when(hop > 0)
            def _():
                z_copy(kind, hop).start()

            return carry

        lax.fori_loop(0, n_deep, sum_plane, 0)

    def dense_end(kind):
        value = made[kind][part(row, deep, core)].astype(full)
        for hop in range(1, n_deep):
            z_copy(kind, hop).wait_recv()
            value += from_deep[kind][hop].astype(full)
        return value


    def upright(value):
        return jnp.concatenate([value, jnp.zeros((128 - value.shape[0], tokens), full)], axis=0).T

    small = w_kv[:, 1024:].astype(full).T
    gain_one, gain_two = small[16:17], small[17:18]
    gates, dgates = upright(gates_in[...]), upright(dgates_in[...])
    dlogits = (gates * (dgates - jnp.sum(gates * dgates, axis=1, keepdims=True))).astype(low)
    dxtwo = dx_in[...] + mul(dlogits, w_kv[:, 1024:], NT)
    h = hidden_in[...]
    scale_two = norm_scale(h)
    weighted = gain_two * dxtwo
    dgain_two = jnp.sum(dxtwo * h * scale_two, axis=0, keepdims=True)
    input_out[...] = (
        g_in[...].astype(full)
        + scale_two * weighted
        - h * (scale_two * scale_two * scale_two) * jnp.mean(weighted * h, axis=1, keepdims=True)
    )
    dbranch = (RESIDUAL * input_out[...]).astype(low)
    drouter = mul(xtwo_in[...], dlogits, TN)
    for lo in range(0, width, 256):
        grads_o[lo:lo + 256] = mul(dbranch[:, lo:lo + 256], mixed_in[...], TN).astype(low)
    dense_start(0)

    loads[1].wait()
    half_lane = lax.broadcasted_iota(jnp.int32, (block, 128), 1) < 64
    for head in range(8):
        both = mul(dbranch, w_qo[:, 1024 + 128 * head:1152 + 128 * head], NN)
        for t in range(2):
            value = both[block * t:block * (t + 1)]
            other = pltpu.roll(value, 64, 1)
            if head % 2 == 0:
                first, second = jnp.where(half_lane, value, 0.0), jnp.where(half_lane, other, 0.0)
            else:
                first, second = jnp.where(half_lane, 0.0, other), jnp.where(half_lane, 0.0, value)
            outs[t * 8 + head, :block] = first.astype(low)
            outs[t * 8 + head, block:] = second.astype(low)

    dense_cores(0)

    def kd_copy(hop, t):
        return remote(kv.at[hop * 2 + (1 - core), t], dkv_core.at[hop, t], kd_send.at[hop, t], kd_recv.at[hop, t], sibling)

    def k_copy(hop, t):
        return remote(kv.at[hop * 2 + core, t], dkv_deep.at[hop - 1, t], k_send.at[hop, t], k_recv.at[hop, t], (row, seq - 2))

    def k_start(t):
        for hop in range(back, -1, -1):
            @pl.when(deep >= hop)
            def _():
                kd_copy(hop, t).start()

    def k_sum(hop, t):
        @pl.when(deep >= hop)
        def _():
            kd_copy(hop, t).wait_recv()
            kv[hop * 2 + core, t] = (kv[hop * 2 + core, t].astype(full) + dkv_core[hop, t].astype(full)).astype(low)
            if hop < back:
                @pl.when(deep + 1 < n_deep)
                def _():
                    k_copy(hop + 1, t).wait_recv()
                    kv[hop * 2 + core, t] = (kv[hop * 2 + core, t].astype(full) + dkv_deep[hop, t].astype(full)).astype(low)

            k_copy(hop, t).start()

    lane = lax.broadcasted_iota(jnp.int32, (tokens, 128), 1)
    for copy in loads[2:]:
        copy.wait()
    places = window_slots(core, slots)
    kv[jnp.where(core == 0, 1, 2 * back)] = jnp.zeros(kv.shape[1:], low)
    for t in range(2):
        visible = visibility(seq, slots, block, start_in[block * t:block * (t + 1)])

        def attend(pair, carry):
            lanes = pl.ds(pl.multiple_of(128 * pair, 128), 128)
            value_lanes = pl.ds(pl.multiple_of(512 + 128 * pair, 128), 128)
            keys = jnp.concatenate([kv[slot, t, :, lanes] for slot in places], axis=0)
            values = jnp.concatenate([kv[slot, t, :, value_lanes] for slot in places], axis=0)
            dk, dv = 0.0, 0.0
            for half in range(2):
                head = 2 * pair + half
                query, dout = queries[t * 8 + head], outs[t * 8 + head]
                scores = jnp.where(visible, SCORE_SCALE * mul(query, keys, NT), NEGATIVE)
                total_log = jnp.sum(jnp.where(lane == head, lse_in[t], 0.0), axis=1, keepdims=True)
                probs = jnp.exp(scores - total_log)
                dprobs = mul(dout, values, NT)
                inner = jnp.sum(probs * dprobs, axis=1, keepdims=True)
                dscores = (probs * (dprobs - inner)).astype(low)
                dquery = SCORE_SCALE * mul(dscores, keys, NN)
                if half == 0:
                    joined = jnp.where(half_lane, dquery[:block], pltpu.roll(dquery[block:], 64, 1))
                else:
                    joined = jnp.where(half_lane, pltpu.roll(dquery[:block], 64, 1), dquery[block:])
                dq[block * t:block * (t + 1), pl.ds(pl.multiple_of(128 * head, 128), 128)] = joined
                dk += SCORE_SCALE * mul(dscores, query, TN)
                dv += mul(probs.astype(low), dout, TN)
            for d, slot in enumerate(places[1:], 1):
                kv[slot, t, :, lanes] = dk[block * d:block * (d + 1)].astype(low)
                kv[slot, t, :, value_lanes] = dv[block * d:block * (d + 1)].astype(low)
            dkv_own[t, :, lanes] = dk[:block]
            dkv_own[t, :, value_lanes] = dv[:block]
            return carry

        lax.fori_loop(0, 4, attend, 0)
        k_start(t)
        if t == 0:
            dense_plane(0)
            k_sum(back, 0)


    for hop in range(back - 1, 0, -1):
        k_sum(hop, 0)
    k_sum(back, 1)
    cosine, sine = cos_in[...], sin_in[...]

    def turn_back(value):
        return value * cosine - jnp.where(lane % 64 < 32, pltpu.roll(value, 96, 1), pltpu.roll(value, 32, 1)) * sine

    for head in range(8):
        lanes = slice(128 * head, 128 * (head + 1))
        dqkv[:, lanes] = turn_back(dq[:, lanes]).astype(low)
    for lo in range(0, width, 256):
        grads_q[lo:lo + 256] = mul(normed_in[:, lo:lo + 256], dqkv[:, :1024], TN).astype(low)
    dense_start(1)
    for hop in range(back - 1, 0, -1):
        k_sum(hop, 1)

    for lo in range(0, width, 256):
        part_q = slice(lo, lo + 256)
        dq[:, part_q] = mul(dqkv[:, :1024], w_qo[part_q, :1024], NT)
    dense_cores(1)
    experts_start(total * 5 // 8, total)
    for t in range(2):
        kd_copy(0, t).wait_recv()
        dkv_own[t] += dkv_core[0, t].astype(full)

        @pl.when(deep + 1 < n_deep)
        def _():
            k_copy(1, t).wait_recv()
            dkv_own[t] += dkv_deep[0, t].astype(full)

    for pair in range(4):
        lanes = slice(128 * pair, 128 * (pair + 1))
        value_lanes = slice(512 + 128 * pair, 640 + 128 * pair)
        dkey = jnp.concatenate([dkv_own[0, :, lanes], dkv_own[1, :, lanes]], axis=0)
        dqkv[:, 1024 + 128 * pair:1152 + 128 * pair] = turn_back(dkey).astype(low)
        dvalue = jnp.concatenate([dkv_own[0, :, value_lanes], dkv_own[1, :, value_lanes]], axis=0)
        dqkv[:, 1536 + 128 * pair:1664 + 128 * pair] = dvalue.astype(low)
    for lo in range(0, width, 256):
        grads_k[lo:lo + 256, :1024] = mul(normed_in[:, lo:lo + 256], dqkv[:, 1024:], TN).astype(low)
    x = x_in[...].astype(full)
    scale_one = norm_scale(x)
    for lo in range(0, width, 256):
        part_k = slice(lo, lo + 256)
        dq[:, part_k] += mul(dqkv[:, 1024:], w_kv[part_k, :1024], NT)
    dxone = dq[...]
    weighted = gain_one * dxone
    dgain_one = jnp.sum(dxone * x * scale_one, axis=0, keepdims=True)
    wide = lax.broadcasted_iota(jnp.int32, (width, 128), 1)
    grads_k[:, 1024:] = jnp.where(
        wide == 16, column(dgain_one), jnp.where(wide == 17, column(dgain_two), drouter)
    ).astype(low)
    dense_start(2)
    dense_plane(1)
    input_out[...] = (
        input_out[...]
        + scale_one * weighted
        - x * (scale_one * scale_one * scale_one) * jnp.mean(weighted * x, axis=1, keepdims=True)
    )
    dense_cores(2)
    dense_plane(2)
    o_out[...] = dense_end(0)
    q_out[...] = dense_end(1)
    last = dense_end(2)
    k_out[...] = last[:, :512]
    v_out[...] = last[:, 512:1024]
    spread_out[:rows] = last[:, 1024:]
    small_out[...] = spread_out[...].T
    for kind in range(3):
        def settle_d(index, carry):
            hop, step = index // 4, index % 4
            d_copy(kind, step, hop).wait_send()

            @pl.when(step > 0)
            def _():
                p_copy(kind, step, hop).wait_send()

            return carry

        lax.fori_loop(0, 4 * n_deep, settle_d, 0)

        def settle_z(hop, carry):
            z_copy(kind, hop).wait_send()
            return carry

        lax.fori_loop(1, n_deep, settle_z, 0)

    for hop in range(back + 1):
        for t in range(2):
            @pl.when(deep >= hop)
            def _():
                kd_copy(hop, t).wait_send()
                if hop > 0:
                    k_copy(hop, t).wait_send()

    expert_own.wait()

    def settle_experts(step, carry):
        other = (me + total - step) % total
        expert_copy(step).wait_send()
        there = held.at[other % n_seq // 4, other // n_seq * 4 + other % 4]
        remote(there, there, e_send.at[step], e_recv.at[step], sibling).wait_recv()
        return carry

    lax.fori_loop(1, total, settle_experts, 0)


def window_of(length, block, n_deep):
    back = length // 2 // (2 * block)
    assert back * 4 * block == length and 0 < back < n_deep
    return back


def run_backward(n_row, n_seq, length, w_kv, w_qo, kv, queries, normed, mixed, x, g, cosine, sine, start,
                 hidden, xtwo, gates, dgates, dx, lse, expert_grads):
    tokens, width = x.shape
    total, n_deep = n_row * n_seq, n_seq // 2
    rows, block = width // total, tokens // 2
    back = window_of(length, block, n_deep)
    columns = (1024, 1024, w_kv.shape[1])
    low, full = jnp.bfloat16, jnp.float32
    dma, shape = pltpu.SemaphoreType.DMA, jax.ShapeDtypeStruct
    return pl.pallas_call(
        functools.partial(backward_kernel, n_row, n_seq, back),
        out_shape=(
            shape((tokens, width), full),
            shape((rows, 1024), full),
            shape((rows, 512), full),
            shape((rows, 512), full),
            shape((rows, 1024), full),
            shape((128, 128), full),
            shape((n_seq // 4, n_row * 4, rows, expert_grads.shape[1]), low),
        ),
        in_specs=[ANY] * 4 + [VMEM] * 13 + [ANY],
        out_specs=(VMEM,) * 6 + (ANY,),
        scratch_shapes=[
            pltpu.VMEM(w_kv.shape, low),
            pltpu.VMEM(w_qo.shape, low),
            pltpu.VMEM(kv.shape, low),
            pltpu.VMEM((16, tokens, 128), low),
            pltpu.VMEM((16, tokens, 128), low),
            pltpu.VMEM((tokens, 1024), full),
            pltpu.VMEM((tokens, 2048), low),
            pltpu.VMEM(kv.shape[1:], full),
            pltpu.VMEM((back + 1,) + kv.shape[1:], low),
            pltpu.VMEM((back,) + kv.shape[1:], low),
        ]
        + [pltpu.VMEM((width, c), low) for c in columns]
        + [pltpu.VMEM((n_deep, 4, rows, c), low) for c in columns]
        + [pltpu.VMEM((n_deep, 3, rows, c), low) for c in columns]
        + [pltpu.VMEM((n_deep, rows, c), low) for c in columns]
        + [
            pltpu.VMEM((128, 128), full),
            dma((4,)),
            dma((back + 1, 2)), dma((back + 1, 2)), dma((back + 1, 2)), dma((back + 1, 2)),
            dma((total,)), dma((total,)), dma,
            dma((3, n_deep, 4)), dma((3, n_deep, 4)), dma((3, n_deep, 4)), dma((3, n_deep, 4)),
            dma((3, n_deep)), dma((3, n_deep)),
        ],
        compiler_params=pltpu.CompilerParams(
            collective_id=2, has_side_effects=True, vmem_limit_bytes=62 << 20
        ),
        name="backward",
    )(w_kv, w_qo, kv, queries, normed, mixed, x, g, cosine, sine, start, hidden, xtwo, gates, dgates, dx, lse,
      expert_grads)


def results_kernel(
    held, counts, small, *refs
):
    passed, copied = refs[:6], refs[6:12]
    gate_out, up_out, down_out, router_out, one_out, two_out, counts_out = refs[12:]
    ff = gate_out.shape[2]
    rows = router_out.shape[1]
    for source, target in zip(passed[:2], copied[:2]):
        target[...] = source[...]

    @pl.when(pl.program_id(0) == 0)
    def _():
        for source, target in zip(passed[2:], copied[2:]):
            target[...] = source[...]
        router_out[...] = small[:EXPERTS, :rows]
        one_out[...] = small[EXPERTS:EXPERTS + 1, :rows]
        two_out[...] = small[EXPERTS + 1:EXPERTS + 2, :rows]
        counts_out[...] = pltpu.roll(counts[...], 96, 1)[:1].astype(jnp.int32)

    for out, lo in ((gate_out, 0), (up_out, ff), (down_out, 2 * ff)):
        value = held[0, :, :, lo:lo + ff].astype(jnp.float32)
        for group in range(1, held.shape[0]):
            value += held[group, :, :, lo:lo + ff].astype(jnp.float32)
        out[...] = value


def run_results(held, counts, small, *passed):
    groups, experts, rows, wide = held.shape
    ff, full = wide // 3, jnp.float32
    some = experts // 4
    shape = jax.ShapeDtypeStruct
    whole = lambda i: (0, 0)
    moved = [pl.BlockSpec((a.shape[0] // 4, a.shape[1]), lambda i: (i, 0)) for a in passed[:2]]
    moved += [pl.BlockSpec(a.shape, whole) for a in passed[2:]]
    return pl.pallas_call(
        results_kernel,
        grid=(4,),
        out_shape=tuple(shape(a.shape, a.dtype) for a in passed) + (
            shape((experts, rows, ff), full),
            shape((experts, rows, ff), full),
            shape((experts, rows, ff), full),
            shape((EXPERTS, rows), full),
            shape((1, rows), full),
            shape((1, rows), full),
            shape((1, 128), jnp.int32),
        ),
        in_specs=[
            pl.BlockSpec((groups, some, rows, wide), lambda i: (0, i, 0, 0)),
            pl.BlockSpec((8, 128), whole),
            pl.BlockSpec((128, 128), whole),
        ] + moved,
        out_specs=tuple(moved) + (pl.BlockSpec((some, rows, ff), lambda i: (i, 0, 0)),) * 3 + (
            pl.BlockSpec((EXPERTS, rows), whole),
            pl.BlockSpec((1, rows), whole),
            pl.BlockSpec((1, rows), whole),
            pl.BlockSpec((1, 128), whole),
        ),
        name="results",
    )(held, counts, small, *passed)


def body(
    n_row,
    n_seq,
    tokens,
    segment_ids,
    expert_ids,
    norm1_gain,
    w_query,
    w_key,
    w_value,
    w_out,
    norm2_gain,
    w_router,
    w_gate,
    w_up,
    w_down,
    out_grad,
):
    row_count, block_len, width = tokens.shape
    token_count = row_count * block_len
    length = segment_ids.shape[1]
    rows = w_query.shape[0]
    full = jnp.float32
    small = jnp.concatenate([w_router.T, norm1_gain[None], norm2_gain[None], jnp.zeros((14, rows), norm1_gain.dtype)])
    lanes = np.arange(128) % HEAD
    half = HEAD // 2
    frequency = (THETA ** (-2.0 * (lanes % half) / HEAD)).astype(np.float32)
    turns = np.zeros((8, 128), np.float32)
    turns[0], turns[1] = frequency, np.where(lanes < half, -1.0, 1.0)
    x = tokens.reshape(token_count, width)
    g = out_grad.reshape(token_count, width)
    (cosine, sine, start, xtwo, gates, counts, hidden, mixed, lse, normed, queries, kv, w_kv, w_qo,
     group_g, group_x, group_gates, expert_weights) = run_forward(
        n_row, n_seq, length, w_key, w_value, w_query, w_out.T, small.astype(full), jnp.asarray(turns), segment_ids,
        jnp.swapaxes(expert_ids[0], 1, 2), x, g, w_gate, w_up, jnp.swapaxes(w_down, 1, 2)
    )
    layer_out, dx, dgates, expert_grads = run_experts(
        n_row, n_seq, group_x, group_g, group_gates, expert_weights, hidden
    )
    input_grad, dq, dk, dv, do, small, held = run_backward(
        n_row, n_seq, length, w_kv, w_qo, kv, queries, normed, mixed, x, g, cosine, sine, start,
        hidden, xtwo, gates, dgates, dx, lse, expert_grads,
    )
    layer_out, input_grad, dq, dk, dv, do, d_gate, d_up, d_down, router, one, two, counts = run_results(
        held, counts, small, layer_out, input_grad, dq, dk, dv, do
    )
    return (
        layer_out.reshape(row_count, block_len, width),
        input_grad.reshape(row_count, block_len, width),
        one[0],
        dq,
        dk,
        dv,
        do.T,
        two[0],
        router.T,
        d_gate,
        d_up,
        jnp.swapaxes(d_down, 1, 2),
        counts[0, :EXPERTS],
    )


def solution(mesh):
    in_specs = (
        P("row", "seq", None),
        P("row", None),
        P("seq", "row", None, None),
        P(("row", "seq")),
        P(("row", "seq"), None),
        P(("row", "seq"), None),
        P(("row", "seq"), None),
        P(None, ("row", "seq")),
        P(("row", "seq")),
        P(("row", "seq"), None),
        P(None, ("row", "seq"), None),
        P(None, ("row", "seq"), None),
        P(None, None, ("row", "seq")),
        P("row", "seq", None),
    )
    out_specs = (
        P("row", "seq", None),
        P("row", "seq", None),
        P(("row", "seq")),
        P(("row", "seq"), None),
        P(("row", "seq"), None),
        P(("row", "seq"), None),
        P(None, ("row", "seq")),
        P(("row", "seq")),
        P(("row", "seq"), None),
        P(None, ("row", "seq"), None),
        P(None, ("row", "seq"), None),
        P(None, None, ("row", "seq")),
        P(),
    )
    return jax.shard_map(
        functools.partial(body, mesh.shape["row"], mesh.shape["seq"]),
        mesh=mesh,
        in_specs=in_specs,
        out_specs=out_specs,
        check_vma=False,
    )
```

```python
import functools

import jax
import jax.numpy as jnp
import numpy as np
from jax import lax
from jax.experimental import pallas as pl
from jax.experimental.pallas import tpu as pltpu
from jax.sharding import PartitionSpec as P

HEAD = 64
EXPERTS = 16
TOPK = 8

EPSILON = 1e-06
SCORE_SCALE = 0.015625
RESIDUAL = 0.22
THETA = 10000.0
NEGATIVE = -1e30

MESH = pl.DeviceIdType.MESH
STRIDE = 11
ANY = pl.BlockSpec(memory_space=pl.ANY)
VMEM = pl.BlockSpec(memory_space=pltpu.VMEM)


def norm_scale(value):
    return lax.rsqrt(jnp.mean(value * value, axis=-1, keepdims=True) + EPSILON)


def greet_all(n_row, n_seq, wait=True):
    row, seq = lax.axis_index("row"), lax.axis_index("seq")
    me, total = row * n_seq + seq, n_row * n_seq
    barrier = pltpu.get_barrier_semaphore()

    def greet(step, carry):
        other = (me + step) % total
        pl.semaphore_signal(
            barrier, inc=1, device_id=(other // n_seq, other % n_seq), device_id_type=MESH
        )
        return carry

    lax.fori_loop(1, total, greet, 0)
    if wait:
        pl.semaphore_wait(barrier, total - 1)


NN = (((1,), (0,)), ((), ()))
NT = (((1,), (1,)), ((), ()))
TN = (((0,), (0,)), ((), ()))


def mul(a, b, dims):
    return lax.dot_general(a, b, dims, preferred_element_type=jnp.float32)


def column(row_values):
    return jnp.broadcast_to(row_values, (128, row_values.shape[1])).T


def peer_of(row, seq, step):
    other_row = (row // 2 + step // 4) % 2 * 2 + (row % 2 + step // 2 % 2) % 2
    other_seq = seq // 4 * 4 + (seq // 2 % 2 + step % 2) % 2 * 2 + seq % 2
    return (other_row, other_seq)


def row_of(row, step):
    return (row // 2 + step // 2) % 2 * 2 + (row % 2 + step % 2) % 2


def remote(source, target, send, recv, device):
    return pltpu.make_async_remote_copy(
        src_ref=source, dst_ref=target, send_sem=send, recv_sem=recv, device_id=device,
        device_id_type=MESH,
    )


def thirds_of(rows):
    cut = rows * 3 // 8
    rest = (rows - cut) // 2
    return ((0, cut), (cut, rest), (cut + rest, rest))


def tree_rounds(row, seq, own, slots, send, recv):
    thirds = thirds_of(own.shape[0])

    def hop(source, slot, toward, index):
        return remote(source, slot, send.at[index], recv.at[index], peer_of(row, seq, toward))

    def piece(slot, third):
        return slots.at[slot, pl.ds(*thirds[third])]

    first = lambda i: hop(own, slots.at[(1, 2, 4)[i]], (1, 2, 4)[i], i)
    second = lambda i: hop(slots.at[(2, 4, 1)[i]], slots.at[(3, 6, 5)[i]], (1, 2, 4)[i], 3 + i)
    third = lambda i: hop(piece((6, 5, 3)[i], i), piece(7, i), (1, 2, 4)[i], 6 + i)

    def start(make):
        for i in range(3):
            make(i).start()

    def landed(make):
        for i in range(3):
            make(i).wait_recv()

    def round_one():
        start(first)

    def round_two():
        landed(first)
        start(second)

    def round_three():
        landed(second)
        start(third)

    def last():
        landed(third)

    def sent():
        for make in (first, second, third):
            for i in range(3):
                make(i).wait_send()

    return round_one, round_two, round_three, last, sent


def forward_kernel(
    n_row, n_seq, back,
    key_in, value_in, query_in, out_in, small_in, turns_in, segments_in, ids_in, x_in, g_in, gate, up, down,
    cos_in, sin_in, start_in, xtwo_out, gates_out, counts_out, hidden_out, mixed_out, lse_out, normed_out, queries_out, kv_out,
    w_kv_out, w_qo_out, g_out, xs_out, gates_all, held,
    pack_kv, pack_qo, upright, picks_in, w_kv, w_qo, kv, queries, normed, mixed, hidden, lse,
    z_send, z_recv, p_send, p_recv, d_send, d_recv, kv_send, kv_recv, kvd_send, kvd_recv,
    g_send, g_recv, x_send, x_recv, gate_send, gate_recv, group_local, e_send, e_recv, e_local, pass_send, pass_recv, local, store,
):
    row, seq = lax.axis_index("row"), lax.axis_index("seq")
    core, deep, n_deep = seq % 2, seq // 2, n_seq // 2
    me, total = row * n_seq + seq, n_row * n_seq
    sibling = (row, deep * 2 + (1 - core))
    rows = key_in.shape[0]
    tokens, width = x_in.shape
    block = tokens // 2
    low, full = jnp.bfloat16, jnp.float32
    slots = kv.shape[0]
    packs, walls = (pack_kv, pack_qo), (w_kv, w_qo)
    greet_all(n_row, n_seq, False)

    sublane = lax.broadcasted_iota(jnp.int32, (128, 128), 0)
    for t in range(2):
        chosen = jnp.zeros((128, block), full)
        for choice in range(TOPK):
            chosen += jnp.where(ids_in[t, choice:choice + 1] == sublane, 1.0, 0.0)
        picks_in[block * t:block * (t + 1)] = chosen.T
    count = jnp.broadcast_to(jnp.sum(picks_in[...], axis=0, keepdims=True), (8, 128))
    upright[...] = jnp.zeros_like(upright)
    upright[:small_in.shape[0], :rows] = small_in[...]
    small = upright[...].T[:rows]
    counts = jnp.where(sublane[:rows] == 0, pltpu.roll(count, 32, 1)[:1], 0.0)
    pack_kv[:, :512] = key_in[...]
    pack_kv[:, 512:1024] = value_in[...]
    pack_kv[:, 1024:] = (small + counts).astype(low)
    pack_qo[:, :1024] = query_in[...]
    pack_qo[:, 1024:] = out_in[...]
    pl.semaphore_wait(pltpu.get_barrier_semaphore(), total - 1)

    def part(kind, of_row, of_deep, of_core):
        start = (of_row * n_seq + of_deep * 2 + of_core) * rows
        return walls[kind].at[pl.ds(pl.multiple_of(start, rows), rows)]

    own_copies = [
        pltpu.make_async_copy(packs[kind], part(kind, row, deep, core), local.at[kind]) for kind in range(2)
    ]
    for copy in own_copies:
        copy.start()

    def z_copy(kind, step):
        return remote(packs[kind], part(kind, row, deep, core), z_send.at[kind, step], z_recv.at[kind, step],
                      (row, (deep + step) % n_deep * 2 + core))

    def plane_copy(kind, step, hop, source):
        here = part(kind, row, (deep + n_deep - hop) % n_deep, core)
        return remote(here if source is None else source, here, p_send.at[kind, hop, step], p_recv.at[kind, hop, step],
                      (row_of(row, step), seq))

    def corner_copy(kind, step, hop):
        here = part(kind, row_of(row, step), (deep + n_deep - hop) % n_deep, core)
        return remote(here, here, p_send.at[kind, hop, 3], p_recv.at[kind, hop, 3], (row_of(row, 3 - step), seq))

    def core_copy(kind, step, hop, source):
        here = part(kind, row_of(row, step), (deep + n_deep - hop) % n_deep, core)
        return remote(here if source is None else source, here, d_send.at[kind, hop, step], d_recv.at[kind, hop, step],
                      sibling)

    def dense_start(kind):
        def start_z(step, carry):
            z_copy(kind, step).start()
            return carry

        lax.fori_loop(1, n_deep, start_z, 0)
        for step in range(1, 3):
            plane_copy(kind, step, 0, packs[kind]).start()
        core_copy(kind, 0, 0, packs[kind]).start()

    def dense_relay(kind):
        def relay(hop, carry):
            there = part(kind, row, (deep + n_deep - hop) % n_deep, core)
            remote(there, there, z_send.at[kind, hop], z_recv.at[kind, hop], sibling).wait_recv()
            for step in range(1, 3):
                plane_copy(kind, step, hop, None).start()
            core_copy(kind, 0, hop, None).start()
            return carry

        lax.fori_loop(1, n_deep, relay, 0)

    def dense_finish(kind):
        def landed(hop, step):
            there = part(kind, row_of(row, step), (deep + n_deep - hop) % n_deep, core)
            remote(there, there, p_send.at[kind, hop, step], p_recv.at[kind, hop, step], sibling).wait_recv()
            core_copy(kind, step, hop, None).start()

        def spread(hop, carry):
            for step in range(1, 3):
                landed(hop, step)

                @pl.when(hop % 2 == step - 1)
                def _():
                    corner_copy(kind, step, hop).start()

            return carry

        lax.fori_loop(0, n_deep, spread, 0)

        def corner(hop, carry):
            landed(hop, 3)
            return carry

        lax.fori_loop(0, n_deep, corner, 0)
        own_copies[kind].wait()

        def gathered(index, carry):
            hop, step = index // 4, index % 4
            there = part(kind, row_of(row, step), (deep + n_deep - hop) % n_deep, 1 - core)
            remote(there, there, d_send.at[kind, hop, step], d_recv.at[kind, hop, step], sibling).wait_recv()
            return carry

        lax.fori_loop(0, n_deep * 4, gathered, 0)

    def expert_copy(kind, source, step):
        other = (me + step) % total
        other_row, other_seq = other // n_seq, other % n_seq
        return remote(
            source.at[other_row * 4 + other_seq % 4],
            held.at[other_seq % 2, kind, pl.ds(pl.multiple_of(me * rows, rows), rows)],
            e_send.at[kind, step], e_recv.at[kind, step], (other_row, other_seq),
        )

    sources = (gate, up, down)
    expert_own = [
        pltpu.make_async_copy(
            source.at[row * 4 + seq % 4],
            held.at[core, kind, pl.ds(pl.multiple_of(me * rows, rows), rows)],
            e_local.at[kind],
        )
        for kind, source in enumerate(sources)
    ]

    def experts_start(lo, hi):
        for kind in range(3):
            def start_experts(index, carry):
                expert_copy(kind, sources[kind], index * STRIDE % total).start()
                return carry

            lax.fori_loop(lo, hi, start_experts, 0)

    g_one, g_two, g_three, g_last, g_sent = tree_rounds(row, seq, g_in, g_out, g_send, g_recv)
    g_own = pltpu.make_async_copy(g_in, g_out.at[0], group_local.at[0])

    dense_start(0)
    dense_start(1)
    for copy in expert_own:
        copy.start()
    g_own.start()
    experts_start(1, total * 5 // 8)
    x = x_in[...].astype(full)
    scale_one = norm_scale(x)
    for t in range(2):
        own = segments_in[t:t + 1, pl.ds(pl.multiple_of(seq * block, block), block)].astype(full)
        own = column(own)
        smaller = jnp.zeros((block, 128), full)
        for lo in range(0, segments_in.shape[1], 128):
            smaller += jnp.where(segments_in[t:t + 1, lo:lo + 128].astype(full) < own, 1.0, 0.0)
        begin = jnp.broadcast_to(jnp.sum(smaller, axis=1, keepdims=True), (block, 128))
        start_in[block * t:block * (t + 1)] = begin.astype(jnp.int32)
        place = lax.broadcasted_iota(jnp.int32, (block, 128), 0) + seq * block
        angle = (place.astype(full) - begin) * turns_in[:1]
        cos_in[block * t:block * (t + 1)] = jnp.cos(angle)
        sin_in[block * t:block * (t + 1)] = jnp.sin(angle) * turns_in[1:2]

    dense_relay(0)
    dense_finish(0)
    small = w_kv[:, 1024:].astype(full)
    counts_out[...] = jnp.broadcast_to(jnp.sum(small, axis=0, keepdims=True), (8, 128))
    small = small.T
    gain_one, gain_two = small[16:17], small[17:18]
    normed[...] = (x * scale_one * gain_one).astype(low)

    lane = lax.broadcasted_iota(jnp.int32, (tokens, 128), 1)
    cosine, sine = cos_in[...], sin_in[...]

    def turn(value):
        return value * cosine + jnp.where(lane % 64 < 32, pltpu.roll(value, 96, 1), pltpu.roll(value, 32, 1)) * sine

    for pair in range(4):
        lanes = slice(128 * pair, 128 * (pair + 1))
        value_lanes = slice(512 + 128 * pair, 640 + 128 * pair)
        key = turn(mul(normed[...], w_kv[:, lanes], NN)).astype(low)
        value = mul(normed[...], w_kv[:, value_lanes], NN).astype(low)
        for t in range(2):
            here = slice(block * t, block * (t + 1))
            kv[core, t, :, lanes] = key[here]
            kv[core, t, :, value_lanes] = value[here]

    def kv_copy(hop):
        return remote(kv.at[(hop - 1) * 2 + core], kv.at[hop * 2 + core], kv_send.at[hop], kv_recv.at[hop],
                      (row, seq + 2))

    def kv_pass(hop, of_core):
        there = kv.at[hop * 2 + of_core]
        return remote(there, there, kvd_send.at[hop], kvd_recv.at[hop], sibling)

    @pl.when(deep + 1 < n_deep)
    def _():
        kv_copy(1).start()

    for hop in range(1, back + 1):
        @pl.when(deep < hop)
        def _():
            kv[2 * hop] = jnp.zeros(kv.shape[1:], low)
            kv[2 * hop + 1] = jnp.zeros(kv.shape[1:], low)

    kv_pass(0, core).start()
    dense_relay(1)
    g_one()
    dense_finish(1)
    g_two()
    half_lane = lax.broadcasted_iota(jnp.int32, (block, 128), 1) < 64
    for head in range(8):
        both = turn(mul(normed[...], w_qo[:, 128 * head:128 * (head + 1)], NN))
        for t in range(2):
            value = both[block * t:block * (t + 1)]
            other = pltpu.roll(value, 64, 1)
            if head % 2 == 0:
                first, second = jnp.where(half_lane, value, 0.0), jnp.where(half_lane, other, 0.0)
            else:
                first, second = jnp.where(half_lane, 0.0, other), jnp.where(half_lane, 0.0, value)
            queries[t * 8 + head, :block] = first.astype(low)
            queries[t * 8 + head, block:] = second.astype(low)

    for hop in range(1, back + 1):
        @pl.when(deep >= hop)
        def _():
            kv_copy(hop).wait_recv()
            if hop < back:
                @pl.when(deep + 1 < n_deep)
                def _():
                    kv_copy(hop + 1).start()

            kv_pass(hop, core).start()

        if hop == 1:
            experts_start(total * 5 // 8, total)

    kv_pass(0, 1 - core).wait_recv()
    for hop in range(1, back + 1):
        @pl.when(deep >= hop)
        def _():
            kv_pass(hop, 1 - core).wait_recv()

    g_three()
    places = window_slots(core, slots)
    for t in range(2):
        visible = visibility(seq, slots, block, start_in[block * t:block * (t + 1)])

        def attend(pair, carry):
            lanes = pl.ds(pl.multiple_of(128 * pair, 128), 128)
            value_lanes = pl.ds(pl.multiple_of(512 + 128 * pair, 128), 128)
            values = jnp.concatenate([kv[slot, t, :, value_lanes] for slot in places], axis=0)
            for half in range(2):
                head = 2 * pair + half
                query = queries[t * 8 + head]
                scores = jnp.concatenate(
                    [mul(query, kv[slot, t, :, lanes], NT) for slot in places], axis=1
                )
                scores = jnp.where(visible, SCORE_SCALE * scores, NEGATIVE)
                peak = jnp.max(scores, axis=1, keepdims=True)
                raised = jnp.exp(scores - peak)
                denominator = jnp.sum(raised, axis=1, keepdims=True)
                probs = (raised / denominator).astype(low)
                out = mul(probs, values, NN)
                if half == 0:
                    joined = jnp.where(half_lane, out[:block], pltpu.roll(out[block:], 64, 1))
                else:
                    joined = jnp.where(half_lane, pltpu.roll(out[:block], 64, 1), out[block:])
                mixed[block * t:block * (t + 1), pl.ds(pl.multiple_of(128 * head, 128), 128)] = joined.astype(low)
                lse[t] = jnp.where(lane == head, peak + jnp.log(denominator), lse[t])
            return carry

        lax.fori_loop(0, 4, attend, 0)

    for lo in range(0, width, 256):
        branch = mul(mixed[...], w_qo[lo:lo + 256, 1024:], NT)
        hidden[:, lo:lo + 256] = x_in[:, lo:lo + 256].astype(full) + RESIDUAL * branch
    scale_two = norm_scale(hidden[...])
    xtwo_out[...] = (hidden[...] * scale_two * gain_two).astype(low)
    x_one, x_two, x_three, x_last, x_sent = tree_rounds(row, seq, xtwo_out, xs_out, x_send, x_recv)
    x_one()
    logits = mul(xtwo_out[...], w_kv[:, 1024:], NN)
    picked = picks_in[...] > 0
    logits = jnp.where(picked, logits, NEGATIVE)
    raised = jnp.where(picked, jnp.exp(logits - jnp.max(logits, axis=1, keepdims=True)), 0.0)
    gates = raised / jnp.sum(raised, axis=1, keepdims=True)
    gates_out[...] = gates.T[:EXPERTS]

    def gate_copy(step):
        return remote(gates_out, gates_all.at[step], gate_send.at[step], gate_recv.at[step], peer_of(row, seq, step))

    def send_gates(step, carry):
        gate_copy(step).start()
        return carry

    lax.fori_loop(1, 8, send_gates, 0)
    group_own = [
        g_own,
        pltpu.make_async_copy(xtwo_out, xs_out.at[0], group_local.at[1]),
        pltpu.make_async_copy(gates_out, gates_all.at[0], group_local.at[2]),
    ]
    for copy in group_own[1:]:
        copy.start()

    stores = [
        pltpu.make_async_copy(source, target, store.at[i])
        for i, (source, target) in enumerate((
            (w_kv, w_kv_out), (w_qo, w_qo_out), (kv, kv_out), (queries, queries_out), (normed, normed_out),
            (mixed, mixed_out), (hidden, hidden_out), (lse, lse_out),
        ))
    ]
    for copy in stores:
        copy.start()

    def share(kind, of_core):
        there = held.at[of_core, kind]
        return remote(there, there, pass_send.at[kind], pass_recv.at[kind], sibling)

    for kind in range(3):
        def arrived(step, carry):
            other = (me + total - step) % total
            there = held.at[core, kind, pl.ds(pl.multiple_of(other * rows, rows), rows)]
            remote(there, there, e_send.at[kind, step], e_recv.at[kind, step], sibling).wait_recv()
            return carry

        lax.fori_loop(1, total, arrived, 0)
        expert_own[kind].wait()
        share(kind, core).start()

    def settle_experts(step, carry):
        for kind, source in enumerate(sources):
            expert_copy(kind, source, step).wait_send()
        return carry

    lax.fori_loop(1, total, settle_experts, 0)
    g_last()
    g_sent()
    x_two()
    x_three()
    x_last()
    x_sent()
    for copy in group_own:
        copy.wait()

    def settle_gates(step, carry):
        gate_copy(step).wait()
        return carry

    lax.fori_loop(1, 8, settle_gates, 0)
    for kind in range(2):
        def settle_z(step, carry):
            z_copy(kind, step).wait_send()
            return carry

        lax.fori_loop(1, n_deep, settle_z, 0)

        def settle_plane(index, carry):
            hop, step = index // 4, index % 4
            core_copy(kind, step, hop, None).wait_send()

            @pl.when((step > 0) & (step < 3))
            def _():
                plane_copy(kind, step, hop, None).wait_send()

            @pl.when((step > 0) & (step < 3) & (hop % 2 == step - 1))
            def _():
                corner_copy(kind, step, hop).wait_send()

            return carry

        lax.fori_loop(0, n_deep * 4, settle_plane, 0)

    kv_pass(0, core).wait_send()
    for hop in range(1, back + 1):
        @pl.when((deep + 1 < n_deep) & (deep >= hop - 1))
        def _():
            kv_copy(hop).wait_send()

        @pl.when(deep >= hop)
        def _():
            kv_pass(hop, core).wait_send()

    for copy in stores:
        copy.wait()
    for kind in range(3):
        share(kind, core).wait_send()
        share(kind, 1 - core).wait_recv()


def window_slots(core, slots):
    return [(d + 1 - core) // 2 * 2 + (core + d) % 2 for d in range(slots - 1)]


def visibility(seq, slots, block, start):
    key = lax.broadcasted_iota(jnp.int32, (block, block), 1)
    query = lax.broadcasted_iota(jnp.int32, (block, block), 0) + seq * block
    tiles = []
    for d in range(slots - 1):
        position = key + (seq - d) * block
        seen = jnp.where((position >= start) & (position <= query), 1.0, 0.0)
        tiles.append(jnp.concatenate([seen, seen], axis=0))
    return jnp.concatenate(tiles, axis=1) > 0.5


def run_forward(n_row, n_seq, length, key, value, query, out, small, turns, segments, ids, x, g, gate, up, down):
    tokens, width = x.shape
    experts, rows, hidden = gate.shape
    total, n_deep = n_row * n_seq, n_seq // 2
    block = tokens // 2
    back = window_of(length, block, n_deep)
    slots = 2 * (back + 1)
    low, full = jnp.bfloat16, jnp.float32
    dma = pltpu.SemaphoreType.DMA
    kv = (slots, 2, block, 1024)
    shape = jax.ShapeDtypeStruct
    return pl.pallas_call(
        functools.partial(forward_kernel, n_row, n_seq, back),
        out_shape=(
            shape((tokens, 128), full),
            shape((tokens, 128), full),
            shape((tokens, 128), jnp.int32),
            shape((tokens, width), low),
            shape((EXPERTS, tokens), full),
            shape((8, 128), full),
            shape((tokens, width), full),
            shape((tokens, 1024), low),
            shape((2, 2 * block, 128), full),
            shape((tokens, width), low),
            shape((16, 2 * block, 128), low),
            shape(kv, low),
            shape((width, 1152), low),
            shape((width, 2048), low),
            shape((8, tokens, width), low),
            shape((8, tokens, width), low),
            shape((8, EXPERTS, tokens), full),
            shape((2, 3, width, hidden), low),
        ),
        in_specs=[VMEM] * 9 + [ANY] * 4,
        out_specs=(VMEM,) * 6 + (ANY,) * 12,
        scratch_shapes=[
            pltpu.VMEM((rows, 1152), low),
            pltpu.VMEM((rows, 2048), low),
            pltpu.VMEM((128, 128), full),
            pltpu.VMEM((tokens, 128), full),
            pltpu.VMEM((width, 1152), low),
            pltpu.VMEM((width, 2048), low),
            pltpu.VMEM(kv, low),
            pltpu.VMEM((16, 2 * block, 128), low),
            pltpu.VMEM((tokens, width), low),
            pltpu.VMEM((tokens, 1024), low),
            pltpu.VMEM((tokens, width), full),
            pltpu.VMEM((2, 2 * block, 128), full),
            dma((2, n_deep)), dma((2, n_deep)),
            dma((2, n_deep, 4)), dma((2, n_deep, 4)),
            dma((2, n_deep, 4)), dma((2, n_deep, 4)),
            dma((back + 1,)), dma((back + 1,)),
            dma((back + 1,)), dma((back + 1,)),
            dma((9,)), dma((9,)), dma((9,)), dma((9,)), dma((8,)), dma((8,)), dma((3,)),
            dma((3, total)), dma((3, total)), dma((3,)),
            dma((3,)), dma((3,)), dma((2,)), dma((8,)),
        ],
        compiler_params=pltpu.CompilerParams(
            collective_id=1, has_side_effects=True, vmem_limit_bytes=60 << 20
        ),
        name="forward",
    )(key, value, query, out, small, turns, segments, ids, x, g, gate, up, down)


def experts_kernel(
    n_seq, xs_in, gs_in, gates_in, w_in, hidden_in, layer_out, dx_out, dg_out, grad_out,
    xs, gs, gates, w, acc, mids, far, thirds_got, second_got, last_got, dg_made, dg_got, half_made, half_got,
    t_send, t_recv, s_send, s_recv, l_send, l_recv, dg_send, dg_recv, load, half_send, half_recv, done_sem,
):
    row, seq = lax.axis_index("row"), lax.axis_index("seq")
    core, chip_z = seq % 2, seq // 2 % 2
    tokens, width = hidden_in.shape
    ff = w.shape[1] // 6
    mine = (row * 2 + chip_z) * 2
    low, full = jnp.bfloat16, jnp.float32
    sibling = (row, seq // 2 * 2 + (1 - core))
    thirds = thirds_of(tokens)
    columns = ((0, 0), (0, 1), (1, 0), (1, 1), (0, 2), (1, 2))
    loads = [
        pltpu.make_async_copy(w_in.at[j, kind], w.at[:, pl.ds(col * ff, ff)], load.at[col])
        for col, (j, kind) in enumerate(columns)
    ]
    loads.append(pltpu.make_async_copy(gates_in, gates, load.at[6]))
    loads += [
        pltpu.make_async_copy(source.at[7], target.at[7], load.at[7 + i])
        for i, (source, target) in enumerate(((xs_in, xs), (gs_in, gs)))
    ]
    others = [
        pltpu.make_async_copy(source.at[pl.ds(0, 7)], target.at[pl.ds(0, 7)], load.at[9 + i])
        for i, (source, target) in enumerate(((xs_in, xs), (gs_in, gs)))
    ]
    for copy in loads + others:
        copy.start()
    barrier = pltpu.get_barrier_semaphore()

    def greet(step, carry):
        pl.semaphore_signal(barrier, inc=1, device_id=peer_of(row, seq, step), device_id_type=MESH)
        return carry

    lax.fori_loop(1, 8, greet, 0)
    pl.semaphore_signal(barrier, inc=1, device_id=sibling, device_id_type=MESH)
    acc[...] = jnp.zeros_like(acc)
    pl.semaphore_wait(barrier, 8)
    for copy in loads:
        copy.wait()

    def dg_copy(step):
        return remote(dg_made.at[step], dg_got.at[step], dg_send.at[step], dg_recv.at[step], peer_of(row, seq, step))

    results = (xs, gs)

    def third_copy(i, which):
        rows = pl.ds(*thirds[i])
        return remote(far.at[which, 0, rows], thirds_got.at[which, rows], t_send.at[which, i], t_recv.at[which, i],
                      peer_of(row, seq, (1, 2, 4)[i]))

    def second_copy(i, which):
        return remote(far.at[which, 1 + i], second_got.at[which, i], s_send.at[which, i], s_recv.at[which, i],
                      peer_of(row, seq, (2, 4, 1)[i]))

    def last_copy(i, which):
        slot = (4, 1, 2)[i]
        return remote(results[which].at[slot], last_got.at[which, i], l_send.at[which, i], l_recv.at[which, i],
                      peer_of(row, seq, slot))

    def relay_third(i):
        for which in range(2):
            rows = pl.ds(*thirds[i])
            third_copy(i, which).wait_recv()
            far[which, 1 + i, rows] = (
                far[which, 1 + i, rows].astype(full) + thirds_got[which, rows].astype(full)
            ).astype(low)
            second_copy(i, which).start()

    def relay_second(i):
        for which in range(2):
            slot = (4, 1, 2)[i]
            second_copy(i, which).wait_recv()
            results[which][slot] = (
                results[which][slot].astype(full) + second_got[which, i].astype(full)
            ).astype(low)
            last_copy(i, which).start()

    def order(index):
        step = 7 - index + jnp.where(index == 3, -1, 0) + jnp.where(index == 4, 1, 0)
        return jnp.where(index == 5, 1, jnp.where(index == 6, 2, step))

    def weigh(step, kept):
        for lo in range(0, width, 256):
            part = slice(lo, lo + 256)
            acc[part, :4 * ff] += mul(xs[step, :, part], mids[kept, :, :4 * ff], TN)
            acc[part, 4 * ff:] += mul(gs[step, :, part], mids[kept, :, 4 * ff:], TN)

    def block(is_far, index, carry):
        step, kept = order(index), index if is_far else 4

        @pl.when(index == 1)
        def _():
            for copy in others:
                copy.wait()

        x, g = xs[step], gs[step]
        for j in range(2):
            gate = column(gates[step, pl.ds(mine + j, 1)])[:, :1]
            a = mul(x, w[:, 2 * j * ff:(2 * j + 1) * ff], NN)
            b = mul(x, w[:, (2 * j + 1) * ff:(2 * j + 2) * ff], NN)
            back = RESIDUAL * mul(g, w[:, (4 + j) * ff:(5 + j) * ff], NN)
            sigma = jax.nn.sigmoid(a)
            smooth = a * sigma
            inner = smooth * b
            dgate = jnp.sum(inner * back, axis=1, keepdims=True)
            back = gate * back
            mids[kept, :, (4 + j) * ff:(5 + j) * ff] = (gate * inner).astype(low)
            mids[kept, :, 2 * j * ff:(2 * j + 1) * ff] = (back * b * (sigma + smooth * (1.0 - sigma))).astype(low)
            mids[kept, :, (2 * j + 1) * ff:(2 * j + 2) * ff] = (back * smooth).astype(low)
            dg_made[step, j] = jnp.broadcast_to(dgate, (tokens, 128)).T[:8]
        if not is_far:
            weigh(step, kept)
        for lo in range(0, width, 256):
            part = slice(lo, lo + 256)
            y = mul(mids[kept, :, 4 * ff:], w[part, 4 * ff:], NT).astype(low)
            dx = mul(mids[kept, :, :4 * ff], w[part, :4 * ff], NT).astype(low)
            if is_far:
                far[0, index, :, part] = y
                far[1, index, :, part] = dx
            else:
                xs[step, :, part] = y
                gs[step, :, part] = dx

        @pl.when(index < 7)
        def _():
            dg_copy(step).start()

        @pl.when(index == 0)
        def _():
            for i in range(3):
                for which in range(2):
                    third_copy(i, which).start()

        for i in range(3):
            @pl.when(index == 1 + i)
            def _():
                relay_third(i)

            @pl.when(index == (6, 7, 7)[i])
            def _():
                relay_second(i)

        return carry

    lax.fori_loop(0, 4, functools.partial(block, True), 0)
    lax.fori_loop(4, 8, functools.partial(block, False), 0)

    def weigh_far(index, carry):
        weigh(order(index), index)
        return carry

    lax.fori_loop(0, 4, weigh_far, 0)

    def share_of(j):
        wide = acc[:, pl.ds(pl.multiple_of(j * 2 * ff, 128), 2 * ff)]
        thin = RESIDUAL * acc[:, pl.ds(pl.multiple_of((4 + j) * ff, 128), ff)]
        return wide, thin

    wide, thin = share_of(1 - core)
    half_made[:, :2 * ff] = wide.astype(low)
    half_made[:, 2 * ff:] = thin.astype(low)
    half = remote(half_made, half_got, half_send, half_recv, sibling)
    half.start()
    dg_got[0] = dg_made[0]
    half.wait_recv()
    wide, thin = share_of(core)
    half_got[:, :2 * ff] = (wide + half_got[:, :2 * ff].astype(full)).astype(low)
    half_got[:, 2 * ff:] = (thin + half_got[:, 2 * ff:].astype(full)).astype(low)
    store = pltpu.make_async_copy(half_got, grad_out, done_sem)
    store.start()

    def settle(step, carry):
        dg_copy(step).wait()
        return carry

    lax.fori_loop(1, 8, settle, 0)

    def place(step, carry):
        other_row, other_seq = peer_of(row, seq, step)
        chip = other_row * 2 + other_seq // 2 % 2
        for j in range(2):
            dg_out[pl.ds(chip * 2 + j, 1)] = dg_got[step, j, :1]
        return carry

    lax.fori_loop(0, 8, place, 0)
    for i in range(3):
        for which in range(2):
            last_copy(i, which).wait_recv()
    dx_out[...] = gs[0].astype(full) + sum(last_got[1, i].astype(full) for i in range(3))
    mixture = xs[0].astype(full) + sum(last_got[0, i].astype(full) for i in range(3))
    layer_out[...] = (hidden_in[...] + RESIDUAL * mixture).astype(low)
    for i in range(3):
        for which in range(2):
            third_copy(i, which).wait_send()
            second_copy(i, which).wait_send()
            last_copy(i, which).wait_send()
    half.wait_send()
    store.wait()


def run_experts(n_row, n_seq, xs, gs, gates, w, hidden):
    _, tokens, width = xs.shape
    ff = w.shape[3]
    low, full = jnp.bfloat16, jnp.float32
    dma, shape = pltpu.SemaphoreType.DMA, jax.ShapeDtypeStruct
    return pl.pallas_call(
        functools.partial(experts_kernel, n_seq),
        out_shape=(
            shape((tokens, width), low),
            shape((tokens, width), full),
            shape((EXPERTS, tokens), full),
            shape((width, 3 * ff), low),
        ),
        in_specs=[ANY, ANY, ANY, ANY, VMEM],
        out_specs=(VMEM, VMEM, VMEM, ANY),
        scratch_shapes=[
            pltpu.VMEM((8, tokens, width), low),
            pltpu.VMEM((8, tokens, width), low),
            pltpu.VMEM((8, EXPERTS, tokens), full),
            pltpu.VMEM((width, 6 * ff), low),
            pltpu.VMEM((width, 6 * ff), full),
            pltpu.VMEM((5, tokens, 6 * ff), low),
            pltpu.VMEM((2, 4, tokens, width), low),
            pltpu.VMEM((2, tokens, width), low),
            pltpu.VMEM((2, 3, tokens, width), low),
            pltpu.VMEM((2, 3, tokens, width), low),
            pltpu.VMEM((8, 2, 8, tokens), full),
            pltpu.VMEM((8, 2, 8, tokens), full),
            pltpu.VMEM((width, 3 * ff), low),
            pltpu.VMEM((width, 3 * ff), low),
            dma((2, 3)), dma((2, 3)), dma((2, 3)), dma((2, 3)), dma((2, 3)), dma((2, 3)),
            dma((8,)), dma((8,)), dma((11,)),
            dma, dma, dma,
        ],
        compiler_params=pltpu.CompilerParams(
            collective_id=3, has_side_effects=True, vmem_limit_bytes=62 << 20
        ),
        name="experts",
    )(xs, gs, gates, w, hidden)


def backward_kernel(
    n_row, n_seq, back,
    w_kv_in, w_qo_in, kv_in, queries_in, normed_in, mixed_in, x_in, g_in, cos_in, sin_in, start_in,
    hidden_in, xtwo_in, gates_in, dgates_in, dx_in, lse_in, expert_grads,
    input_out, q_out, k_out, v_out, o_out, small_out, held,
    w_kv, w_qo, kv, queries, outs, dq, dqkv, dkv_own, dkv_core, dkv_deep,
    grads_o, grads_q, grads_k, core_o, core_q, core_k, plane_o, plane_q, plane_k, deep_o, deep_q, deep_k,
    spread_out, load, k_send, k_recv, kd_send, kd_recv, e_send, e_recv, e_local,
    d_send, d_recv, p_send, p_recv, z_send, z_recv,
):
    row, seq = lax.axis_index("row"), lax.axis_index("seq")
    core, deep, n_deep = seq % 2, seq // 2, n_seq // 2
    me, total = row * n_seq + seq, n_row * n_seq
    sibling = (row, deep * 2 + (1 - core))
    rows = q_out.shape[0]
    tokens, width = x_in.shape
    block = tokens // 2
    low, full = jnp.bfloat16, jnp.float32
    slots = kv.shape[0]
    loads = [
        pltpu.make_async_copy(source, target, load.at[i])
        for i, (source, target) in enumerate(((w_kv_in, w_kv), (w_qo_in, w_qo), (kv_in, kv), (queries_in, queries)))
    ]
    for copy in loads:
        copy.start()
    greet_all(n_row, n_seq)

    def expert_copy(step):
        other = (me + step) % total
        return remote(
            expert_grads.at[pl.ds(pl.multiple_of(other * rows, rows), rows)],
            held.at[seq // 4, row * 4 + seq % 4],
            e_send.at[step], e_recv.at[step], (other // n_seq, other % n_seq),
        )

    expert_own = pltpu.make_async_copy(
        expert_grads.at[pl.ds(pl.multiple_of(me * rows, rows), rows)],
        held.at[seq // 4, row * 4 + seq % 4], e_local,
    )
    expert_own.start()

    def experts_start(lo, hi):
        def start_experts(index, carry):
            expert_copy(index * STRIDE % total).start()
            return carry

        lax.fori_loop(lo, hi, start_experts, 0)

    experts_start(1, total * 5 // 8)
    loads[0].wait()

    made, from_core = (grads_o, grads_q, grads_k), (core_o, core_q, core_k)
    from_plane, from_deep = (plane_o, plane_q, plane_k), (deep_o, deep_q, deep_k)

    def part(of_row, of_deep, of_core):
        return pl.ds(pl.multiple_of((of_row * n_seq + of_deep * 2 + of_core) * rows, rows), rows)

    def d_copy(kind, step, hop):
        there = part(row_of(row, step), (deep + hop) % n_deep, 1 - core)
        return remote(made[kind].at[there], from_core[kind].at[hop, step], d_send.at[kind, hop, step],
                      d_recv.at[kind, hop, step], sibling)

    def p_copy(kind, step, hop):
        there = part(row_of(row, step), (deep + hop) % n_deep, core)
        return remote(made[kind].at[there], from_plane[kind].at[hop, step - 1], p_send.at[kind, hop, step],
                      p_recv.at[kind, hop, step], (row_of(row, step), seq))

    def z_copy(kind, hop):
        there = part(row, (deep + hop) % n_deep, core)
        return remote(made[kind].at[there], from_deep[kind].at[hop], z_send.at[kind, hop], z_recv.at[kind, hop],
                      (row, (deep + hop) % n_deep * 2 + core))

    def dense_start(kind):
        def start_d(index, carry):
            d_copy(kind, 3 - index % 4, n_deep - 1 - index // 4).start()
            return carry

        lax.fori_loop(0, 4 * n_deep, start_d, 0)

    def dense_cores(kind):
        def sum_cores(index, carry):
            step, hop = 3 - index % 4, n_deep - 1 - index // 4
            d_copy(kind, step, hop).wait_recv()
            there = part(row_of(row, step), (deep + hop) % n_deep, core)
            made[kind][there] = (made[kind][there].astype(full) + from_core[kind][hop, step].astype(full)).astype(low)

            @pl.when(step > 0)
            def _():
                p_copy(kind, step, hop).start()

            return carry

        lax.fori_loop(0, 4 * n_deep, sum_cores, 0)

    def dense_plane(kind):
        def sum_plane(index, carry):
            hop = n_deep - 1 - index
            there = part(row, (deep + hop) % n_deep, core)
            for step in range(1, 4):
                p_copy(kind, step, hop).wait_recv()
            value = made[kind][there].astype(full)
            for step in range(1, 4):
                value += from_plane[kind][hop, step - 1].astype(full)
            made[kind][there] = value.astype(low)

            @pl.when(hop > 0)
            def _():
                z_copy(kind, hop).start()

            return carry

        lax.fori_loop(0, n_deep, sum_plane, 0)

    def dense_end(kind):
        value = made[kind][part(row, deep, core)].astype(full)
        for hop in range(1, n_deep):
            z_copy(kind, hop).wait_recv()
            value += from_deep[kind][hop].astype(full)
        return value


    def upright(value):
        return jnp.concatenate([value, jnp.zeros((128 - value.shape[0], tokens), full)], axis=0).T

    small = w_kv[:, 1024:].astype(full).T
    gain_one, gain_two = small[16:17], small[17:18]
    gates, dgates = upright(gates_in[...]), upright(dgates_in[...])
    dlogits = (gates * (dgates - jnp.sum(gates * dgates, axis=1, keepdims=True))).astype(low)
    dxtwo = dx_in[...] + mul(dlogits, w_kv[:, 1024:], NT)
    h = hidden_in[...]
    scale_two = norm_scale(h)
    weighted = gain_two * dxtwo
    dgain_two = jnp.sum(dxtwo * h * scale_two, axis=0, keepdims=True)
    input_out[...] = (
        g_in[...].astype(full)
        + scale_two * weighted
        - h * (scale_two * scale_two * scale_two) * jnp.mean(weighted * h, axis=1, keepdims=True)
    )
    dbranch = (RESIDUAL * input_out[...]).astype(low)
    drouter = mul(xtwo_in[...], dlogits, TN)
    for lo in range(0, width, 256):
        grads_o[lo:lo + 256] = mul(dbranch[:, lo:lo + 256], mixed_in[...], TN).astype(low)
    dense_start(0)

    loads[1].wait()
    half_lane = lax.broadcasted_iota(jnp.int32, (block, 128), 1) < 64
    for head in range(8):
        both = mul(dbranch, w_qo[:, 1024 + 128 * head:1152 + 128 * head], NN)
        for t in range(2):
            value = both[block * t:block * (t + 1)]
            other = pltpu.roll(value, 64, 1)
            if head % 2 == 0:
                first, second = jnp.where(half_lane, value, 0.0), jnp.where(half_lane, other, 0.0)
            else:
                first, second = jnp.where(half_lane, 0.0, other), jnp.where(half_lane, 0.0, value)
            outs[t * 8 + head, :block] = first.astype(low)
            outs[t * 8 + head, block:] = second.astype(low)

    dense_cores(0)

    def kd_copy(hop, t):
        return remote(kv.at[hop * 2 + (1 - core), t], dkv_core.at[hop, t], kd_send.at[hop, t], kd_recv.at[hop, t], sibling)

    def k_copy(hop, t):
        return remote(kv.at[hop * 2 + core, t], dkv_deep.at[hop - 1, t], k_send.at[hop, t], k_recv.at[hop, t], (row, seq - 2))

    def k_start(t):
        for hop in range(back, -1, -1):
            @pl.when(deep >= hop)
            def _():
                kd_copy(hop, t).start()

    def k_sum(hop, t):
        @pl.when(deep >= hop)
        def _():
            kd_copy(hop, t).wait_recv()
            kv[hop * 2 + core, t] = (kv[hop * 2 + core, t].astype(full) + dkv_core[hop, t].astype(full)).astype(low)
            if hop < back:
                @pl.when(deep + 1 < n_deep)
                def _():
                    k_copy(hop + 1, t).wait_recv()
                    kv[hop * 2 + core, t] = (kv[hop * 2 + core, t].astype(full) + dkv_deep[hop, t].astype(full)).astype(low)

            k_copy(hop, t).start()

    lane = lax.broadcasted_iota(jnp.int32, (tokens, 128), 1)
    for copy in loads[2:]:
        copy.wait()
    places = window_slots(core, slots)
    kv[jnp.where(core == 0, 1, 2 * back)] = jnp.zeros(kv.shape[1:], low)
    for t in range(2):
        visible = visibility(seq, slots, block, start_in[block * t:block * (t + 1)])

        def attend(pair, carry):
            lanes = pl.ds(pl.multiple_of(128 * pair, 128), 128)
            value_lanes = pl.ds(pl.multiple_of(512 + 128 * pair, 128), 128)
            keys = jnp.concatenate([kv[slot, t, :, lanes] for slot in places], axis=0)
            values = jnp.concatenate([kv[slot, t, :, value_lanes] for slot in places], axis=0)
            dk, dv = 0.0, 0.0
            for half in range(2):
                head = 2 * pair + half
                query, dout = queries[t * 8 + head], outs[t * 8 + head]
                scores = jnp.where(visible, SCORE_SCALE * mul(query, keys, NT), NEGATIVE)
                total_log = jnp.sum(jnp.where(lane == head, lse_in[t], 0.0), axis=1, keepdims=True)
                probs = jnp.exp(scores - total_log)
                dprobs = mul(dout, values, NT)
                inner = jnp.sum(probs * dprobs, axis=1, keepdims=True)
                dscores = (probs * (dprobs - inner)).astype(low)
                dquery = SCORE_SCALE * mul(dscores, keys, NN)
                if half == 0:
                    joined = jnp.where(half_lane, dquery[:block], pltpu.roll(dquery[block:], 64, 1))
                else:
                    joined = jnp.where(half_lane, pltpu.roll(dquery[:block], 64, 1), dquery[block:])
                dq[block * t:block * (t + 1), pl.ds(pl.multiple_of(128 * head, 128), 128)] = joined
                dk += SCORE_SCALE * mul(dscores, query, TN)
                dv += mul(probs.astype(low), dout, TN)
            for d, slot in enumerate(places[1:], 1):
                kv[slot, t, :, lanes] = dk[block * d:block * (d + 1)].astype(low)
                kv[slot, t, :, value_lanes] = dv[block * d:block * (d + 1)].astype(low)
            dkv_own[t, :, lanes] = dk[:block]
            dkv_own[t, :, value_lanes] = dv[:block]
            return carry

        lax.fori_loop(0, 4, attend, 0)
        k_start(t)
        if t == 0:
            dense_plane(0)
            k_sum(back, 0)


    for hop in range(back - 1, 0, -1):
        k_sum(hop, 0)
    k_sum(back, 1)
    cosine, sine = cos_in[...], sin_in[...]

    def turn_back(value):
        return value * cosine - jnp.where(lane % 64 < 32, pltpu.roll(value, 96, 1), pltpu.roll(value, 32, 1)) * sine

    for head in range(8):
        lanes = slice(128 * head, 128 * (head + 1))
        dqkv[:, lanes] = turn_back(dq[:, lanes]).astype(low)
    for lo in range(0, width, 256):
        grads_q[lo:lo + 256] = mul(normed_in[:, lo:lo + 256], dqkv[:, :1024], TN).astype(low)
    dense_start(1)
    for hop in range(back - 1, 0, -1):
        k_sum(hop, 1)

    for lo in range(0, width, 256):
        part_q = slice(lo, lo + 256)
        dq[:, part_q] = mul(dqkv[:, :1024], w_qo[part_q, :1024], NT)
    dense_cores(1)
    experts_start(total * 5 // 8, total)
    for t in range(2):
        kd_copy(0, t).wait_recv()
        dkv_own[t] += dkv_core[0, t].astype(full)

        @pl.when(deep + 1 < n_deep)
        def _():
            k_copy(1, t).wait_recv()
            dkv_own[t] += dkv_deep[0, t].astype(full)

    for pair in range(4):
        lanes = slice(128 * pair, 128 * (pair + 1))
        value_lanes = slice(512 + 128 * pair, 640 + 128 * pair)
        dkey = jnp.concatenate([dkv_own[0, :, lanes], dkv_own[1, :, lanes]], axis=0)
        dqkv[:, 1024 + 128 * pair:1152 + 128 * pair] = turn_back(dkey).astype(low)
        dvalue = jnp.concatenate([dkv_own[0, :, value_lanes], dkv_own[1, :, value_lanes]], axis=0)
        dqkv[:, 1536 + 128 * pair:1664 + 128 * pair] = dvalue.astype(low)
    for lo in range(0, width, 256):
        grads_k[lo:lo + 256, :1024] = mul(normed_in[:, lo:lo + 256], dqkv[:, 1024:], TN).astype(low)
    x = x_in[...].astype(full)
    scale_one = norm_scale(x)
    for lo in range(0, width, 256):
        part_k = slice(lo, lo + 256)
        dq[:, part_k] += mul(dqkv[:, 1024:], w_kv[part_k, :1024], NT)
    dxone = dq[...]
    weighted = gain_one * dxone
    dgain_one = jnp.sum(dxone * x * scale_one, axis=0, keepdims=True)
    wide = lax.broadcasted_iota(jnp.int32, (width, 128), 1)
    grads_k[:, 1024:] = jnp.where(
        wide == 16, column(dgain_one), jnp.where(wide == 17, column(dgain_two), drouter)
    ).astype(low)
    dense_start(2)
    dense_plane(1)
    input_out[...] = (
        input_out[...]
        + scale_one * weighted
        - x * (scale_one * scale_one * scale_one) * jnp.mean(weighted * x, axis=1, keepdims=True)
    )
    dense_cores(2)
    dense_plane(2)
    o_out[...] = dense_end(0)
    q_out[...] = dense_end(1)
    last = dense_end(2)
    k_out[...] = last[:, :512]
    v_out[...] = last[:, 512:1024]
    spread_out[:rows] = last[:, 1024:]
    small_out[...] = spread_out[...].T
    for kind in range(3):
        def settle_d(index, carry):
            hop, step = index // 4, index % 4
            d_copy(kind, step, hop).wait_send()

            @pl.when(step > 0)
            def _():
                p_copy(kind, step, hop).wait_send()

            return carry

        lax.fori_loop(0, 4 * n_deep, settle_d, 0)

        def settle_z(hop, carry):
            z_copy(kind, hop).wait_send()
            return carry

        lax.fori_loop(1, n_deep, settle_z, 0)

    for hop in range(back + 1):
        for t in range(2):
            @pl.when(deep >= hop)
            def _():
                kd_copy(hop, t).wait_send()
                if hop > 0:
                    k_copy(hop, t).wait_send()

    expert_own.wait()

    def settle_experts(step, carry):
        other = (me + total - step) % total
        expert_copy(step).wait_send()
        there = held.at[other % n_seq // 4, other // n_seq * 4 + other % 4]
        remote(there, there, e_send.at[step], e_recv.at[step], sibling).wait_recv()
        return carry

    lax.fori_loop(1, total, settle_experts, 0)


def window_of(length, block, n_deep):
    back = length // 2 // (2 * block)
    assert back * 4 * block == length and 0 < back < n_deep
    return back


def run_backward(n_row, n_seq, length, w_kv, w_qo, kv, queries, normed, mixed, x, g, cosine, sine, start,
                 hidden, xtwo, gates, dgates, dx, lse, expert_grads):
    tokens, width = x.shape
    total, n_deep = n_row * n_seq, n_seq // 2
    rows, block = width // total, tokens // 2
    back = window_of(length, block, n_deep)
    columns = (1024, 1024, w_kv.shape[1])
    low, full = jnp.bfloat16, jnp.float32
    dma, shape = pltpu.SemaphoreType.DMA, jax.ShapeDtypeStruct
    return pl.pallas_call(
        functools.partial(backward_kernel, n_row, n_seq, back),
        out_shape=(
            shape((tokens, width), full),
            shape((rows, 1024), full),
            shape((rows, 512), full),
            shape((rows, 512), full),
            shape((rows, 1024), full),
            shape((128, 128), full),
            shape((n_seq // 4, n_row * 4, rows, expert_grads.shape[1]), low),
        ),
        in_specs=[ANY] * 4 + [VMEM] * 13 + [ANY],
        out_specs=(VMEM,) * 6 + (ANY,),
        scratch_shapes=[
            pltpu.VMEM(w_kv.shape, low),
            pltpu.VMEM(w_qo.shape, low),
            pltpu.VMEM(kv.shape, low),
            pltpu.VMEM((16, tokens, 128), low),
            pltpu.VMEM((16, tokens, 128), low),
            pltpu.VMEM((tokens, 1024), full),
            pltpu.VMEM((tokens, 2048), low),
            pltpu.VMEM(kv.shape[1:], full),
            pltpu.VMEM((back + 1,) + kv.shape[1:], low),
            pltpu.VMEM((back,) + kv.shape[1:], low),
        ]
        + [pltpu.VMEM((width, c), low) for c in columns]
        + [pltpu.VMEM((n_deep, 4, rows, c), low) for c in columns]
        + [pltpu.VMEM((n_deep, 3, rows, c), low) for c in columns]
        + [pltpu.VMEM((n_deep, rows, c), low) for c in columns]
        + [
            pltpu.VMEM((128, 128), full),
            dma((4,)),
            dma((back + 1, 2)), dma((back + 1, 2)), dma((back + 1, 2)), dma((back + 1, 2)),
            dma((total,)), dma((total,)), dma,
            dma((3, n_deep, 4)), dma((3, n_deep, 4)), dma((3, n_deep, 4)), dma((3, n_deep, 4)),
            dma((3, n_deep)), dma((3, n_deep)),
        ],
        compiler_params=pltpu.CompilerParams(
            collective_id=2, has_side_effects=True, vmem_limit_bytes=62 << 20
        ),
        name="backward",
    )(w_kv, w_qo, kv, queries, normed, mixed, x, g, cosine, sine, start, hidden, xtwo, gates, dgates, dx, lse,
      expert_grads)


def results_kernel(
    held, counts, small, *refs
):
    passed, copied = refs[:6], refs[6:12]
    gate_out, up_out, down_out, router_out, one_out, two_out, counts_out = refs[12:]
    ff = gate_out.shape[2]
    rows = router_out.shape[1]
    for source, target in zip(passed[:2], copied[:2]):
        target[...] = source[...]

    @pl.when(pl.program_id(0) == 0)
    def _():
        for source, target in zip(passed[2:], copied[2:]):
            target[...] = source[...]
        router_out[...] = small[:EXPERTS, :rows]
        one_out[...] = small[EXPERTS:EXPERTS + 1, :rows]
        two_out[...] = small[EXPERTS + 1:EXPERTS + 2, :rows]
        counts_out[...] = pltpu.roll(counts[...], 96, 1)[:1].astype(jnp.int32)

    for out, lo in ((gate_out, 0), (up_out, ff), (down_out, 2 * ff)):
        value = held[0, :, :, lo:lo + ff].astype(jnp.float32)
        for group in range(1, held.shape[0]):
            value += held[group, :, :, lo:lo + ff].astype(jnp.float32)
        out[...] = value


def run_results(held, counts, small, *passed):
    groups, experts, rows, wide = held.shape
    ff, full = wide // 3, jnp.float32
    some = experts // 4
    shape = jax.ShapeDtypeStruct
    whole = lambda i: (0, 0)
    moved = [pl.BlockSpec((a.shape[0] // 4, a.shape[1]), lambda i: (i, 0)) for a in passed[:2]]
    moved += [pl.BlockSpec(a.shape, whole) for a in passed[2:]]
    return pl.pallas_call(
        results_kernel,
        grid=(4,),
        out_shape=tuple(shape(a.shape, a.dtype) for a in passed) + (
            shape((experts, rows, ff), full),
            shape((experts, rows, ff), full),
            shape((experts, rows, ff), full),
            shape((EXPERTS, rows), full),
            shape((1, rows), full),
            shape((1, rows), full),
            shape((1, 128), jnp.int32),
        ),
        in_specs=[
            pl.BlockSpec((groups, some, rows, wide), lambda i: (0, i, 0, 0)),
            pl.BlockSpec((8, 128), whole),
            pl.BlockSpec((128, 128), whole),
        ] + moved,
        out_specs=tuple(moved) + (pl.BlockSpec((some, rows, ff), lambda i: (i, 0, 0)),) * 3 + (
            pl.BlockSpec((EXPERTS, rows), whole),
            pl.BlockSpec((1, rows), whole),
            pl.BlockSpec((1, rows), whole),
            pl.BlockSpec((1, 128), whole),
        ),
        name="results",
    )(held, counts, small, *passed)


def body(
    n_row,
    n_seq,
    tokens,
    segment_ids,
    expert_ids,
    norm1_gain,
    w_query,
    w_key,
    w_value,
    w_out,
    norm2_gain,
    w_router,
    w_gate,
    w_up,
    w_down,
    out_grad,
):
    row_count, block_len, width = tokens.shape
    token_count = row_count * block_len
    length = segment_ids.shape[1]
    rows = w_query.shape[0]
    full = jnp.float32
    small = jnp.concatenate([w_router.T, norm1_gain[None], norm2_gain[None], jnp.zeros((14, rows), norm1_gain.dtype)])
    lanes = np.arange(128) % HEAD
    half = HEAD // 2
    frequency = (THETA ** (-2.0 * (lanes % half) / HEAD)).astype(np.float32)
    turns = np.zeros((8, 128), np.float32)
    turns[0], turns[1] = frequency, np.where(lanes < half, -1.0, 1.0)
    x = tokens.reshape(token_count, width)
    g = out_grad.reshape(token_count, width)
    (cosine, sine, start, xtwo, gates, counts, hidden, mixed, lse, normed, queries, kv, w_kv, w_qo,
     group_g, group_x, group_gates, expert_weights) = run_forward(
        n_row, n_seq, length, w_key, w_value, w_query, w_out.T, small.astype(full), jnp.asarray(turns), segment_ids,
        jnp.swapaxes(expert_ids[0], 1, 2), x, g, w_gate, w_up, jnp.swapaxes(w_down, 1, 2)
    )
    layer_out, dx, dgates, expert_grads = run_experts(
        n_row, n_seq, group_x, group_g, group_gates, expert_weights, hidden
    )
    input_grad, dq, dk, dv, do, small, held = run_backward(
        n_row, n_seq, length, w_kv, w_qo, kv, queries, normed, mixed, x, g, cosine, sine, start,
        hidden, xtwo, gates, dgates, dx, lse, expert_grads,
    )
    layer_out, input_grad, dq, dk, dv, do, d_gate, d_up, d_down, router, one, two, counts = run_results(
        held, counts, small, layer_out, input_grad, dq, dk, dv, do
    )
    return (
        layer_out.reshape(row_count, block_len, width),
        input_grad.reshape(row_count, block_len, width),
        one[0],
        dq,
        dk,
        dv,
        do.T,
        two[0],
        router.T,
        d_gate,
        d_up,
        jnp.swapaxes(d_down, 1, 2),
        counts[0, :EXPERTS],
    )


def solution(mesh):
    in_specs = (
        P("row", "seq", None),
        P("row", None),
        P("seq", "row", None, None),
        P(("row", "seq")),
        P(("row", "seq"), None),
        P(("row", "seq"), None),
        P(("row", "seq"), None),
        P(None, ("row", "seq")),
        P(("row", "seq")),
        P(("row", "seq"), None),
        P(None, ("row", "seq"), None),
        P(None, ("row", "seq"), None),
        P(None, None, ("row", "seq")),
        P("row", "seq", None),
    )
    out_specs = (
        P("row", "seq", None),
        P("row", "seq", None),
        P(("row", "seq")),
        P(("row", "seq"), None),
        P(("row", "seq"), None),
        P(("row", "seq"), None),
        P(None, ("row", "seq")),
        P(("row", "seq")),
        P(("row", "seq"), None),
        P(None, ("row", "seq"), None),
        P(None, ("row", "seq"), None),
        P(None, None, ("row", "seq")),
        P(),
    )
    return jax.shard_map(
        functools.partial(body, mesh.shape["row"], mesh.shape["seq"]),
        mesh=mesh,
        in_specs=in_specs,
        out_specs=out_specs,
        check_vma=False,
    )
```

```python
import functools

import jax
import jax.numpy as jnp
import numpy as np
from jax import lax
from jax.experimental import pallas as pl
from jax.experimental.pallas import tpu as pltpu
from jax.sharding import PartitionSpec as P

HEAD = 64
EXPERTS = 16
TOPK = 8

EPSILON = 1e-06
SCORE_SCALE = 0.015625
RESIDUAL = 0.22
THETA = 10000.0
NEGATIVE = -1e30

MESH = pl.DeviceIdType.MESH
STRIDE = 11
ANY = pl.BlockSpec(memory_space=pl.ANY)
VMEM = pl.BlockSpec(memory_space=pltpu.VMEM)


def norm_scale(value):
    return lax.rsqrt(jnp.mean(value * value, axis=-1, keepdims=True) + EPSILON)


def greet_all(n_row, n_seq, wait=True):
    row, seq = lax.axis_index("row"), lax.axis_index("seq")
    me, total = row * n_seq + seq, n_row * n_seq
    barrier = pltpu.get_barrier_semaphore()

    def greet(step, carry):
        other = (me + step) % total
        pl.semaphore_signal(
            barrier, inc=1, device_id=(other // n_seq, other % n_seq), device_id_type=MESH
        )
        return carry

    lax.fori_loop(1, total, greet, 0)
    if wait:
        pl.semaphore_wait(barrier, total - 1)


NN = (((1,), (0,)), ((), ()))
NT = (((1,), (1,)), ((), ()))
TN = (((0,), (0,)), ((), ()))


def mul(a, b, dims):
    return lax.dot_general(a, b, dims, preferred_element_type=jnp.float32)


def column(row_values):
    return jnp.broadcast_to(row_values, (128, row_values.shape[1])).T


def peer_of(row, seq, step):
    other_row = (row // 2 + step // 4) % 2 * 2 + (row % 2 + step // 2 % 2) % 2
    other_seq = seq // 4 * 4 + (seq // 2 % 2 + step % 2) % 2 * 2 + seq % 2
    return (other_row, other_seq)


def row_of(row, step):
    return (row // 2 + step // 2) % 2 * 2 + (row % 2 + step % 2) % 2


def remote(source, target, send, recv, device):
    return pltpu.make_async_remote_copy(
        src_ref=source, dst_ref=target, send_sem=send, recv_sem=recv, device_id=device,
        device_id_type=MESH,
    )


def thirds_of(rows):
    cut = rows * 3 // 8
    rest = (rows - cut) // 2
    return ((0, cut), (cut, rest), (cut + rest, rest))


def tree_rounds(row, seq, own, slots, send, recv):
    thirds = thirds_of(own.shape[0])

    def hop(source, slot, toward, index):
        return remote(source, slot, send.at[index], recv.at[index], peer_of(row, seq, toward))

    def piece(slot, third):
        return slots.at[slot, pl.ds(*thirds[third])]

    first = lambda i: hop(own, slots.at[(1, 2, 4)[i]], (1, 2, 4)[i], i)
    second = lambda i: hop(slots.at[(2, 4, 1)[i]], slots.at[(3, 6, 5)[i]], (1, 2, 4)[i], 3 + i)
    third = lambda i: hop(piece((6, 5, 3)[i], i), piece(7, i), (1, 2, 4)[i], 6 + i)

    def start(make):
        for i in range(3):
            make(i).start()

    def landed(make):
        for i in range(3):
            make(i).wait_recv()

    def round_one():
        start(first)

    def round_two():
        landed(first)
        start(second)

    def round_three():
        landed(second)
        start(third)

    def last():
        landed(third)

    def sent():
        for make in (first, second, third):
            for i in range(3):
                make(i).wait_send()

    return round_one, round_two, round_three, last, sent


def forward_kernel(
    n_row, n_seq, back,
    key_in, value_in, query_in, out_in, small_in, turns_in, segments_in, ids_in, x_in, g_in, gate, up, down,
    cos_in, sin_in, start_in, xtwo_out, gates_out, counts_out, hidden_out, mixed_out, lse_out, normed_out, queries_out, kv_out,
    w_kv_out, w_qo_out, g_out, xs_out, gates_all, held,
    pack_kv, pack_qo, upright, picks_in, w_kv, w_qo, kv, queries, normed, mixed, hidden, lse,
    z_send, z_recv, p_send, p_recv, d_send, d_recv, kv_send, kv_recv, kvd_send, kvd_recv,
    g_send, g_recv, x_send, x_recv, gate_send, gate_recv, group_local, e_send, e_recv, e_local, pass_send, pass_recv, local, store,
):
    row, seq = lax.axis_index("row"), lax.axis_index("seq")
    core, deep, n_deep = seq % 2, seq // 2, n_seq // 2
    me, total = row * n_seq + seq, n_row * n_seq
    sibling = (row, deep * 2 + (1 - core))
    rows = key_in.shape[0]
    tokens, width = x_in.shape
    block = tokens // 2
    low, full = jnp.bfloat16, jnp.float32
    slots = kv.shape[0]
    packs, walls = (pack_kv, pack_qo), (w_kv, w_qo)
    greet_all(n_row, n_seq, False)

    sublane = lax.broadcasted_iota(jnp.int32, (128, 128), 0)
    for t in range(2):
        chosen = jnp.zeros((128, block), full)
        for choice in range(TOPK):
            chosen += jnp.where(ids_in[t, choice:choice + 1] == sublane, 1.0, 0.0)
        picks_in[block * t:block * (t + 1)] = chosen.T
    count = jnp.broadcast_to(jnp.sum(picks_in[...], axis=0, keepdims=True), (8, 128))
    upright[...] = jnp.zeros_like(upright)
    upright[:small_in.shape[0], :rows] = small_in[...]
    small = upright[...].T[:rows]
    counts = jnp.where(sublane[:rows] == 0, pltpu.roll(count, 32, 1)[:1], 0.0)
    pack_kv[:, :512] = key_in[...]
    pack_kv[:, 512:1024] = value_in[...]
    pack_kv[:, 1024:] = (small + counts).astype(low)
    pack_qo[:, :1024] = query_in[...]
    pack_qo[:, 1024:] = out_in[...]
    pl.semaphore_wait(pltpu.get_barrier_semaphore(), total - 1)

    def part(kind, of_row, of_deep, of_core):
        start = (of_row * n_seq + of_deep * 2 + of_core) * rows
        return walls[kind].at[pl.ds(pl.multiple_of(start, rows), rows)]

    own_copies = [
        pltpu.make_async_copy(packs[kind], part(kind, row, deep, core), local.at[kind]) for kind in range(2)
    ]
    for copy in own_copies:
        copy.start()

    def z_copy(kind, step):
        return remote(packs[kind], part(kind, row, deep, core), z_send.at[kind, step], z_recv.at[kind, step],
                      (row, (deep + step) % n_deep * 2 + core))

    def plane_copy(kind, step, hop, source):
        here = part(kind, row, (deep + n_deep - hop) % n_deep, core)
        return remote(here if source is None else source, here, p_send.at[kind, hop, step], p_recv.at[kind, hop, step],
                      (row_of(row, step), seq))

    def corner_copy(kind, step, hop):
        here = part(kind, row_of(row, step), (deep + n_deep - hop) % n_deep, core)
        return remote(here, here, p_send.at[kind, hop, 3], p_recv.at[kind, hop, 3], (row_of(row, 3 - step), seq))

    def core_copy(kind, step, hop, source):
        here = part(kind, row_of(row, step), (deep + n_deep - hop) % n_deep, core)
        return remote(here if source is None else source, here, d_send.at[kind, hop, step], d_recv.at[kind, hop, step],
                      sibling)

    def dense_start(kind):
        def start_z(step, carry):
            z_copy(kind, step).start()
            return carry

        lax.fori_loop(1, n_deep, start_z, 0)
        for step in range(1, 3):
            plane_copy(kind, step, 0, packs[kind]).start()
        core_copy(kind, 0, 0, packs[kind]).start()

    def dense_relay(kind):
        def relay(hop, carry):
            there = part(kind, row, (deep + n_deep - hop) % n_deep, core)
            remote(there, there, z_send.at[kind, hop], z_recv.at[kind, hop], sibling).wait_recv()
            for step in range(1, 3):
                plane_copy(kind, step, hop, None).start()
            core_copy(kind, 0, hop, None).start()
            return carry

        lax.fori_loop(1, n_deep, relay, 0)

    def dense_finish(kind):
        def landed(hop, step):
            there = part(kind, row_of(row, step), (deep + n_deep - hop) % n_deep, core)
            remote(there, there, p_send.at[kind, hop, step], p_recv.at[kind, hop, step], sibling).wait_recv()
            core_copy(kind, step, hop, None).start()

        def spread(hop, carry):
            for step in range(1, 3):
                landed(hop, step)

                @pl.when(hop % 2 == step - 1)
                def _():
                    corner_copy(kind, step, hop).start()

            return carry

        lax.fori_loop(0, n_deep, spread, 0)

        def corner(hop, carry):
            landed(hop, 3)
            return carry

        lax.fori_loop(0, n_deep, corner, 0)
        own_copies[kind].wait()

        def gathered(index, carry):
            hop, step = index // 4, index % 4
            there = part(kind, row_of(row, step), (deep + n_deep - hop) % n_deep, 1 - core)
            remote(there, there, d_send.at[kind, hop, step], d_recv.at[kind, hop, step], sibling).wait_recv()
            return carry

        lax.fori_loop(0, n_deep * 4, gathered, 0)

    def expert_copy(kind, source, step):
        other = (me + step) % total
        other_row, other_seq = other // n_seq, other % n_seq
        return remote(
            source.at[other_row * 4 + other_seq % 4],
            held.at[other_seq % 2, kind, pl.ds(pl.multiple_of(me * rows, rows), rows)],
            e_send.at[kind, step], e_recv.at[kind, step], (other_row, other_seq),
        )

    sources = (gate, up, down)
    expert_own = [
        pltpu.make_async_copy(
            source.at[row * 4 + seq % 4],
            held.at[core, kind, pl.ds(pl.multiple_of(me * rows, rows), rows)],
            e_local.at[kind],
        )
        for kind, source in enumerate(sources)
    ]

    def experts_start(lo, hi):
        for kind in range(3):
            def start_experts(index, carry):
                expert_copy(kind, sources[kind], index * STRIDE % total).start()
                return carry

            lax.fori_loop(lo, hi, start_experts, 0)

    g_one, g_two, g_three, g_last, g_sent = tree_rounds(row, seq, g_in, g_out, g_send, g_recv)
    g_own = pltpu.make_async_copy(g_in, g_out.at[0], group_local.at[0])

    dense_start(0)
    dense_start(1)
    for copy in expert_own:
        copy.start()
    g_own.start()
    experts_start(1, total * 5 // 8)
    x = x_in[...].astype(full)
    scale_one = norm_scale(x)
    for t in range(2):
        own = segments_in[t:t + 1, pl.ds(pl.multiple_of(seq * block, block), block)].astype(full)
        own = column(own)
        smaller = jnp.zeros((block, 128), full)
        for lo in range(0, segments_in.shape[1], 128):
            smaller += jnp.where(segments_in[t:t + 1, lo:lo + 128].astype(full) < own, 1.0, 0.0)
        begin = jnp.broadcast_to(jnp.sum(smaller, axis=1, keepdims=True), (block, 128))
        start_in[block * t:block * (t + 1)] = begin.astype(jnp.int32)
        place = lax.broadcasted_iota(jnp.int32, (block, 128), 0) + seq * block
        angle = (place.astype(full) - begin) * turns_in[:1]
        cos_in[block * t:block * (t + 1)] = jnp.cos(angle)
        sin_in[block * t:block * (t + 1)] = jnp.sin(angle) * turns_in[1:2]

    dense_relay(0)
    dense_finish(0)
    small = w_kv[:, 1024:].astype(full)
    counts_out[...] = jnp.broadcast_to(jnp.sum(small, axis=0, keepdims=True), (8, 128))
    small = small.T
    gain_one, gain_two = small[16:17], small[17:18]
    normed[...] = (x * scale_one * gain_one).astype(low)

    lane = lax.broadcasted_iota(jnp.int32, (tokens, 128), 1)
    cosine, sine = cos_in[...], sin_in[...]

    def turn(value):
        return value * cosine + jnp.where(lane % 64 < 32, pltpu.roll(value, 96, 1), pltpu.roll(value, 32, 1)) * sine

    for pair in range(4):
        lanes = slice(128 * pair, 128 * (pair + 1))
        value_lanes = slice(512 + 128 * pair, 640 + 128 * pair)
        key = turn(mul(normed[...], w_kv[:, lanes], NN)).astype(low)
        value = mul(normed[...], w_kv[:, value_lanes], NN).astype(low)
        for t in range(2):
            here = slice(block * t, block * (t + 1))
            kv[core, t, :, lanes] = key[here]
            kv[core, t, :, value_lanes] = value[here]

    def kv_copy(hop):
        return remote(kv.at[(hop - 1) * 2 + core], kv.at[hop * 2 + core], kv_send.at[hop], kv_recv.at[hop],
                      (row, seq + 2))

    def kv_pass(hop, of_core):
        there = kv.at[hop * 2 + of_core]
        return remote(there, there, kvd_send.at[hop], kvd_recv.at[hop], sibling)

    @pl.when(deep + 1 < n_deep)
    def _():
        kv_copy(1).start()

    for hop in range(1, back + 1):
        @pl.when(deep < hop)
        def _():
            kv[2 * hop] = jnp.zeros(kv.shape[1:], low)
            kv[2 * hop + 1] = jnp.zeros(kv.shape[1:], low)

    kv_pass(0, core).start()
    dense_relay(1)
    g_one()
    dense_finish(1)
    g_two()
    half_lane = lax.broadcasted_iota(jnp.int32, (block, 128), 1) < 64
    for head in range(8):
        both = turn(mul(normed[...], w_qo[:, 128 * head:128 * (head + 1)], NN))
        for t in range(2):
            value = both[block * t:block * (t + 1)]
            other = pltpu.roll(value, 64, 1)
            if head % 2 == 0:
                first, second = jnp.where(half_lane, value, 0.0), jnp.where(half_lane, other, 0.0)
            else:
                first, second = jnp.where(half_lane, 0.0, other), jnp.where(half_lane, 0.0, value)
            queries[t * 8 + head, :block] = first.astype(low)
            queries[t * 8 + head, block:] = second.astype(low)

    for hop in range(1, back + 1):
        @pl.when(deep >= hop)
        def _():
            kv_copy(hop).wait_recv()
            if hop < back:
                @pl.when(deep + 1 < n_deep)
                def _():
                    kv_copy(hop + 1).start()

            kv_pass(hop, core).start()

        if hop == 1:
            experts_start(total * 5 // 8, total)

    kv_pass(0, 1 - core).wait_recv()
    for hop in range(1, back + 1):
        @pl.when(deep >= hop)
        def _():
            kv_pass(hop, 1 - core).wait_recv()

    g_three()
    places = window_slots(core, slots)
    for t in range(2):
        visible = visibility(seq, slots, block, start_in[block * t:block * (t + 1)])

        def attend(pair, carry):
            lanes = pl.ds(pl.multiple_of(128 * pair, 128), 128)
            value_lanes = pl.ds(pl.multiple_of(512 + 128 * pair, 128), 128)
            values = jnp.concatenate([kv[slot, t, :, value_lanes] for slot in places], axis=0)
            for half in range(2):
                head = 2 * pair + half
                query = queries[t * 8 + head]
                scores = jnp.concatenate(
                    [mul(query, kv[slot, t, :, lanes], NT) for slot in places], axis=1
                )
                scores = jnp.where(visible, SCORE_SCALE * scores, NEGATIVE)
                peak = jnp.max(scores, axis=1, keepdims=True)
                raised = jnp.exp(scores - peak)
                denominator = jnp.sum(raised, axis=1, keepdims=True)
                probs = (raised / denominator).astype(low)
                out = mul(probs, values, NN)
                if half == 0:
                    joined = jnp.where(half_lane, out[:block], pltpu.roll(out[block:], 64, 1))
                else:
                    joined = jnp.where(half_lane, pltpu.roll(out[:block], 64, 1), out[block:])
                mixed[block * t:block * (t + 1), pl.ds(pl.multiple_of(128 * head, 128), 128)] = joined.astype(low)
                lse[t] = jnp.where(lane == head, peak + jnp.log(denominator), lse[t])
            return carry

        lax.fori_loop(0, 4, attend, 0)

    for lo in range(0, width, 256):
        branch = mul(mixed[...], w_qo[lo:lo + 256, 1024:], NT)
        hidden[:, lo:lo + 256] = x_in[:, lo:lo + 256].astype(full) + RESIDUAL * branch
    scale_two = norm_scale(hidden[...])
    xtwo_out[...] = (hidden[...] * scale_two * gain_two).astype(low)
    x_one, x_two, x_three, x_last, x_sent = tree_rounds(row, seq, xtwo_out, xs_out, x_send, x_recv)
    x_one()
    logits = mul(xtwo_out[...], w_kv[:, 1024:], NN)
    picked = picks_in[...] > 0
    logits = jnp.where(picked, logits, NEGATIVE)
    raised = jnp.where(picked, jnp.exp(logits - jnp.max(logits, axis=1, keepdims=True)), 0.0)
    gates = raised / jnp.sum(raised, axis=1, keepdims=True)
    gates_out[...] = gates.T[:EXPERTS]

    def gate_copy(step):
        return remote(gates_out, gates_all.at[step], gate_send.at[step], gate_recv.at[step], peer_of(row, seq, step))

    def send_gates(step, carry):
        gate_copy(step).start()
        return carry

    lax.fori_loop(1, 8, send_gates, 0)
    group_own = [
        g_own,
        pltpu.make_async_copy(xtwo_out, xs_out.at[0], group_local.at[1]),
        pltpu.make_async_copy(gates_out, gates_all.at[0], group_local.at[2]),
    ]
    for copy in group_own[1:]:
        copy.start()

    stores = [
        pltpu.make_async_copy(source, target, store.at[i])
        for i, (source, target) in enumerate((
            (w_kv, w_kv_out), (w_qo, w_qo_out), (kv, kv_out), (queries, queries_out), (normed, normed_out),
            (mixed, mixed_out), (hidden, hidden_out), (lse, lse_out),
        ))
    ]
    for copy in stores:
        copy.start()

    def share(kind, of_core):
        there = held.at[of_core, kind]
        return remote(there, there, pass_send.at[kind], pass_recv.at[kind], sibling)

    for kind in range(3):
        def arrived(step, carry):
            other = (me + total - step) % total
            there = held.at[core, kind, pl.ds(pl.multiple_of(other * rows, rows), rows)]
            remote(there, there, e_send.at[kind, step], e_recv.at[kind, step], sibling).wait_recv()
            return carry

        lax.fori_loop(1, total, arrived, 0)
        expert_own[kind].wait()
        share(kind, core).start()

    def settle_experts(step, carry):
        for kind, source in enumerate(sources):
            expert_copy(kind, source, step).wait_send()
        return carry

    lax.fori_loop(1, total, settle_experts, 0)
    g_last()
    g_sent()
    x_two()
    x_three()
    x_last()
    x_sent()
    for copy in group_own:
        copy.wait()

    def settle_gates(step, carry):
        gate_copy(step).wait()
        return carry

    lax.fori_loop(1, 8, settle_gates, 0)
    for kind in range(2):
        def settle_z(step, carry):
            z_copy(kind, step).wait_send()
            return carry

        lax.fori_loop(1, n_deep, settle_z, 0)

        def settle_plane(index, carry):
            hop, step = index // 4, index % 4
            core_copy(kind, step, hop, None).wait_send()

            @pl.when((step > 0) & (step < 3))
            def _():
                plane_copy(kind, step, hop, None).wait_send()

            @pl.when((step > 0) & (step < 3) & (hop % 2 == step - 1))
            def _():
                corner_copy(kind, step, hop).wait_send()

            return carry

        lax.fori_loop(0, n_deep * 4, settle_plane, 0)

    kv_pass(0, core).wait_send()
    for hop in range(1, back + 1):
        @pl.when((deep + 1 < n_deep) & (deep >= hop - 1))
        def _():
            kv_copy(hop).wait_send()

        @pl.when(deep >= hop)
        def _():
            kv_pass(hop, core).wait_send()

    for copy in stores:
        copy.wait()
    for kind in range(3):
        share(kind, core).wait_send()
        share(kind, 1 - core).wait_recv()


def window_slots(core, slots):
    return [(d + 1 - core) // 2 * 2 + (core + d) % 2 for d in range(slots - 1)]


def visibility(seq, slots, block, start):
    key = lax.broadcasted_iota(jnp.int32, (block, block), 1)
    query = lax.broadcasted_iota(jnp.int32, (block, block), 0) + seq * block
    tiles = []
    for d in range(slots - 1):
        position = key + (seq - d) * block
        seen = jnp.where((position >= start) & (position <= query), 1.0, 0.0)
        tiles.append(jnp.concatenate([seen, seen], axis=0))
    return jnp.concatenate(tiles, axis=1) > 0.5


def run_forward(n_row, n_seq, length, key, value, query, out, small, turns, segments, ids, x, g, gate, up, down):
    tokens, width = x.shape
    experts, rows, hidden = gate.shape
    total, n_deep = n_row * n_seq, n_seq // 2
    block = tokens // 2
    back = window_of(length, block, n_deep)
    slots = 2 * (back + 1)
    low, full = jnp.bfloat16, jnp.float32
    dma = pltpu.SemaphoreType.DMA
    kv = (slots, 2, block, 1024)
    shape = jax.ShapeDtypeStruct
    return pl.pallas_call(
        functools.partial(forward_kernel, n_row, n_seq, back),
        out_shape=(
            shape((tokens, 128), full),
            shape((tokens, 128), full),
            shape((tokens, 128), jnp.int32),
            shape((tokens, width), low),
            shape((EXPERTS, tokens), full),
            shape((8, 128), full),
            shape((tokens, width), full),
            shape((tokens, 1024), low),
            shape((2, 2 * block, 128), full),
            shape((tokens, width), low),
            shape((16, 2 * block, 128), low),
            shape(kv, low),
            shape((width, 1152), low),
            shape((width, 2048), low),
            shape((8, tokens, width), low),
            shape((8, tokens, width), low),
            shape((8, EXPERTS, tokens), full),
            shape((2, 3, width, hidden), low),
        ),
        in_specs=[VMEM] * 9 + [ANY] * 4,
        out_specs=(VMEM,) * 6 + (ANY,) * 12,
        scratch_shapes=[
            pltpu.VMEM((rows, 1152), low),
            pltpu.VMEM((rows, 2048), low),
            pltpu.VMEM((128, 128), full),
            pltpu.VMEM((tokens, 128), full),
            pltpu.VMEM((width, 1152), low),
            pltpu.VMEM((width, 2048), low),
            pltpu.VMEM(kv, low),
            pltpu.VMEM((16, 2 * block, 128), low),
            pltpu.VMEM((tokens, width), low),
            pltpu.VMEM((tokens, 1024), low),
            pltpu.VMEM((tokens, width), full),
            pltpu.VMEM((2, 2 * block, 128), full),
            dma((2, n_deep)), dma((2, n_deep)),
            dma((2, n_deep, 4)), dma((2, n_deep, 4)),
            dma((2, n_deep, 4)), dma((2, n_deep, 4)),
            dma((back + 1,)), dma((back + 1,)),
            dma((back + 1,)), dma((back + 1,)),
            dma((9,)), dma((9,)), dma((9,)), dma((9,)), dma((8,)), dma((8,)), dma((3,)),
            dma((3, total)), dma((3, total)), dma((3,)),
            dma((3,)), dma((3,)), dma((2,)), dma((8,)),
        ],
        compiler_params=pltpu.CompilerParams(
            collective_id=1, has_side_effects=True, vmem_limit_bytes=60 << 20
        ),
        name="forward",
    )(key, value, query, out, small, turns, segments, ids, x, g, gate, up, down)


def experts_kernel(
    n_seq, xs_in, gs_in, gates_in, w_in, hidden_in, layer_out, dx_out, dg_out, grad_out,
    xs, gs, gates, w, acc, mids, far, thirds_got, second_got, last_got, dg_made, dg_got, half_made, half_got,
    t_send, t_recv, s_send, s_recv, l_send, l_recv, dg_send, dg_recv, load, half_send, half_recv, done_sem,
):
    row, seq = lax.axis_index("row"), lax.axis_index("seq")
    core, chip_z = seq % 2, seq // 2 % 2
    tokens, width = hidden_in.shape
    ff = w.shape[1] // 6
    mine = (row * 2 + chip_z) * 2
    low, full = jnp.bfloat16, jnp.float32
    sibling = (row, seq // 2 * 2 + (1 - core))
    thirds = thirds_of(tokens)
    columns = ((0, 0), (0, 1), (1, 0), (1, 1), (0, 2), (1, 2))
    loads = [
        pltpu.make_async_copy(w_in.at[j, kind], w.at[:, pl.ds(col * ff, ff)], load.at[col])
        for col, (j, kind) in enumerate(columns)
    ]
    loads.append(pltpu.make_async_copy(gates_in, gates, load.at[6]))
    loads += [
        pltpu.make_async_copy(source.at[7], target.at[7], load.at[7 + i])
        for i, (source, target) in enumerate(((xs_in, xs), (gs_in, gs)))
    ]
    others = [
        pltpu.make_async_copy(source.at[pl.ds(0, 7)], target.at[pl.ds(0, 7)], load.at[9 + i])
        for i, (source, target) in enumerate(((xs_in, xs), (gs_in, gs)))
    ]
    for copy in loads + others:
        copy.start()
    barrier = pltpu.get_barrier_semaphore()

    def greet(step, carry):
        pl.semaphore_signal(barrier, inc=1, device_id=peer_of(row, seq, step), device_id_type=MESH)
        return carry

    lax.fori_loop(1, 8, greet, 0)
    pl.semaphore_signal(barrier, inc=1, device_id=sibling, device_id_type=MESH)
    acc[...] = jnp.zeros_like(acc)
    pl.semaphore_wait(barrier, 8)
    for copy in loads:
        copy.wait()

    def dg_copy(step):
        return remote(dg_made.at[step], dg_got.at[step], dg_send.at[step], dg_recv.at[step], peer_of(row, seq, step))

    results = (xs, gs)

    def third_copy(i, which):
        rows = pl.ds(*thirds[i])
        return remote(far.at[which, 0, rows], thirds_got.at[which, rows], t_send.at[which, i], t_recv.at[which, i],
                      peer_of(row, seq, (1, 2, 4)[i]))

    def second_copy(i, which):
        return remote(far.at[which, 1 + i], second_got.at[which, i], s_send.at[which, i], s_recv.at[which, i],
                      peer_of(row, seq, (2, 4, 1)[i]))

    def last_copy(i, which):
        slot = (4, 1, 2)[i]
        return remote(results[which].at[slot], last_got.at[which, i], l_send.at[which, i], l_recv.at[which, i],
                      peer_of(row, seq, slot))

    def relay_third(i):
        for which in range(2):
            rows = pl.ds(*thirds[i])
            third_copy(i, which).wait_recv()
            far[which, 1 + i, rows] = (
                far[which, 1 + i, rows].astype(full) + thirds_got[which, rows].astype(full)
            ).astype(low)
            second_copy(i, which).start()

    def relay_second(i):
        for which in range(2):
            slot = (4, 1, 2)[i]
            second_copy(i, which).wait_recv()
            results[which][slot] = (
                results[which][slot].astype(full) + second_got[which, i].astype(full)
            ).astype(low)
            last_copy(i, which).start()

    def order(index):
        step = 7 - index + jnp.where(index == 3, -1, 0) + jnp.where(index == 4, 1, 0)
        return jnp.where(index == 5, 1, jnp.where(index == 6, 2, step))

    def weigh(step, kept):
        for lo in range(0, width, 256):
            part = slice(lo, lo + 256)
            acc[part, :4 * ff] += mul(xs[step, :, part], mids[kept, :, :4 * ff], TN)
            acc[part, 4 * ff:] += mul(gs[step, :, part], mids[kept, :, 4 * ff:], TN)

    def block(is_far, index, carry):
        step, kept = order(index), index if is_far else 4

        if is_far:
            @pl.when(index == 1)
            def _():
                for copy in others:
                    copy.wait()

        x, g = xs[step], gs[step]
        for j in range(2):
            gate = column(gates[step, pl.ds(mine + j, 1)])[:, :1]
            a = mul(x, w[:, 2 * j * ff:(2 * j + 1) * ff], NN)
            b = mul(x, w[:, (2 * j + 1) * ff:(2 * j + 2) * ff], NN)
            back = RESIDUAL * mul(g, w[:, (4 + j) * ff:(5 + j) * ff], NN)
            sigma = jax.nn.sigmoid(a)
            smooth = a * sigma
            inner = smooth * b
            dgate = jnp.sum(inner * back, axis=1, keepdims=True)
            back = gate * back
            mids[kept, :, (4 + j) * ff:(5 + j) * ff] = (gate * inner).astype(low)
            mids[kept, :, 2 * j * ff:(2 * j + 1) * ff] = (back * b * (sigma + smooth * (1.0 - sigma))).astype(low)
            mids[kept, :, (2 * j + 1) * ff:(2 * j + 2) * ff] = (back * smooth).astype(low)
            dg_made[step, j] = jnp.broadcast_to(dgate, (tokens, 128)).T[:8]
        if not is_far:
            weigh(step, kept)
        for lo in range(0, width, 256):
            part = slice(lo, lo + 256)
            y = mul(mids[kept, :, 4 * ff:], w[part, 4 * ff:], NT).astype(low)
            dx = mul(mids[kept, :, :4 * ff], w[part, :4 * ff], NT).astype(low)
            if is_far:
                far[0, index, :, part] = y
                far[1, index, :, part] = dx
            else:
                xs[step, :, part] = y
                gs[step, :, part] = dx

        @pl.when(index < 7)
        def _():
            dg_copy(step).start()

        if is_far:
            @pl.when(index == 0)
            def _():
                for i in range(3):
                    for which in range(2):
                        third_copy(i, which).start()

            for i in range(3):
                @pl.when(index == 1 + i)
                def _():
                    relay_third(i)

        else:
            for i in range(3):
                @pl.when(index == (6, 7, 7)[i])
                def _():
                    relay_second(i)

        return carry

    lax.fori_loop(0, 4, functools.partial(block, True), 0)
    lax.fori_loop(4, 8, functools.partial(block, False), 0)

    def weigh_far(index, carry):
        weigh(order(index), index)
        return carry

    lax.fori_loop(0, 4, weigh_far, 0)

    def share_of(j):
        wide = acc[:, pl.ds(pl.multiple_of(j * 2 * ff, 128), 2 * ff)]
        thin = RESIDUAL * acc[:, pl.ds(pl.multiple_of((4 + j) * ff, 128), ff)]
        return wide, thin

    wide, thin = share_of(1 - core)
    half_made[:, :2 * ff] = wide.astype(low)
    half_made[:, 2 * ff:] = thin.astype(low)
    half = remote(half_made, half_got, half_send, half_recv, sibling)
    half.start()
    dg_got[0] = dg_made[0]
    half.wait_recv()
    wide, thin = share_of(core)
    half_got[:, :2 * ff] = (wide + half_got[:, :2 * ff].astype(full)).astype(low)
    half_got[:, 2 * ff:] = (thin + half_got[:, 2 * ff:].astype(full)).astype(low)
    store = pltpu.make_async_copy(half_got, grad_out, done_sem)
    store.start()

    def settle(step, carry):
        dg_copy(step).wait()
        return carry

    lax.fori_loop(1, 8, settle, 0)

    def place(step, carry):
        other_row, other_seq = peer_of(row, seq, step)
        chip = other_row * 2 + other_seq // 2 % 2
        for j in range(2):
            dg_out[pl.ds(chip * 2 + j, 1)] = dg_got[step, j, :1]
        return carry

    lax.fori_loop(0, 8, place, 0)
    for i in range(3):
        for which in range(2):
            last_copy(i, which).wait_recv()
    dx_out[...] = gs[0].astype(full) + sum(last_got[1, i].astype(full) for i in range(3))
    mixture = xs[0].astype(full) + sum(last_got[0, i].astype(full) for i in range(3))
    layer_out[...] = (hidden_in[...] + RESIDUAL * mixture).astype(low)
    for i in range(3):
        for which in range(2):
            third_copy(i, which).wait_send()
            second_copy(i, which).wait_send()
            last_copy(i, which).wait_send()
    half.wait_send()
    store.wait()


def run_experts(n_row, n_seq, xs, gs, gates, w, hidden):
    _, tokens, width = xs.shape
    ff = w.shape[3]
    low, full = jnp.bfloat16, jnp.float32
    dma, shape = pltpu.SemaphoreType.DMA, jax.ShapeDtypeStruct
    return pl.pallas_call(
        functools.partial(experts_kernel, n_seq),
        out_shape=(
            shape((tokens, width), low),
            shape((tokens, width), full),
            shape((EXPERTS, tokens), full),
            shape((width, 3 * ff), low),
        ),
        in_specs=[ANY, ANY, ANY, ANY, VMEM],
        out_specs=(VMEM, VMEM, VMEM, ANY),
        scratch_shapes=[
            pltpu.VMEM((8, tokens, width), low),
            pltpu.VMEM((8, tokens, width), low),
            pltpu.VMEM((8, EXPERTS, tokens), full),
            pltpu.VMEM((width, 6 * ff), low),
            pltpu.VMEM((width, 6 * ff), full),
            pltpu.VMEM((5, tokens, 6 * ff), low),
            pltpu.VMEM((2, 4, tokens, width), low),
            pltpu.VMEM((2, tokens, width), low),
            pltpu.VMEM((2, 3, tokens, width), low),
            pltpu.VMEM((2, 3, tokens, width), low),
            pltpu.VMEM((8, 2, 8, tokens), full),
            pltpu.VMEM((8, 2, 8, tokens), full),
            pltpu.VMEM((width, 3 * ff), low),
            pltpu.VMEM((width, 3 * ff), low),
            dma((2, 3)), dma((2, 3)), dma((2, 3)), dma((2, 3)), dma((2, 3)), dma((2, 3)),
            dma((8,)), dma((8,)), dma((11,)),
            dma, dma, dma,
        ],
        compiler_params=pltpu.CompilerParams(
            collective_id=3, has_side_effects=True, vmem_limit_bytes=62 << 20
        ),
        name="experts",
    )(xs, gs, gates, w, hidden)


def backward_kernel(
    n_row, n_seq, back,
    w_kv_in, w_qo_in, kv_in, queries_in, normed_in, mixed_in, x_in, g_in, cos_in, sin_in, start_in,
    hidden_in, xtwo_in, gates_in, dgates_in, dx_in, lse_in, expert_grads,
    input_out, q_out, k_out, v_out, o_out, small_out, held,
    w_kv, w_qo, kv, queries, outs, dq, dqkv, dkv_own, dkv_core, dkv_deep,
    grads_o, grads_q, grads_k, core_o, core_q, core_k, plane_o, plane_q, plane_k, deep_o, deep_q, deep_k,
    spread_out, load, k_send, k_recv, kd_send, kd_recv, e_send, e_recv, e_local,
    d_send, d_recv, p_send, p_recv, z_send, z_recv,
):
    row, seq = lax.axis_index("row"), lax.axis_index("seq")
    core, deep, n_deep = seq % 2, seq // 2, n_seq // 2
    me, total = row * n_seq + seq, n_row * n_seq
    sibling = (row, deep * 2 + (1 - core))
    rows = q_out.shape[0]
    tokens, width = x_in.shape
    block = tokens // 2
    low, full = jnp.bfloat16, jnp.float32
    slots = kv.shape[0]
    loads = [
        pltpu.make_async_copy(source, target, load.at[i])
        for i, (source, target) in enumerate(((w_kv_in, w_kv), (w_qo_in, w_qo), (kv_in, kv), (queries_in, queries)))
    ]
    for copy in loads:
        copy.start()
    greet_all(n_row, n_seq)

    def expert_copy(step):
        other = (me + step) % total
        return remote(
            expert_grads.at[pl.ds(pl.multiple_of(other * rows, rows), rows)],
            held.at[seq // 4, row * 4 + seq % 4],
            e_send.at[step], e_recv.at[step], (other // n_seq, other % n_seq),
        )

    expert_own = pltpu.make_async_copy(
        expert_grads.at[pl.ds(pl.multiple_of(me * rows, rows), rows)],
        held.at[seq // 4, row * 4 + seq % 4], e_local,
    )
    expert_own.start()

    def experts_start(lo, hi):
        def start_experts(index, carry):
            expert_copy(index * STRIDE % total).start()
            return carry

        lax.fori_loop(lo, hi, start_experts, 0)

    experts_start(1, total * 5 // 8)
    loads[0].wait()

    made, from_core = (grads_o, grads_q, grads_k), (core_o, core_q, core_k)
    from_plane, from_deep = (plane_o, plane_q, plane_k), (deep_o, deep_q, deep_k)

    def part(of_row, of_deep, of_core):
        return pl.ds(pl.multiple_of((of_row * n_seq + of_deep * 2 + of_core) * rows, rows), rows)

    def d_copy(kind, step, hop):
        there = part(row_of(row, step), (deep + hop) % n_deep, 1 - core)
        return remote(made[kind].at[there], from_core[kind].at[hop, step], d_send.at[kind, hop, step],
                      d_recv.at[kind, hop, step], sibling)

    def p_copy(kind, step, hop):
        there = part(row_of(row, step), (deep + hop) % n_deep, core)
        return remote(made[kind].at[there], from_plane[kind].at[hop, step - 1], p_send.at[kind, hop, step],
                      p_recv.at[kind, hop, step], (row_of(row, step), seq))

    def z_copy(kind, hop):
        there = part(row, (deep + hop) % n_deep, core)
        return remote(made[kind].at[there], from_deep[kind].at[hop], z_send.at[kind, hop], z_recv.at[kind, hop],
                      (row, (deep + hop) % n_deep * 2 + core))

    def dense_start(kind):
        def start_d(index, carry):
            d_copy(kind, 3 - index % 4, n_deep - 1 - index // 4).start()
            return carry

        lax.fori_loop(0, 4 * n_deep, start_d, 0)

    def dense_cores(kind):
        def sum_cores(index, carry):
            step, hop = 3 - index % 4, n_deep - 1 - index // 4
            d_copy(kind, step, hop).wait_recv()
            there = part(row_of(row, step), (deep + hop) % n_deep, core)
            made[kind][there] = (made[kind][there].astype(full) + from_core[kind][hop, step].astype(full)).astype(low)

            @pl.when(step > 0)
            def _():
                p_copy(kind, step, hop).start()

            return carry

        lax.fori_loop(0, 4 * n_deep, sum_cores, 0)

    def dense_plane(kind):
        def sum_plane(index, carry):
            hop = n_deep - 1 - index
            there = part(row, (deep + hop) % n_deep, core)
            for step in range(1, 4):
                p_copy(kind, step, hop).wait_recv()
            value = made[kind][there].astype(full)
            for step in range(1, 4):
                value += from_plane[kind][hop, step - 1].astype(full)
            made[kind][there] = value.astype(low)

            @pl.when(hop > 0)
            def _():
                z_copy(kind, hop).start()

            return carry

        lax.fori_loop(0, n_deep, sum_plane, 0)

    def dense_end(kind):
        value = made[kind][part(row, deep, core)].astype(full)
        for hop in range(1, n_deep):
            z_copy(kind, hop).wait_recv()
            value += from_deep[kind][hop].astype(full)
        return value


    def upright(value):
        return jnp.concatenate([value, jnp.zeros((128 - value.shape[0], tokens), full)], axis=0).T

    small = w_kv[:, 1024:].astype(full).T
    gain_one, gain_two = small[16:17], small[17:18]
    gates, dgates = upright(gates_in[...]), upright(dgates_in[...])
    dlogits = (gates * (dgates - jnp.sum(gates * dgates, axis=1, keepdims=True))).astype(low)
    dxtwo = dx_in[...] + mul(dlogits, w_kv[:, 1024:], NT)
    h = hidden_in[...]
    scale_two = norm_scale(h)
    weighted = gain_two * dxtwo
    dgain_two = jnp.sum(dxtwo * h * scale_two, axis=0, keepdims=True)
    input_out[...] = (
        g_in[...].astype(full)
        + scale_two * weighted
        - h * (scale_two * scale_two * scale_two) * jnp.mean(weighted * h, axis=1, keepdims=True)
    )
    dbranch = (RESIDUAL * input_out[...]).astype(low)
    drouter = mul(xtwo_in[...], dlogits, TN)
    for lo in range(0, width, 256):
        grads_o[lo:lo + 256] = mul(dbranch[:, lo:lo + 256], mixed_in[...], TN).astype(low)
    dense_start(0)

    loads[1].wait()
    half_lane = lax.broadcasted_iota(jnp.int32, (block, 128), 1) < 64
    for head in range(8):
        both = mul(dbranch, w_qo[:, 1024 + 128 * head:1152 + 128 * head], NN)
        for t in range(2):
            value = both[block * t:block * (t + 1)]
            other = pltpu.roll(value, 64, 1)
            if head % 2 == 0:
                first, second = jnp.where(half_lane, value, 0.0), jnp.where(half_lane, other, 0.0)
            else:
                first, second = jnp.where(half_lane, 0.0, other), jnp.where(half_lane, 0.0, value)
            outs[t * 8 + head, :block] = first.astype(low)
            outs[t * 8 + head, block:] = second.astype(low)

    dense_cores(0)

    def kd_copy(hop, t):
        return remote(kv.at[hop * 2 + (1 - core), t], dkv_core.at[hop, t], kd_send.at[hop, t], kd_recv.at[hop, t], sibling)

    def k_copy(hop, t):
        return remote(kv.at[hop * 2 + core, t], dkv_deep.at[hop - 1, t], k_send.at[hop, t], k_recv.at[hop, t], (row, seq - 2))

    def k_start(t):
        for hop in range(back, -1, -1):
            @pl.when(deep >= hop)
            def _():
                kd_copy(hop, t).start()

    def k_sum(hop, t):
        @pl.when(deep >= hop)
        def _():
            kd_copy(hop, t).wait_recv()
            kv[hop * 2 + core, t] = (kv[hop * 2 + core, t].astype(full) + dkv_core[hop, t].astype(full)).astype(low)
            if hop < back:
                @pl.when(deep + 1 < n_deep)
                def _():
                    k_copy(hop + 1, t).wait_recv()
                    kv[hop * 2 + core, t] = (kv[hop * 2 + core, t].astype(full) + dkv_deep[hop, t].astype(full)).astype(low)

            k_copy(hop, t).start()

    lane = lax.broadcasted_iota(jnp.int32, (tokens, 128), 1)
    for copy in loads[2:]:
        copy.wait()
    places = window_slots(core, slots)
    kv[jnp.where(core == 0, 1, 2 * back)] = jnp.zeros(kv.shape[1:], low)
    for t in range(2):
        visible = visibility(seq, slots, block, start_in[block * t:block * (t + 1)])

        def attend(pair, carry):
            lanes = pl.ds(pl.multiple_of(128 * pair, 128), 128)
            value_lanes = pl.ds(pl.multiple_of(512 + 128 * pair, 128), 128)
            keys = jnp.concatenate([kv[slot, t, :, lanes] for slot in places], axis=0)
            values = jnp.concatenate([kv[slot, t, :, value_lanes] for slot in places], axis=0)
            dk, dv = 0.0, 0.0
            for half in range(2):
                head = 2 * pair + half
                query, dout = queries[t * 8 + head], outs[t * 8 + head]
                scores = jnp.where(visible, SCORE_SCALE * mul(query, keys, NT), NEGATIVE)
                total_log = jnp.sum(jnp.where(lane == head, lse_in[t], 0.0), axis=1, keepdims=True)
                probs = jnp.exp(scores - total_log)
                dprobs = mul(dout, values, NT)
                inner = jnp.sum(probs * dprobs, axis=1, keepdims=True)
                dscores = (probs * (dprobs - inner)).astype(low)
                dquery = SCORE_SCALE * mul(dscores, keys, NN)
                if half == 0:
                    joined = jnp.where(half_lane, dquery[:block], pltpu.roll(dquery[block:], 64, 1))
                else:
                    joined = jnp.where(half_lane, pltpu.roll(dquery[:block], 64, 1), dquery[block:])
                dq[block * t:block * (t + 1), pl.ds(pl.multiple_of(128 * head, 128), 128)] = joined
                dk += SCORE_SCALE * mul(dscores, query, TN)
                dv += mul(probs.astype(low), dout, TN)
            for d, slot in enumerate(places[1:], 1):
                kv[slot, t, :, lanes] = dk[block * d:block * (d + 1)].astype(low)
                kv[slot, t, :, value_lanes] = dv[block * d:block * (d + 1)].astype(low)
            dkv_own[t, :, lanes] = dk[:block]
            dkv_own[t, :, value_lanes] = dv[:block]
            return carry

        lax.fori_loop(0, 4, attend, 0)
        k_start(t)
        if t == 0:
            dense_plane(0)
            k_sum(back, 0)


    for hop in range(back - 1, 0, -1):
        k_sum(hop, 0)
    k_sum(back, 1)
    cosine, sine = cos_in[...], sin_in[...]

    def turn_back(value):
        return value * cosine - jnp.where(lane % 64 < 32, pltpu.roll(value, 96, 1), pltpu.roll(value, 32, 1)) * sine

    for head in range(8):
        lanes = slice(128 * head, 128 * (head + 1))
        dqkv[:, lanes] = turn_back(dq[:, lanes]).astype(low)
    for lo in range(0, width, 256):
        grads_q[lo:lo + 256] = mul(normed_in[:, lo:lo + 256], dqkv[:, :1024], TN).astype(low)
    dense_start(1)
    for hop in range(back - 1, 0, -1):
        k_sum(hop, 1)

    for lo in range(0, width, 256):
        part_q = slice(lo, lo + 256)
        dq[:, part_q] = mul(dqkv[:, :1024], w_qo[part_q, :1024], NT)
    dense_cores(1)
    experts_start(total * 5 // 8, total)
    for t in range(2):
        kd_copy(0, t).wait_recv()
        dkv_own[t] += dkv_core[0, t].astype(full)

        @pl.when(deep + 1 < n_deep)
        def _():
            k_copy(1, t).wait_recv()
            dkv_own[t] += dkv_deep[0, t].astype(full)

    for pair in range(4):
        lanes = slice(128 * pair, 128 * (pair + 1))
        value_lanes = slice(512 + 128 * pair, 640 + 128 * pair)
        dkey = jnp.concatenate([dkv_own[0, :, lanes], dkv_own[1, :, lanes]], axis=0)
        dqkv[:, 1024 + 128 * pair:1152 + 128 * pair] = turn_back(dkey).astype(low)
        dvalue = jnp.concatenate([dkv_own[0, :, value_lanes], dkv_own[1, :, value_lanes]], axis=0)
        dqkv[:, 1536 + 128 * pair:1664 + 128 * pair] = dvalue.astype(low)
    for lo in range(0, width, 256):
        grads_k[lo:lo + 256, :1024] = mul(normed_in[:, lo:lo + 256], dqkv[:, 1024:], TN).astype(low)
    x = x_in[...].astype(full)
    scale_one = norm_scale(x)
    for lo in range(0, width, 256):
        part_k = slice(lo, lo + 256)
        dq[:, part_k] += mul(dqkv[:, 1024:], w_kv[part_k, :1024], NT)
    dxone = dq[...]
    weighted = gain_one * dxone
    dgain_one = jnp.sum(dxone * x * scale_one, axis=0, keepdims=True)
    wide = lax.broadcasted_iota(jnp.int32, (width, 128), 1)
    grads_k[:, 1024:] = jnp.where(
        wide == 16, column(dgain_one), jnp.where(wide == 17, column(dgain_two), drouter)
    ).astype(low)
    dense_start(2)
    dense_plane(1)
    input_out[...] = (
        input_out[...]
        + scale_one * weighted
        - x * (scale_one * scale_one * scale_one) * jnp.mean(weighted * x, axis=1, keepdims=True)
    )
    dense_cores(2)
    dense_plane(2)
    o_out[...] = dense_end(0)
    q_out[...] = dense_end(1)
    last = dense_end(2)
    k_out[...] = last[:, :512]
    v_out[...] = last[:, 512:1024]
    spread_out[:rows] = last[:, 1024:]
    small_out[...] = spread_out[...].T
    for kind in range(3):
        def settle_d(index, carry):
            hop, step = index // 4, index % 4
            d_copy(kind, step, hop).wait_send()

            @pl.when(step > 0)
            def _():
                p_copy(kind, step, hop).wait_send()

            return carry

        lax.fori_loop(0, 4 * n_deep, settle_d, 0)

        def settle_z(hop, carry):
            z_copy(kind, hop).wait_send()
            return carry

        lax.fori_loop(1, n_deep, settle_z, 0)

    for hop in range(back + 1):
        for t in range(2):
            @pl.when(deep >= hop)
            def _():
                kd_copy(hop, t).wait_send()
                if hop > 0:
                    k_copy(hop, t).wait_send()

    expert_own.wait()

    def settle_experts(step, carry):
        other = (me + total - step) % total
        expert_copy(step).wait_send()
        there = held.at[other % n_seq // 4, other // n_seq * 4 + other % 4]
        remote(there, there, e_send.at[step], e_recv.at[step], sibling).wait_recv()
        return carry

    lax.fori_loop(1, total, settle_experts, 0)


def window_of(length, block, n_deep):
    back = length // 2 // (2 * block)
    assert back * 4 * block == length and 0 < back < n_deep
    return back


def run_backward(n_row, n_seq, length, w_kv, w_qo, kv, queries, normed, mixed, x, g, cosine, sine, start,
                 hidden, xtwo, gates, dgates, dx, lse, expert_grads):
    tokens, width = x.shape
    total, n_deep = n_row * n_seq, n_seq // 2
    rows, block = width // total, tokens // 2
    back = window_of(length, block, n_deep)
    columns = (1024, 1024, w_kv.shape[1])
    low, full = jnp.bfloat16, jnp.float32
    dma, shape = pltpu.SemaphoreType.DMA, jax.ShapeDtypeStruct
    return pl.pallas_call(
        functools.partial(backward_kernel, n_row, n_seq, back),
        out_shape=(
            shape((tokens, width), full),
            shape((rows, 1024), full),
            shape((rows, 512), full),
            shape((rows, 512), full),
            shape((rows, 1024), full),
            shape((128, 128), full),
            shape((n_seq // 4, n_row * 4, rows, expert_grads.shape[1]), low),
        ),
        in_specs=[ANY] * 4 + [VMEM] * 13 + [ANY],
        out_specs=(VMEM,) * 6 + (ANY,),
        scratch_shapes=[
            pltpu.VMEM(w_kv.shape, low),
            pltpu.VMEM(w_qo.shape, low),
            pltpu.VMEM(kv.shape, low),
            pltpu.VMEM((16, tokens, 128), low),
            pltpu.VMEM((16, tokens, 128), low),
            pltpu.VMEM((tokens, 1024), full),
            pltpu.VMEM((tokens, 2048), low),
            pltpu.VMEM(kv.shape[1:], full),
            pltpu.VMEM((back + 1,) + kv.shape[1:], low),
            pltpu.VMEM((back,) + kv.shape[1:], low),
        ]
        + [pltpu.VMEM((width, c), low) for c in columns]
        + [pltpu.VMEM((n_deep, 4, rows, c), low) for c in columns]
        + [pltpu.VMEM((n_deep, 3, rows, c), low) for c in columns]
        + [pltpu.VMEM((n_deep, rows, c), low) for c in columns]
        + [
            pltpu.VMEM((128, 128), full),
            dma((4,)),
            dma((back + 1, 2)), dma((back + 1, 2)), dma((back + 1, 2)), dma((back + 1, 2)),
            dma((total,)), dma((total,)), dma,
            dma((3, n_deep, 4)), dma((3, n_deep, 4)), dma((3, n_deep, 4)), dma((3, n_deep, 4)),
            dma((3, n_deep)), dma((3, n_deep)),
        ],
        compiler_params=pltpu.CompilerParams(
            collective_id=2, has_side_effects=True, vmem_limit_bytes=62 << 20
        ),
        name="backward",
    )(w_kv, w_qo, kv, queries, normed, mixed, x, g, cosine, sine, start, hidden, xtwo, gates, dgates, dx, lse,
      expert_grads)


def results_kernel(
    held, counts, small, *refs
):
    passed, copied = refs[:6], refs[6:12]
    gate_out, up_out, down_out, router_out, one_out, two_out, counts_out = refs[12:]
    ff = gate_out.shape[2]
    rows = router_out.shape[1]
    for source, target in zip(passed[:2], copied[:2]):
        target[...] = source[...]

    @pl.when(pl.program_id(0) == 0)
    def _():
        for source, target in zip(passed[2:], copied[2:]):
            target[...] = source[...]
        router_out[...] = small[:EXPERTS, :rows]
        one_out[...] = small[EXPERTS:EXPERTS + 1, :rows]
        two_out[...] = small[EXPERTS + 1:EXPERTS + 2, :rows]
        counts_out[...] = pltpu.roll(counts[...], 96, 1)[:1].astype(jnp.int32)

    for out, lo in ((gate_out, 0), (up_out, ff), (down_out, 2 * ff)):
        value = held[0, :, :, lo:lo + ff].astype(jnp.float32)
        for group in range(1, held.shape[0]):
            value += held[group, :, :, lo:lo + ff].astype(jnp.float32)
        out[...] = value


def run_results(held, counts, small, *passed):
    groups, experts, rows, wide = held.shape
    ff, full = wide // 3, jnp.float32
    some = experts // 4
    shape = jax.ShapeDtypeStruct
    whole = lambda i: (0, 0)
    moved = [pl.BlockSpec((a.shape[0] // 4, a.shape[1]), lambda i: (i, 0)) for a in passed[:2]]
    moved += [pl.BlockSpec(a.shape, whole) for a in passed[2:]]
    return pl.pallas_call(
        results_kernel,
        grid=(4,),
        out_shape=tuple(shape(a.shape, a.dtype) for a in passed) + (
            shape((experts, rows, ff), full),
            shape((experts, rows, ff), full),
            shape((experts, rows, ff), full),
            shape((EXPERTS, rows), full),
            shape((1, rows), full),
            shape((1, rows), full),
            shape((1, 128), jnp.int32),
        ),
        in_specs=[
            pl.BlockSpec((groups, some, rows, wide), lambda i: (0, i, 0, 0)),
            pl.BlockSpec((8, 128), whole),
            pl.BlockSpec((128, 128), whole),
        ] + moved,
        out_specs=tuple(moved) + (pl.BlockSpec((some, rows, ff), lambda i: (i, 0, 0)),) * 3 + (
            pl.BlockSpec((EXPERTS, rows), whole),
            pl.BlockSpec((1, rows), whole),
            pl.BlockSpec((1, rows), whole),
            pl.BlockSpec((1, 128), whole),
        ),
        name="results",
    )(held, counts, small, *passed)


def body(
    n_row,
    n_seq,
    tokens,
    segment_ids,
    expert_ids,
    norm1_gain,
    w_query,
    w_key,
    w_value,
    w_out,
    norm2_gain,
    w_router,
    w_gate,
    w_up,
    w_down,
    out_grad,
):
    row_count, block_len, width = tokens.shape
    token_count = row_count * block_len
    length = segment_ids.shape[1]
    rows = w_query.shape[0]
    full = jnp.float32
    small = jnp.concatenate([w_router.T, norm1_gain[None], norm2_gain[None], jnp.zeros((14, rows), norm1_gain.dtype)])
    lanes = np.arange(128) % HEAD
    half = HEAD // 2
    frequency = (THETA ** (-2.0 * (lanes % half) / HEAD)).astype(np.float32)
    turns = np.zeros((8, 128), np.float32)
    turns[0], turns[1] = frequency, np.where(lanes < half, -1.0, 1.0)
    x = tokens.reshape(token_count, width)
    g = out_grad.reshape(token_count, width)
    (cosine, sine, start, xtwo, gates, counts, hidden, mixed, lse, normed, queries, kv, w_kv, w_qo,
     group_g, group_x, group_gates, expert_weights) = run_forward(
        n_row, n_seq, length, w_key, w_value, w_query, w_out.T, small.astype(full), jnp.asarray(turns), segment_ids,
        jnp.swapaxes(expert_ids[0], 1, 2), x, g, w_gate, w_up, jnp.swapaxes(w_down, 1, 2)
    )
    layer_out, dx, dgates, expert_grads = run_experts(
        n_row, n_seq, group_x, group_g, group_gates, expert_weights, hidden
    )
    input_grad, dq, dk, dv, do, small, held = run_backward(
        n_row, n_seq, length, w_kv, w_qo, kv, queries, normed, mixed, x, g, cosine, sine, start,
        hidden, xtwo, gates, dgates, dx, lse, expert_grads,
    )
    layer_out, input_grad, dq, dk, dv, do, d_gate, d_up, d_down, router, one, two, counts = run_results(
        held, counts, small, layer_out, input_grad, dq, dk, dv, do
    )
    return (
        layer_out.reshape(row_count, block_len, width),
        input_grad.reshape(row_count, block_len, width),
        one[0],
        dq,
        dk,
        dv,
        do.T,
        two[0],
        router.T,
        d_gate,
        d_up,
        jnp.swapaxes(d_down, 1, 2),
        counts[0, :EXPERTS],
    )


def solution(mesh):
    in_specs = (
        P("row", "seq", None),
        P("row", None),
        P("seq", "row", None, None),
        P(("row", "seq")),
        P(("row", "seq"), None),
        P(("row", "seq"), None),
        P(("row", "seq"), None),
        P(None, ("row", "seq")),
        P(("row", "seq")),
        P(("row", "seq"), None),
        P(None, ("row", "seq"), None),
        P(None, ("row", "seq"), None),
        P(None, None, ("row", "seq")),
        P("row", "seq", None),
    )
    out_specs = (
        P("row", "seq", None),
        P("row", "seq", None),
        P(("row", "seq")),
        P(("row", "seq"), None),
        P(("row", "seq"), None),
        P(("row", "seq"), None),
        P(None, ("row", "seq")),
        P(("row", "seq")),
        P(("row", "seq"), None),
        P(None, ("row", "seq"), None),
        P(None, ("row", "seq"), None),
        P(None, None, ("row", "seq")),
        P(),
    )
    return jax.shard_map(
        functools.partial(body, mesh.shape["row"], mesh.shape["seq"]),
        mesh=mesh,
        in_specs=in_specs,
        out_specs=out_specs,
        check_vma=False,
    )
```
